32 devices in a mesh: dp: 4 (over x, core), tensor: 8 (over z, y).
Axes of the slice: x: 2, y: 2, z: 4, core: 2. Of those that a mesh axis runs over, the one named last changes fastest.
Arguments:
- hidden_in: bfloat16 [8192, 2048], P('dp'), may hold values from -6 to 6
- seq_lengths: int32 [4], P('dp'), may hold values from 1024 to 2048, as said below
- out_grad: bfloat16 [8192, 2048], P('dp'), may hold values from -6 to 6
- attn_gain: float32 [2048], replicated, may hold values from 0.5 to 1.5
- mlp_gain: float32 [2048], replicated, may hold values from 0.5 to 1.5
- w_query: bfloat16 [2048, 2048], P(None, 'tensor'), may hold values from -0.5 to 0.5
- w_key: bfloat16 [2048, 512], P('tensor'), may hold values from -0.5 to 0.5
- w_value: bfloat16 [2048, 512], P('tensor'), may hold values from -0.125 to 0.125
- w_out: bfloat16 [2048, 2048], P('tensor'), may hold values from -2 to 2
- w_gate: bfloat16 [2048, 8192], P(None, 'tensor'), may hold values from -0.125 to 0.125
- w_up: bfloat16 [2048, 8192], P(None, 'tensor'), may hold values from -0.125 to 0.125
- w_down: bfloat16 [8192, 2048], P('tensor'), may hold values from -0.5 to 0.5
Outputs:
- layer_out: bfloat16 [8192, 2048], P(('dp', 'tensor'))
- in_grad: float32 [8192, 2048], P(('dp', 'tensor'))
- attn_gain_grad: float32 [2048], P(('dp', 'tensor'))
- mlp_gain_grad: float32 [2048], P(('dp', 'tensor'))
- w_query_grad: float32 [2048, 2048], P('dp', 'tensor')
- w_key_grad: float32 [2048, 512], P(('dp', 'tensor'))
- w_value_grad: float32 [2048, 512], P(('dp', 'tensor'))
- w_out_grad: float32 [2048, 2048], P('tensor', 'dp')
- w_gate_grad: float32 [2048, 8192], P('dp', 'tensor')
- w_up_grad: float32 [2048, 8192], P('dp', 'tensor')
- w_down_grad: float32 [8192, 2048], P('tensor', 'dp')
The draws below stay inside these ranges and needn't reach their ends.
Inputs may be any that keep to these rules, and one draw needn't show every extreme that they name: `seq_lengths`: each sequence has between half of its 2048 slots and all of them valid; some sequence is full and some is exactly half full.
All inputs are finite; a program needn't handle non-finite values.
Results may differ from the reference program's by a relative error of at most 0.02.
Values may be sent and summed in bfloat16 or wider, within the bound.
No kernel may reach another device: no remote copies, remote signals or barrier semaphores. Data moves between devices by JAX's collectives and lax.ppermute only.
A program may use at most 256 MiB of HBM per device.

```python
import math
import jax
import jax.numpy as jnp
from jax import lax

D = 2048
H = 32
KVH = 8
HD = 64
FF = 8192
SEQ_LEN = 2048
QB = 512
NSEQ = 4
TOKENS = 8192


def draw_seq_lengths(key, part):
    first_key = jax.random.fold_in(key, 11)
    second_key = jax.random.fold_in(key, 23)
    drawn = jax.random.randint(first_key, (NSEQ,), SEQ_LEN // 2, SEQ_LEN + 1)
    order = jax.random.permutation(second_key, NSEQ)
    drawn = drawn.at[order[0]].set(SEQ_LEN)
    drawn = drawn.at[order[1]].set(SEQ_LEN // 2)
    return drawn.astype(jnp.int32)


def block_scale(stream_key, extent, split, least, top_value):
    level = 1.0
    for position, blocks in split:
        heights = jax.random.uniform(jax.random.fold_in(jax.random.fold_in(stream_key, 6), position), (blocks,), jnp.float32, least / len(split), top_value / len(split))
        level = level * jnp.repeat(jnp.exp(heights), extent[position] // blocks).reshape((-1,) + (1,) * (len(extent) - 1 - position))
    return level


def gaussian(own_key, dims, spread, reach, cuts=(), held_as=jnp.bfloat16):
    array = jax.random.normal(own_key, dims, jnp.float32) * spread
    if len(cuts) > 0:
        array = block_scale(own_key, dims, cuts, -0.22, 0.18) * array
    return jnp.clip(array, min=-reach, max=reach).astype(held_as)


def setup_inputs(seed: int = 0) -> dict:
    seeds = jax.random.split(jax.random.key(seed), 13)
    hidden_in = gaussian(seeds[0], (TOKENS, D), 1.0, 6.0, ((0, 4),))
    seq_lengths = draw_seq_lengths(jax.random.fold_in(seeds[12], 71), 0)
    out_grad = gaussian(seeds[2], (TOKENS, D), 1.0, 6.0, ((0, 4),))
    attn_gain = jnp.clip(1.0 + 0.1 * jax.random.normal(seeds[3], (D,), jnp.float32), 0.5, 1.5)
    mlp_gain = jnp.clip(1.0 + 0.1 * jax.random.normal(seeds[4], (D,), jnp.float32), 0.5, 1.5)
    w_query = gaussian(seeds[5], (D, H * HD), (D // 16) ** -0.5, 0.5, ((1, 8),))
    w_key = gaussian(seeds[6], (D, KVH * HD), (D // 16) ** -0.5, 0.5, ((0, 8),))
    w_value = gaussian(seeds[7], (D, KVH * HD), D ** -0.5, 0.125, ((0, 8),))
    w_out = gaussian(seeds[8], (H * HD, D), 8 ** -0.5, 2.0, ((0, 8),))
    w_gate = gaussian(seeds[9], (D, FF), D ** -0.5, 0.125, ((1, 8),))
    w_up = gaussian(seeds[10], (D, FF), D ** -0.5, 0.125, ((1, 8),))
    w_down = gaussian(seeds[11], (FF, D), (FF // 64) ** -0.5, 0.5, ((0, 8),))
    return {"hidden_in": hidden_in, "seq_lengths": seq_lengths, "out_grad": out_grad, "attn_gain": attn_gain, "mlp_gain": mlp_gain, "w_query": w_query, "w_key": w_key, "w_value": w_value, "w_out": w_out, "w_gate": w_gate, "w_up": w_up, "w_down": w_down}


@jax.custom_vjp
def low(v):
    return lax.optimization_barrier(v.astype(jnp.bfloat16)).astype(jnp.float32)

@jax.custom_vjp
def low_back(v):
    return v

def low_keep(v):
    return (low(v), None)

def low_pass(kept, grad):
    return (grad,)

def back_keep(v):
    return (v, None)

def back_low(kept, grad):
    return (low(grad),)
low.defvjp(low_keep, low_pass)
low_back.defvjp(back_keep, back_low)
RESID = 0.22
ATTN_SCALE = 0.015625
EPSILON = 1e-05
THETA_LOG = math.log(10000000.0)
MASKED = -1e+30

def dot_high(left, right):
    return jnp.dot(left, right, precision=lax.Precision.HIGHEST, preferred_element_type=jnp.float32)

def rope_tables():
    positions = jnp.arange(SEQ_LEN, dtype=jnp.int32).astype(jnp.float32)[:, None]
    freqs = jnp.exp(-THETA_LOG * jnp.arange(0, HD, 2, dtype=jnp.int32).astype(jnp.float32) / HD)[None, :]
    angle_rows = positions * freqs
    angle_rows = jnp.concatenate([angle_rows, angle_rows], 1)
    return (jnp.cos(angle_rows), jnp.sin(angle_rows))

def rotate(values, cosines, sines):
    half = HD // 2
    turned = jnp.concatenate([-values[..., half:], values[..., :half]], -1)
    return values * cosines[:, None, :] + turned * sines[:, None, :]

def rms_norm(rows, gain):
    return rows * lax.rsqrt(lax.optimization_barrier(jnp.mean(rows * rows, axis=-1, keepdims=True)) + EPSILON) * gain

def attend(queries, keys, values, length):

    def one_block(index):
        start = index * QB
        query_rows = lax.dynamic_slice_in_dim(queries, start, QB, 0)
        raw = jnp.einsum('qhd,khd->hqk', query_rows, keys, precision=lax.Precision.HIGHEST) * ATTN_SCALE
        raw = low_back(raw)
        query_pos = start + jnp.arange(QB, dtype=jnp.int32)
        key_pos = jnp.arange(SEQ_LEN, dtype=jnp.int32)
        allowed = (key_pos[None, :] <= query_pos[:, None]) & (key_pos[None, :] < length)
        scores = jnp.where(allowed[None], raw, MASKED)
        probs = low(jax.nn.softmax(scores, axis=-1))
        return jnp.einsum('hqk,khd->qhd', probs, values, precision=lax.Precision.HIGHEST)
    blocks_out = lax.map(jax.checkpoint(one_block), jnp.arange(SEQ_LEN // QB, dtype=jnp.int32))
    return blocks_out.reshape(SEQ_LEN, H, HD)

def layer(rows_in, attn_gain, mlp_gain, w_query, w_key, w_value, w_out, w_gate, w_up, w_down, length):
    cosines, sines = rope_tables()
    group = H // KVH
    normed_one = low(rms_norm(rows_in, attn_gain))
    queries = low_back(dot_high(normed_one, w_query)).reshape(SEQ_LEN, H, HD)
    queries = low(rotate(queries, cosines, sines))
    keys = jnp.repeat(dot_high(normed_one, w_key).reshape(SEQ_LEN, KVH, HD), group, axis=1)
    keys = low(rotate(low_back(keys), cosines, sines))
    values = jnp.repeat(dot_high(normed_one, w_value).reshape(SEQ_LEN, KVH, HD), group, axis=1)
    values = low(low_back(values))
    attended = attend(queries, keys, values, length).reshape(SEQ_LEN, H * HD)
    attended = low(low_back(attended))
    middle = rows_in + RESID * low_back(dot_high(attended, w_out))
    normed_two = low(rms_norm(middle, mlp_gain))
    gate_rows = low_back(dot_high(normed_two, w_gate))
    up_rows = low_back(dot_high(normed_two, w_up))
    activ = low(jax.nn.silu(gate_rows) * up_rows)
    return middle + RESID * low_back(dot_high(activ, w_down))

def reference(hidden_in, seq_lengths, out_grad, attn_gain, mlp_gain, w_query, w_key, w_value, w_out, w_gate, w_up, w_down):
    params = tuple((p.astype(jnp.float32) for p in (attn_gain, mlp_gain, w_query, w_key, w_value, w_out, w_gate, w_up, w_down)))
    inputs = hidden_in.astype(jnp.float32).reshape(NSEQ, SEQ_LEN, D)
    cotangents = out_grad.astype(jnp.float32).reshape(NSEQ, SEQ_LEN, D)

    def per_sequence(totals, entry):
        rows_in, cotangent, length = entry
        valid_rows = (jnp.arange(SEQ_LEN, dtype=jnp.int32) < length).astype(jnp.float32)[:, None]

        def forward(first, *rest):
            return layer(first, *rest, length)
        output, pullback = jax.vjp(forward, rows_in, *params)
        gradients = pullback(cotangent * valid_rows)
        totals = tuple((total + grad for total, grad in zip(totals, gradients[1:])))
        return (totals, (output, gradients[0]))
    starting = tuple((jnp.zeros(p.shape, jnp.float32) for p in params))
    totals, (outputs, input_grads) = lax.scan(per_sequence, starting, (inputs, cotangents, seq_lengths))
    layer_out = outputs.reshape(NSEQ * SEQ_LEN, D).astype(jnp.bfloat16)
    in_grad = input_grads.reshape(NSEQ * SEQ_LEN, D)
    return (layer_out, in_grad, totals[0], totals[1], totals[2], totals[3], totals[4], totals[5], totals[6], totals[7], totals[8])
```

```python
import functools
import math

import jax
import jax.numpy as jnp
from jax import lax
from jax.experimental import pallas as pl
from jax.experimental.pallas import tpu as pltpu
from jax.sharding import PartitionSpec as P

H = 32
KVH = 8
HD = 64
SEQ_LEN = 2048
QB = 256
WIDE = 512

RESID = 0.22
ATTN_SCALE = 0.015625
EPSILON = 1e-05
THETA_LOG = math.log(10000000.0)
MASKED = -1e30

f32 = jnp.float32
bf16 = jnp.bfloat16
NN = (((1,), (0,)), ((), ()))
NT = (((1,), (1,)), ((), ()))
TN = (((0,), (0,)), ((), ()))


def mm(left, right, dims):
    return lax.dot_general(left, right, dims, preferred_element_type=f32)


def grant(mib):
    return pltpu.CompilerParams(vmem_limit_bytes=mib * 1024 * 1024)


def cost(flops, nbytes):
    return pl.CostEstimate(flops=int(flops), bytes_accessed=int(nbytes), transcendentals=0)


def rope_tables(count):
    positions = jnp.arange(count, dtype=jnp.int32).astype(f32)[:, None]
    lane = jnp.arange(128, dtype=jnp.int32) % (HD // 2)
    freqs = jnp.exp(-THETA_LOG * (2 * lane).astype(f32) / HD)[None, :]
    angle_rows = positions * freqs
    return (jnp.cos(angle_rows), jnp.sin(angle_rows))


def widen(table, count):
    return table if count == 128 else jnp.concatenate([table] * (count // 128), 1)


def swap_halves(rows):
    count = rows.shape[1]
    lane = lax.broadcasted_iota(jnp.int32, rows.shape, 1)
    ahead = pltpu.roll(rows, count - HD // 2, 1)
    behind = pltpu.roll(rows, HD // 2, 1)
    return jnp.where(lane % HD < HD // 2, ahead, behind)


def half_sign(shape):
    lane = lax.broadcasted_iota(jnp.int32, shape, 1)
    return jnp.where(lane % HD < HD // 2, -1.0, 1.0)


def rotate(rows, cosines, sines):
    count = rows.shape[1]
    turned = swap_halves(rows) * half_sign(rows.shape)
    return rows * widen(cosines, count) + turned * widen(sines, count)


def unrotate(rows, cosines, sines):
    count = rows.shape[1]
    turned = swap_halves(rows * widen(sines, count)) * half_sign(rows.shape)
    return rows * widen(cosines, count) - turned


def front_kernel(
    length_ref,
    rows_ref,
    gain_ref,
    wq_ref,
    wkv_ref,
    cos_ref,
    sin_ref,
    normed_ref,
    q_ref,
    k_ref,
    kt_ref,
    v_ref,
    vt_ref,
):
    rows = rows_ref[...].astype(f32)
    row_scale = lax.rsqrt(jnp.mean(rows * rows, axis=-1, keepdims=True) + EPSILON)
    normed_ref[...] = (rows * row_scale * gain_ref[...]).astype(bf16)
    normed = normed_ref[...]
    cosines = cos_ref[...]
    sines = sin_ref[...]
    q_raw = mm(normed, wq_ref[...], NN)
    q_ref[...] = (rotate(q_raw, cosines, sines).astype(bf16).astype(f32) * ATTN_SCALE).astype(bf16)
    kv_raw = mm(normed, wkv_ref[...], NN)
    lane = lax.broadcasted_iota(jnp.int32, kv_raw.shape, 1)
    position = pl.program_id(0) * QB + lax.broadcasted_iota(jnp.int32, kv_raw.shape, 0)
    turned = rotate(kv_raw, cosines, sines)
    keys = jnp.where(lane < HD, turned, 0.0)
    blocked = jnp.where((lane == HD) & (position >= length_ref[0]), MASKED, 0.0)
    k_ref[...] = (keys + blocked).astype(bf16)
    kt_ref[...] = keys.T.astype(bf16)
    values = jnp.concatenate([kv_raw[:, HD:], kv_raw[:, :HD]], 1)
    values = jnp.where(lane < HD, values, 1.0)
    v_ref[...] = values.astype(bf16)
    vt_ref[...] = values.T.astype(bf16)


def front(length, hidden, gain, w_query, w_kv, cosines, sines):
    count, width = hidden.shape
    q_cols = w_query.shape[1]
    row = lambda i, s: (i, 0)
    col = lambda i, s: (0, i)
    whole = lambda i, s: (0, 0)
    return pl.pallas_call(
        front_kernel,
        grid_spec=pltpu.PrefetchScalarGridSpec(
            num_scalar_prefetch=1,
            grid=(count // QB,),
            in_specs=[
                pl.BlockSpec((QB, width), row),
                pl.BlockSpec((1, width), whole),
                pl.BlockSpec((width, q_cols), whole),
                pl.BlockSpec((width, 128), whole),
                pl.BlockSpec((QB, 128), row),
                pl.BlockSpec((QB, 128), row),
            ],
            out_specs=[
                pl.BlockSpec((QB, width), row),
                pl.BlockSpec((QB, q_cols), row),
                pl.BlockSpec((QB, 128), row),
                pl.BlockSpec((128, QB), col),
                pl.BlockSpec((QB, 128), row),
                pl.BlockSpec((128, QB), col),
            ],
        ),
        out_shape=[
            jax.ShapeDtypeStruct((count, width), bf16),
            jax.ShapeDtypeStruct((count, q_cols), bf16),
            jax.ShapeDtypeStruct((count, 128), bf16),
            jax.ShapeDtypeStruct((128, count), bf16),
            jax.ShapeDtypeStruct((count, 128), bf16),
            jax.ShapeDtypeStruct((128, count), bf16),
        ],
        cost_estimate=cost(2 * count * width * (q_cols + 128), 5 * count * width),
        name="norm_and_project",
    )(length, hidden, gain, w_query, w_kv, cosines, sines)


def head_slab(rows, head, fill):
    pair = rows[:, 128 * (head // 2) : 128 * (head // 2) + 128]
    if head % 2:
        pair = jnp.concatenate([pair[:, HD:], pair[:, :HD]], 1)
    lane = lax.broadcasted_iota(jnp.int32, pair.shape, 1)
    other = jnp.where(lane == HD, jnp.full(pair.shape, fill, f32), 0.0).astype(pair.dtype)
    return jnp.where(lane < HD, pair, other)


def causal(keys_count, rows_count):
    key = lax.broadcasted_iota(jnp.int32, (keys_count, rows_count), 0)
    return key <= lax.broadcasted_iota(jnp.int32, (keys_count, rows_count), 1)


def attend_kernel(heads, q_ref, k_ref, vt_ref, o_ref, lse_ref, slab_ref, high_ref, total_ref):
    block = pl.program_id(0)
    rows = q_ref[...]
    for head in range(heads):
        slab_ref[head] = head_slab(rows, head, 1.0)
    high_ref[...] = jnp.full(high_ref.shape, MASKED, f32)
    total_ref[...] = jnp.zeros(total_ref.shape, f32)

    def step(start, width, diagonal):
        keys = k_ref[pl.ds(start, width), :]
        values = vt_ref[:, pl.ds(start, width)]
        scores = [mm(keys, slab_ref[head], NT) for head in range(heads)]
        for head in range(heads):
            score = scores[head]
            if diagonal:
                score = jnp.where(causal(width, QB), score, MASKED)
            old = high_ref[head : head + 1, :]
            new = jnp.maximum(old, jnp.max(score, axis=0, keepdims=True))
            probs = jnp.exp(score - new).astype(bf16)
            high_ref[head : head + 1, :] = new
            total_ref[head] = total_ref[head] * jnp.exp(old - new) + mm(values, probs, NN)

    def body(index, carry):
        step(pl.multiple_of(index * WIDE, WIDE), WIDE, False)
        return carry

    lax.fori_loop(0, block // 2, body, 0)

    @pl.when(block % 2 == 1)
    def _():
        step(pl.multiple_of((block - 1) * QB, QB), QB, False)

    step(pl.multiple_of(block * QB, QB), QB, True)
    outs = []
    for head in range(heads):
        total = total_ref[head]
        mass = total[HD : HD + 1, :]
        lse_ref[head : head + 1, :] = high_ref[head : head + 1, :] + jnp.log(mass)
        outs.append(total[:HD, :] * (1.0 / mass))
    o_ref[...] = jnp.concatenate(outs, 0).T.astype(bf16)


def attend(queries, keys, values_t):
    count, q_cols = queries.shape
    heads = q_cols // HD
    return pl.pallas_call(
        functools.partial(attend_kernel, heads),
        grid=(count // QB,),
        in_specs=[
            pl.BlockSpec((QB, q_cols), lambda i: (i, 0)),
            pl.BlockSpec((count, 128), lambda i: (0, 0)),
            pl.BlockSpec((128, count), lambda i: (0, 0)),
        ],
        out_specs=[
            pl.BlockSpec((QB, q_cols), lambda i: (i, 0)),
            pl.BlockSpec((8, QB), lambda i: (0, i)),
        ],
        out_shape=[
            jax.ShapeDtypeStruct((count, q_cols), bf16),
            jax.ShapeDtypeStruct((8, count), f32),
        ],
        scratch_shapes=[
            pltpu.VMEM((heads, QB, 128), bf16),
            pltpu.VMEM((8, QB), f32),
            pltpu.VMEM((heads, 128, QB), f32),
        ],
        cost_estimate=cost(heads * count * count * 512, 4 * count * q_cols),
        name="attend",
    )(queries, keys, values_t)


def attend_back_kernel(
    heads,
    q_ref,
    do_ref,
    o_ref,
    lse_ref,
    k_ref,
    kt_ref,
    v_ref,
    cos_ref,
    sin_ref,
    out_ref,
    qs_ref,
    ds_ref,
    delta_ref,
    dq_ref,
    dk_ref,
    dv_ref,
):
    block = pl.program_id(0)
    blocks = pl.num_programs(0)
    q_cols = heads * HD

    @pl.when(block == 0)
    def _():
        dk_ref[...] = jnp.zeros(dk_ref.shape, f32)
        dv_ref[...] = jnp.zeros(dv_ref.shape, f32)

    rows = q_ref[...]
    grads = do_ref[...]
    product = (grads.astype(f32) * o_ref[...].astype(f32)).T
    for head in range(heads):
        qs_ref[head] = head_slab(rows, head, 1.0)
        ds_ref[head] = head_slab(grads, head, 0.0)
        delta_ref[head : head + 1, :] = jnp.sum(
            product[head * HD : (head + 1) * HD, :], axis=0, keepdims=True
        )
    dq_ref[...] = jnp.zeros(dq_ref.shape, f32)

    def step(start, diagonal):
        here = pl.ds(start, QB)
        keys = k_ref[here, :]
        keys_t = kt_ref[:, here]
        values = v_ref[here, :]
        dk = dk_ref[here, :]
        dv = dv_ref[here, :]

        def products(head):
            return (mm(keys, qs_ref[head], NT), mm(values, ds_ref[head], NT))

        ready = products(0)
        for head in range(heads):
            score, prob_grad = ready
            if head + 1 < heads:
                ready = products(head + 1)
            probs = jnp.exp(score - lse_ref[head : head + 1, :])
            if diagonal:
                probs = jnp.where(causal(QB, QB), probs, 0.0)
            dv = dv + mm(probs.astype(bf16), ds_ref[head], NN)
            score_grad = (probs * (prob_grad - delta_ref[head : head + 1, :])).astype(bf16)
            dk = dk + mm(score_grad, qs_ref[head], NN)
            dq_ref[head] = dq_ref[head] + mm(keys_t, score_grad, NN)
        dk_ref[here, :] = dk
        dv_ref[here, :] = dv

    def body(index, carry):
        step(pl.multiple_of(index * QB, QB), False)
        return carry

    lax.fori_loop(0, block, body, 0)
    step(pl.multiple_of(block * QB, QB), True)
    dq = jnp.concatenate([dq_ref[head, :HD, :] for head in range(heads)], 0).T * ATTN_SCALE
    here = pl.ds(pl.multiple_of(block * QB, QB), QB)
    out_ref[here, :q_cols] = unrotate(dq, cos_ref[here, :], sin_ref[here, :]).astype(bf16)

    @pl.when(block == blocks - 1)
    def _():
        def finish(index, carry):
            there = pl.ds(pl.multiple_of(index * QB, QB), QB)
            dk = dk_ref[there, :]
            lane = lax.broadcasted_iota(jnp.int32, dk.shape, 1)
            dk = unrotate(jnp.where(lane < HD, dk, 0.0), cos_ref[there, :], sin_ref[there, :])
            dv = dv_ref[there, :]
            out_ref[there, q_cols:] = jnp.concatenate([dk[:, :HD], dv[:, :HD]], 1).astype(bf16)
            return carry

        lax.fori_loop(0, blocks, finish, 0)


def attend_back(queries, out_grads, attended, lse, keys, keys_t, values, cosines, sines):
    count, q_cols = queries.shape
    heads = q_cols // HD
    row = lambda i: (i, 0)
    whole = lambda i: (0, 0)
    return pl.pallas_call(
        functools.partial(attend_back_kernel, heads),
        grid=(count // QB,),
        in_specs=[
            pl.BlockSpec((QB, q_cols), row),
            pl.BlockSpec((QB, q_cols), row),
            pl.BlockSpec((QB, q_cols), row),
            pl.BlockSpec((8, QB), lambda i: (0, i)),
            pl.BlockSpec((count, 128), whole),
            pl.BlockSpec((128, count), whole),
            pl.BlockSpec((count, 128), whole),
            pl.BlockSpec((count, 128), whole),
            pl.BlockSpec((count, 128), whole),
        ],
        out_specs=pl.BlockSpec((count, q_cols + 128), whole),
        out_shape=jax.ShapeDtypeStruct((count, q_cols + 128), bf16),
        scratch_shapes=[
            pltpu.VMEM((heads, QB, 128), bf16),
            pltpu.VMEM((heads, QB, 128), bf16),
            pltpu.VMEM((8, QB), f32),
            pltpu.VMEM((heads, 128, QB), f32),
            pltpu.VMEM((count, 128), f32),
            pltpu.VMEM((count, 128), f32),
        ],
        cost_estimate=cost(heads * count * count * 1280, 10 * count * q_cols),
        name="attend_back",
    )(queries, out_grads, attended, lse, keys, keys_t, values, cosines, sines)


def out_norm_kernel(ids_ref, o_ref, w_ref, rows_ref, gain_ref, middle_ref, normed_ref, sum_ref):
    step = pl.program_id(0)

    @pl.when(step == 0)
    def _():
        sum_ref[...] = jnp.zeros(sum_ref.shape, f32)

    sum_ref[...] += mm(o_ref[0], w_ref[...], NN)

    @pl.when(step == pl.num_programs(0) - 1)
    def _():
        middle = rows_ref[...].astype(f32) + RESID * sum_ref[...]
        middle_ref[...] = middle
        row_scale = lax.rsqrt(jnp.mean(middle * middle, axis=-1, keepdims=True) + EPSILON)
        normed_ref[...] = (middle * row_scale * gain_ref[...]).astype(bf16)


def out_norm(ids, attended, w_out, hidden, gain):
    groups, share, q_cols = attended.shape
    width = hidden.shape[1]
    return pl.pallas_call(
        out_norm_kernel,
        grid_spec=pltpu.PrefetchScalarGridSpec(
            num_scalar_prefetch=1,
            grid=(groups,),
            in_specs=[
                pl.BlockSpec((1, share, q_cols), lambda t, s: (t, 0, 0)),
                pl.BlockSpec((q_cols, width), lambda t, s: (t, 0)),
                pl.BlockSpec((share, width), lambda t, s: (s[0], 0)),
                pl.BlockSpec((1, width), lambda t, s: (0, 0)),
            ],
            out_specs=[
                pl.BlockSpec((share, width), lambda t, s: (0, 0)),
                pl.BlockSpec((share, width), lambda t, s: (0, 0)),
            ],
            scratch_shapes=[pltpu.VMEM((share, width), f32)],
        ),
        out_shape=[
            jax.ShapeDtypeStruct((share, width), f32),
            jax.ShapeDtypeStruct((share, width), bf16),
        ],
        cost_estimate=cost(2 * groups * share * q_cols * width, 2 * groups * q_cols * width),
        name="out_project_and_norm",
    )(ids, attended, w_out, hidden, gain)


def back_norm_kernel(
    parts,
    ids_ref,
    *refs,
):
    part_refs = refs[:parts]
    (
        middle_ref,
        gain_ref,
        cotangent_ref,
        w_ref,
        dh_ref,
        da_ref,
        gain_grad_ref,
        do_ref,
    ) = refs[parts:]

    @pl.when(pl.program_id(0) == 0)
    def _():
        incoming = part_refs[0][...].astype(f32)
        for ref in part_refs[1:]:
            incoming = incoming + ref[...].astype(f32)
        middle = middle_ref[...]
        row_scale = lax.rsqrt(jnp.mean(middle * middle, axis=-1, keepdims=True) + EPSILON)
        normed = middle * row_scale
        gain_grad_ref[...] = jnp.sum(incoming * normed, axis=0, keepdims=True)
        scaled = incoming * gain_ref[...]
        branch = row_scale * (scaled - normed * jnp.mean(scaled * normed, axis=-1, keepdims=True))
        share = middle.shape[0]
        position = ids_ref[0] * share + lax.broadcasted_iota(jnp.int32, (share, 1), 0)
        direct = jnp.where(position < ids_ref[1], cotangent_ref[...].astype(f32), 0.0)
        dh = direct + branch
        dh_ref[...] = dh
        da_ref[...] = (RESID * dh).astype(bf16)

    do_ref[0] = mm(da_ref[...], w_ref[...], NT).astype(bf16)


def back_norm(ids, parts, middle, gain, cotangent, w_out, q_cols):
    share, width = middle.shape
    groups = w_out.shape[0] // q_cols
    whole = lambda t, s: (0, 0)
    return pl.pallas_call(
        functools.partial(back_norm_kernel, len(parts)),
        grid_spec=pltpu.PrefetchScalarGridSpec(
            num_scalar_prefetch=1,
            grid=(groups,),
            in_specs=[pl.BlockSpec((share, width), whole)] * len(parts)
            + [
                pl.BlockSpec((share, width), whole),
                pl.BlockSpec((1, width), whole),
                pl.BlockSpec((share, width), lambda t, s: (s[0], 0)),
                pl.BlockSpec((q_cols, width), lambda t, s: (t, 0)),
            ],
            out_specs=[
                pl.BlockSpec((share, width), whole),
                pl.BlockSpec((share, width), whole),
                pl.BlockSpec((1, width), whole),
                pl.BlockSpec((1, share, q_cols), lambda t, s: (t, 0, 0)),
            ],
        ),
        out_shape=[
            jax.ShapeDtypeStruct((share, width), f32),
            jax.ShapeDtypeStruct((share, width), bf16),
            jax.ShapeDtypeStruct((1, width), f32),
            jax.ShapeDtypeStruct((groups, share, q_cols), bf16),
        ],
        cost_estimate=cost(2 * groups * share * q_cols * width, 2 * groups * q_cols * width),
        name="norm_back_and_project",
    )(ids, *parts, middle, gain, cotangent, w_out)


def in_grad_kernel(ids_ref, d_ref, w_ref, rows_ref, gain_ref, dh_ref, out_ref, sum_ref):
    step = pl.program_id(0)

    @pl.when(step == 0)
    def _():
        sum_ref[...] = jnp.zeros(sum_ref.shape, f32)

    sum_ref[...] += mm(d_ref[0], w_ref[0], NT)

    @pl.when(step == pl.num_programs(0) - 1)
    def _():
        rows = rows_ref[...].astype(f32)
        row_scale = lax.rsqrt(jnp.mean(rows * rows, axis=-1, keepdims=True) + EPSILON)
        normed = rows * row_scale
        scaled = sum_ref[...] * gain_ref[...]
        branch = row_scale * (scaled - normed * jnp.mean(scaled * normed, axis=-1, keepdims=True))
        out_ref[...] = dh_ref[...] + branch


def in_grad(ids, grads, w_qkv, hidden, gain, dh):
    groups, share, cols = grads.shape
    width = hidden.shape[1]
    whole = lambda t, s: (0, 0)
    return pl.pallas_call(
        in_grad_kernel,
        grid_spec=pltpu.PrefetchScalarGridSpec(
            num_scalar_prefetch=1,
            grid=(groups,),
            in_specs=[
                pl.BlockSpec((1, share, cols), lambda t, s: (t, 0, 0)),
                pl.BlockSpec((1, width, cols), lambda t, s: (t, 0, 0)),
                pl.BlockSpec((share, width), lambda t, s: (s[0], 0)),
                pl.BlockSpec((1, width), whole),
                pl.BlockSpec((share, width), whole),
            ],
            out_specs=pl.BlockSpec((share, width), whole),
            scratch_shapes=[pltpu.VMEM((share, width), f32)],
        ),
        out_shape=jax.ShapeDtypeStruct((share, width), f32),
        cost_estimate=cost(2 * groups * share * cols * width, 2 * groups * cols * width),
        name="input_grad",
    )(ids, grads, w_qkv, hidden, gain, dh)


def units_kernel(pieces, shares, ids_ref, *refs):
    piece_refs = refs[:pieces]
    cot_refs = refs[pieces : pieces + shares]
    gate_w_ref, up_w_ref, down_w_ref = refs[pieces + shares : pieces + shares + 3]
    outs = refs[-9:]
    normed_ref, down_ref, act_ref, dgate_ref, dup_ref, dn_ref, mlp_ref, dn_sum, mlp_sum = outs
    step = pl.program_id(0)

    @pl.when(step == 0)
    def _():
        at = 0
        for ref in piece_refs:
            normed_ref[at : at + ref.shape[0], :] = ref[...]
            at += ref.shape[0]
        share = cot_refs[0].shape[0]
        for index, ref in enumerate(cot_refs):
            position = ids_ref[1 + index] * share + lax.broadcasted_iota(jnp.int32, (share, 1), 0)
            masked = jnp.where(position < ids_ref[0], ref[...].astype(f32) * RESID, 0.0)
            down_ref[index * share : (index + 1) * share, :] = masked.astype(bf16)
        dn_sum[...] = jnp.zeros(dn_sum.shape, f32)
        mlp_sum[...] = jnp.zeros(mlp_sum.shape, f32)

    normed = normed_ref[...]
    gate = mm(normed, gate_w_ref[...], NN)
    up = mm(normed, up_w_ref[...], NN)
    dact = mm(down_ref[...], down_w_ref[...], NT)
    sg = jax.nn.sigmoid(gate)
    silu = gate * sg
    act_ref[...] = (silu * up).astype(bf16)
    dgate_ref[...] = (dact * up * sg * (1.0 + gate * (1.0 - sg))).astype(bf16)
    dup_ref[...] = (dact * silu).astype(bf16)
    dn_sum[...] += mm(dgate_ref[...], gate_w_ref[...], NT) + mm(dup_ref[...], up_w_ref[...], NT)
    mlp_sum[...] += mm(act_ref[...], down_w_ref[...], NN)

    @pl.when(step == pl.num_programs(0) - 1)
    def _():
        dn_ref[...] = dn_sum[...].astype(bf16)
        mlp_ref[...] = mlp_sum[...].astype(bf16)


def units(ids, pieces, cotangent, weights, slot, buffers, total_rows):
    w_gate, w_up, w_down = weights
    width, unit_count = w_gate.shape
    rows = sum(piece.shape[0] for piece in pieces)
    shares = ids.shape[0] - 1
    share = rows // shares
    block = min(256, unit_count)
    whole = lambda u, s: (0, 0)
    place = slot * share // rows
    in_specs = [pl.BlockSpec(piece.shape, whole) for piece in pieces]
    for index in range(shares):
        in_specs.append(
            pl.BlockSpec((share, width), functools.partial(lambda k, u, s: (s[1 + k], 0), index))
        )
    in_specs += [
        pl.BlockSpec((width, block), lambda u, s: (0, u)),
        pl.BlockSpec((width, block), lambda u, s: (0, u)),
        pl.BlockSpec((block, width), lambda u, s: (u, 0)),
    ]
    operands = [*pieces, *([cotangent] * shares), w_gate, w_up, w_down]
    aliases = {}
    if buffers is not None:
        for index, buffer in enumerate(buffers):
            aliases[1 + len(operands)] = index
            operands.append(buffer)
            in_specs.append(pl.BlockSpec(memory_space=pl.ANY))
    full = lambda u, s: (place, 0)
    part = lambda u, s: (place, u)
    return pl.pallas_call(
        functools.partial(units_kernel, len(pieces), shares),
        grid_spec=pltpu.PrefetchScalarGridSpec(
            num_scalar_prefetch=1,
            grid=(unit_count // block,),
            in_specs=in_specs,
            out_specs=[
                pl.BlockSpec((rows, width), full),
                pl.BlockSpec((rows, width), full),
                pl.BlockSpec((rows, block), part),
                pl.BlockSpec((rows, block), part),
                pl.BlockSpec((rows, block), part),
                pl.BlockSpec((rows, width), whole),
                pl.BlockSpec((rows, width), whole),
            ],
            scratch_shapes=[pltpu.VMEM((rows, width), f32), pltpu.VMEM((rows, width), f32)],
        ),
        out_shape=[
            jax.ShapeDtypeStruct((total_rows, width), bf16),
            jax.ShapeDtypeStruct((total_rows, width), bf16),
            jax.ShapeDtypeStruct((total_rows, unit_count), bf16),
            jax.ShapeDtypeStruct((total_rows, unit_count), bf16),
            jax.ShapeDtypeStruct((total_rows, unit_count), bf16),
            jax.ShapeDtypeStruct((rows, width), bf16),
            jax.ShapeDtypeStruct((rows, width), bf16),
        ],
        input_output_aliases=aliases,
        compiler_params=grant(58),
        cost_estimate=cost(14 * rows * width * unit_count, 6 * width * unit_count + 20 * rows * width),
        name="swiglu_rows",
    )(ids, *operands)


def ring_order(count):
    inner = 2 if count <= 8 else 4
    outer = count // inner
    cells = [(0, 0)]
    for row in range(outer):
        cells += [(row, c) for c in (range(1, inner) if row % 2 == 0 else range(inner - 1, 0, -1))]
    cells += [(row, 0) for row in range(outer - 1, 0, -1)]
    return [row * inner + c for row, c in cells]


def add_low(left, right):
    return (left.astype(f32) + right.astype(f32)).astype(bf16)


def ring_reduce(parts_up, parts_down, far, ahead, behind):
    half = far.shape[0] // 2
    got_up = lax.ppermute(far[:half], "tensor", ahead)
    got_down = lax.ppermute(far[half:], "tensor", behind)
    first = True
    for up, down in zip(reversed(parts_up), reversed(parts_down)):
        if first:
            up = jnp.concatenate([add_low(up[:half], got_up), up[half:]], 0)
            down = jnp.concatenate([down[:half], add_low(down[half:], got_down)], 0)
            first = False
        else:
            up = add_low(up, got_up)
            down = add_low(down, got_down)
        got_up = lax.ppermute(up, "tensor", ahead)
        got_down = lax.ppermute(down, "tensor", behind)
    return got_up, got_down


def local(
    hidden_in,
    seq_lengths,
    out_grad,
    attn_gain,
    mlp_gain,
    w_query,
    w_key,
    w_value,
    w_out,
    w_gate,
    w_up,
    w_down,
):
    rows_total, width = hidden_in.shape
    q_cols = w_query.shape[1]
    heads_here = q_cols // HD
    groups = lax.axis_size("tensor")
    replicas = lax.axis_size("dp")
    member = lax.axis_index("tensor")
    replica = lax.axis_index("dp")
    share = rows_total // groups
    order = ring_order(groups)
    place = [order.index(i) for i in range(groups)]
    ahead = [(order[i], order[(i + 1) % groups]) for i in range(groups)]
    behind = [(b, a) for a, b in ahead]
    half_way = groups // 2
    table = [
        [order[(place[i] + d) % groups] for d in range(-half_way + 1, half_way + 1)]
        for i in range(groups)
    ]
    near = jnp.asarray(table, jnp.int32)[member]
    at = lambda d: near[d + half_way - 1]
    length = seq_lengths[0]
    cosines, sines = rope_tables(rows_total)
    gain_one = attn_gain[None, :]
    gain_two = mlp_gain[None, :]

    def quarter(array):
        count = array.shape[0] // replicas
        return lax.dynamic_slice_in_dim(array, replica * count, count, 0)

    w_out_all = lax.all_gather(quarter(w_out), ("tensor", "dp"), axis=0, tiled=True)
    kv_of = [i * heads_here // (H // KVH) for i in range(groups)]
    pick = lambda w: jnp.stack([w[:, h * HD : (h + 1) * HD] for h in kv_of], 0)
    kv_send = jnp.concatenate([pick(w_key), pick(w_value)], 2)
    w_kv = lax.all_to_all(kv_send, "tensor", 0, 0, tiled=True).reshape(width, 2 * HD)
    w_qkv = jnp.concatenate([w_query, w_kv], 1)
    w_qkv_all = lax.all_gather(quarter(w_qkv), ("tensor", "dp"), axis=0, tiled=True)
    w_qkv_all = w_qkv_all.reshape(groups, width, q_cols + 2 * HD)

    normed_one, queries, keys, keys_t, values, values_t = front(
        seq_lengths, hidden_in, gain_one, w_query, w_kv, cosines, sines
    )
    attended, lse = attend(queries, keys, values_t)
    attended_rows = lax.all_to_all(
        attended.reshape(groups, share, q_cols), "tensor", 0, 0, tiled=True
    )
    own_id = jnp.stack([member, length])
    middle, normed_two = out_norm(own_id, attended_rows, w_out_all, hidden_in, gain_two)

    weights = (w_gate, w_up, w_down)
    buffers = None
    dn_up, dn_down, mlp_up, mlp_down = [], [], [], []
    *buffers, dn_own, mlp_own = units(
        jnp.stack([length, member]), [normed_two], out_grad, weights, groups - 2, None, rows_total
    )
    from_behind = from_ahead = normed_two
    for distance in range(1, half_way):
        from_behind = lax.ppermute(from_behind, "tensor", ahead)
        from_ahead = lax.ppermute(from_ahead, "tensor", behind)
        ids = jnp.stack([length, at(-distance), at(distance)])
        *buffers, dn, mlp = units(
            ids,
            [from_behind, from_ahead],
            out_grad,
            weights,
            2 * (distance - 1),
            buffers,
            rows_total,
        )
        dn_down.append(dn[:share])
        dn_up.append(dn[share:])
        mlp_down.append(mlp[:share])
        mlp_up.append(mlp[share:])
    top = lax.ppermute(from_behind[: share // 2], "tensor", ahead)
    bottom = lax.ppermute(from_ahead[share // 2 :], "tensor", behind)
    *buffers, dn_far, mlp_far = units(
        jnp.stack([length, at(half_way)]),
        [top, bottom],
        out_grad,
        weights,
        groups - 1,
        buffers,
        rows_total,
    )
    normed_ring, down_ring, act, dgate, dup = buffers

    dn_a, dn_b = ring_reduce(dn_up, dn_down, dn_far, ahead, behind)
    middle_grad, branch_grad, mlp_gain_part, do_send = back_norm(
        own_id, [dn_own, dn_a, dn_b], middle, gain_two, out_grad, w_out_all, q_cols
    )
    attended_grad = lax.all_to_all(do_send, "tensor", 0, 0, tiled=True).reshape(rows_total, q_cols)

    mlp_far, _ = lax.optimization_barrier((mlp_far, dn_a))
    mlp_a, mlp_b = ring_reduce(mlp_up, mlp_down, mlp_far, ahead, behind)
    layer_out = (
        middle + RESID * (mlp_own.astype(f32) + mlp_a.astype(f32) + mlp_b.astype(f32))
    ).astype(bf16)

    down_wgrad = mm(act, down_ring, TN).astype(bf16)
    gate_wgrad = mm(normed_ring, dgate, TN).astype(bf16)
    up_wgrad = mm(normed_ring, dup, TN).astype(bf16)
    attended_cols = jnp.swapaxes(attended_rows, 0, 1).reshape(share, groups * q_cols)
    out_wgrad = mm(attended_cols, branch_grad, TN).astype(bf16)

    qkv_grad = attend_back(
        queries, attended_grad, attended, lse, keys, keys_t, values, cosines, sines
    )
    qkv_rows = lax.all_to_all(
        qkv_grad.reshape(groups, share, q_cols + 2 * HD), "tensor", 0, 0, tiled=True
    )
    input_grad = in_grad(own_id, qkv_rows, w_qkv_all, hidden_in, gain_one, middle_grad)

    qkv_wgrad = mm(normed_one, qkv_grad, TN)
    attn_gain_part = jnp.sum(qkv_wgrad * w_qkv.astype(f32), axis=1) / attn_gain
    small = jnp.concatenate(
        [
            qkv_wgrad[:, q_cols:],
            attn_gain_part[:, None],
            mlp_gain_part[0][:, None],
            jnp.zeros((width, 126), f32),
        ],
        1,
    )
    over_dp = lambda a, d: lax.psum_scatter(a, "dp", scatter_dimension=d, tiled=True)
    small = over_dp(small, 0)
    pieces = lax.all_to_all(
        small.reshape(groups, small.shape[0] // groups, 256), "tensor", 0, 0, tiled=True
    )
    gains = jnp.sum(pieces[:, :, 128:130], axis=0)
    kv = pieces[:, :, :128].reshape(KVH, groups // KVH, -1, 128).sum(axis=1)
    kv = jnp.swapaxes(kv, 0, 1)
    key_wgrad = kv[:, :, :HD].reshape(-1, KVH * HD)
    value_wgrad = kv[:, :, HD:].reshape(-1, KVH * HD)
    query_wgrad = over_dp(qkv_wgrad[:, :q_cols].astype(bf16), 0).astype(f32)
    gate_wgrad = over_dp(gate_wgrad, 0).astype(f32)
    up_wgrad = over_dp(up_wgrad, 0).astype(f32)
    down_wgrad = over_dp(down_wgrad, 1).astype(f32)
    out_wgrad = over_dp(out_wgrad, 1)
    out_wgrad = lax.psum_scatter(out_wgrad, "tensor", scatter_dimension=0, tiled=True).astype(f32)
    return (
        layer_out,
        input_grad,
        gains[:, 0],
        gains[:, 1],
        query_wgrad,
        key_wgrad,
        value_wgrad,
        out_wgrad,
        gate_wgrad,
        up_wgrad,
        down_wgrad,
    )


def solution(mesh):
    placed = (
        P("dp", None),
        P("dp"),
        P("dp", None),
        P(),
        P(),
        P(None, "tensor"),
        P("tensor", None),
        P("tensor", None),
        P("tensor", None),
        P(None, "tensor"),
        P(None, "tensor"),
        P("tensor", None),
    )
    return jax.shard_map(
        local,
        mesh=mesh,
        in_specs=placed,
        out_specs=(
            P(("dp", "tensor"), None),
            P(("dp", "tensor"), None),
            P(("dp", "tensor")),
            P(("dp", "tensor")),
            P("dp", "tensor"),
            P(("dp", "tensor"), None),
            P(("dp", "tensor"), None),
            P("tensor", "dp"),
            P("dp", "tensor"),
            P("dp", "tensor"),
            P("tensor", "dp"),
        ),
        check_vma=False,
    )
```

```python
import functools
import math

import jax
import jax.numpy as jnp
from jax import lax
from jax.experimental import pallas as pl
from jax.experimental.pallas import tpu as pltpu
from jax.sharding import PartitionSpec as P

H = 32
KVH = 8
HD = 64
SEQ_LEN = 2048
QB = 256
WIDE = 512

RESID = 0.22
ATTN_SCALE = 0.015625
EPSILON = 1e-05
THETA_LOG = math.log(10000000.0)
MASKED = -1e30

f32 = jnp.float32
bf16 = jnp.bfloat16
NN = (((1,), (0,)), ((), ()))
NT = (((1,), (1,)), ((), ()))
TN = (((0,), (0,)), ((), ()))


def mm(left, right, dims):
    return lax.dot_general(left, right, dims, preferred_element_type=f32)


def grant(mib):
    return pltpu.CompilerParams(vmem_limit_bytes=mib * 1024 * 1024)


def cost(flops, nbytes):
    return pl.CostEstimate(flops=int(flops), bytes_accessed=int(nbytes), transcendentals=0)


def rope_tables(count):
    lane = jnp.arange(128, dtype=jnp.int32) % (HD // 2)
    freqs = jnp.exp(-THETA_LOG * (2 * lane).astype(f32) / HD)[None, :]
    fine = jnp.arange(QB, dtype=jnp.int32)
    coarse = jnp.arange(count // QB * 8, dtype=jnp.int32) // 8 * QB
    angle_rows = jnp.concatenate([fine, coarse]).astype(f32)[:, None] * freqs
    return jnp.concatenate([jnp.cos(angle_rows), jnp.sin(angle_rows)], 1)


def turn_at(table_ref, block):
    fine = table_ref[:QB, :]
    start = pl.multiple_of(QB + block * 8, 8)
    coarse = table_ref[pl.ds(start, 8), :][:1, :]
    cos_f, sin_f, cos_c, sin_c = fine[:, :128], fine[:, 128:], coarse[:, :128], coarse[:, 128:]
    return cos_f * cos_c - sin_f * sin_c, sin_f * cos_c + cos_f * sin_c


def widen(table, count):
    return table if count == 128 else jnp.concatenate([table] * (count // 128), 1)


def swap_halves(rows):
    count = rows.shape[1]
    lane = lax.broadcasted_iota(jnp.int32, rows.shape, 1)
    ahead = pltpu.roll(rows, count - HD // 2, 1)
    behind = pltpu.roll(rows, HD // 2, 1)
    return jnp.where(lane % HD < HD // 2, ahead, behind)


def half_sign(shape):
    lane = lax.broadcasted_iota(jnp.int32, shape, 1)
    return jnp.where(lane % HD < HD // 2, -1.0, 1.0)


def rotate(rows, cosines, sines):
    count = rows.shape[1]
    turned = swap_halves(rows) * half_sign(rows.shape)
    return rows * widen(cosines, count) + turned * widen(sines, count)


def unrotate(rows, cosines, sines):
    count = rows.shape[1]
    turned = swap_halves(rows * widen(sines, count)) * half_sign(rows.shape)
    return rows * widen(cosines, count) - turned


def front_kernel(rows_ref, gain_ref, wq_ref, table_ref, normed_ref, q_ref):
    rows = rows_ref[...].astype(f32)
    row_scale = lax.rsqrt(jnp.mean(rows * rows, axis=-1, keepdims=True) + EPSILON)
    normed_ref[...] = (rows * row_scale * gain_ref[...]).astype(bf16)
    q_raw = mm(normed_ref[...], wq_ref[...], NN)
    turned = rotate(q_raw, *turn_at(table_ref, pl.program_id(0)))
    q_ref[...] = (turned.astype(bf16).astype(f32) * ATTN_SCALE).astype(bf16)


def front(hidden, gain, w_query, table):
    count, width = hidden.shape
    q_cols = w_query.shape[1]
    row = lambda i: (i, 0)
    whole = lambda i: (0, 0)
    return pl.pallas_call(
        front_kernel,
        grid=(count // QB,),
        in_specs=[
            pl.BlockSpec((QB, width), row),
            pl.BlockSpec((1, width), whole),
            pl.BlockSpec((width, q_cols), whole),
            pl.BlockSpec(table.shape, whole),
        ],
        out_specs=[pl.BlockSpec((QB, width), row), pl.BlockSpec((QB, q_cols), row)],
        out_shape=[
            jax.ShapeDtypeStruct((count, width), bf16),
            jax.ShapeDtypeStruct((count, q_cols), bf16),
        ],
        cost_estimate=cost(2 * count * width * q_cols, 5 * count * width),
        name="norm_and_query",
    )(hidden, gain, w_query, table)


def keys_kernel(length_ref, normed_ref, wkv_ref, table_ref, k_ref, kt_ref, v_ref, vt_ref):
    kv_raw = mm(normed_ref[...], wkv_ref[...], NN)
    lane = lax.broadcasted_iota(jnp.int32, kv_raw.shape, 1)
    position = pl.program_id(0) * WIDE + lax.broadcasted_iota(jnp.int32, kv_raw.shape, 0)
    blocks = [turn_at(table_ref, pl.program_id(0) * (WIDE // QB) + i) for i in range(WIDE // QB)]
    cosines, sines = (jnp.concatenate([b[i] for b in blocks], 0) for i in range(2))
    turned = rotate(kv_raw, cosines, sines)
    keys = jnp.where(lane < HD, turned, 0.0)
    blocked = jnp.where((lane == HD) & (position >= length_ref[0]), MASKED, 0.0)
    k_ref[...] = (keys + blocked).astype(bf16)
    kt_ref[...] = keys.T.astype(bf16)
    values = jnp.concatenate([kv_raw[:, HD:], kv_raw[:, :HD]], 1)
    values = jnp.where(lane < HD, values, 1.0)
    v_ref[...] = values.astype(bf16)
    vt_ref[...] = values.T.astype(bf16)


def keys_values(length, normed, w_kv, table):
    count, width = normed.shape
    row = lambda i, s: (i, 0)
    col = lambda i, s: (0, i)
    return pl.pallas_call(
        keys_kernel,
        grid_spec=pltpu.PrefetchScalarGridSpec(
            num_scalar_prefetch=1,
            grid=(count // WIDE,),
            in_specs=[
                pl.BlockSpec((WIDE, width), row),
                pl.BlockSpec((width, 128), lambda i, s: (0, 0)),
                pl.BlockSpec(table.shape, lambda i, s: (0, 0)),
            ],
            out_specs=[
                pl.BlockSpec((WIDE, 128), row),
                pl.BlockSpec((128, WIDE), col),
                pl.BlockSpec((WIDE, 128), row),
                pl.BlockSpec((128, WIDE), col),
            ],
        ),
        out_shape=[
            jax.ShapeDtypeStruct((count, 128), bf16),
            jax.ShapeDtypeStruct((128, count), bf16),
            jax.ShapeDtypeStruct((count, 128), bf16),
            jax.ShapeDtypeStruct((128, count), bf16),
        ],
        cost_estimate=cost(2 * count * width * 128, 2 * count * width),
        name="keys_and_values",
    )(length, normed, w_kv, table)


def pick_kernel(picks, k_ref, v_ref, out_ref):
    for index, head in enumerate(picks):
        both = [ref[:, 128 * (head // 2) : 128 * (head // 2) + 128] for ref in (k_ref, v_ref)]
        at = head % 2 * HD
        out_ref[index] = jnp.concatenate([b[:, at : at + HD] for b in both], 1)


def pick_heads(w_key, w_value, picks):
    return pl.pallas_call(
        functools.partial(pick_kernel, picks),
        out_shape=jax.ShapeDtypeStruct((len(picks), w_key.shape[0], 2 * HD), bf16),
        name="pick_heads",
    )(w_key, w_value)


def head_slab(rows, head, fill):
    pair = rows[:, 128 * (head // 2) : 128 * (head // 2) + 128]
    if head % 2:
        pair = jnp.concatenate([pair[:, HD:], pair[:, :HD]], 1)
    lane = lax.broadcasted_iota(jnp.int32, pair.shape, 1)
    other = jnp.where(lane == HD, jnp.full(pair.shape, fill, f32), 0.0).astype(pair.dtype)
    return jnp.where(lane < HD, pair, other)


def causal(keys_count, rows_count):
    key = lax.broadcasted_iota(jnp.int32, (keys_count, rows_count), 0)
    return key <= lax.broadcasted_iota(jnp.int32, (keys_count, rows_count), 1)


def attend_kernel(heads, q_ref, k_ref, vt_ref, o_ref, lse_ref, slab_ref, high_ref, total_ref):
    block = pl.program_id(0)
    rows = q_ref[...]
    for head in range(heads):
        slab_ref[head] = head_slab(rows, head, 1.0)
    high_ref[...] = jnp.full(high_ref.shape, MASKED, f32)
    total_ref[...] = jnp.zeros(total_ref.shape, f32)

    def step(start, width, diagonal):
        keys = k_ref[pl.ds(start, width), :]
        values = vt_ref[:, pl.ds(start, width)]
        scores = [mm(keys, slab_ref[head], NT) for head in range(heads)]
        for head in range(heads):
            score = scores[head]
            if diagonal:
                score = jnp.where(causal(width, QB), score, MASKED)
            old = high_ref[head : head + 1, :]
            new = jnp.maximum(old, jnp.max(score, axis=0, keepdims=True))
            probs = jnp.exp(score - new).astype(bf16)
            high_ref[head : head + 1, :] = new
            total_ref[head] = total_ref[head] * jnp.exp(old - new) + mm(values, probs, NN)

    def body(index, carry):
        step(pl.multiple_of(index * WIDE, WIDE), WIDE, False)
        return carry

    lax.fori_loop(0, block // 2, body, 0)

    @pl.when(block % 2 == 1)
    def _():
        step(pl.multiple_of((block - 1) * QB, QB), QB, False)

    step(pl.multiple_of(block * QB, QB), QB, True)
    outs = []
    for head in range(heads):
        total = total_ref[head]
        mass = total[HD : HD + 1, :]
        lse_ref[head : head + 1, :] = high_ref[head : head + 1, :] + jnp.log(mass)
        outs.append(total[:HD, :] * (1.0 / mass))
    o_ref[...] = jnp.concatenate(outs, 0).T.astype(bf16)


def attend(queries, keys, values_t):
    count, q_cols = queries.shape
    heads = q_cols // HD
    return pl.pallas_call(
        functools.partial(attend_kernel, heads),
        grid=(count // QB,),
        in_specs=[
            pl.BlockSpec((QB, q_cols), lambda i: (i, 0)),
            pl.BlockSpec((count, 128), lambda i: (0, 0)),
            pl.BlockSpec((128, count), lambda i: (0, 0)),
        ],
        out_specs=[
            pl.BlockSpec((QB, q_cols), lambda i: (i, 0)),
            pl.BlockSpec((8, QB), lambda i: (0, i)),
        ],
        out_shape=[
            jax.ShapeDtypeStruct((count, q_cols), bf16),
            jax.ShapeDtypeStruct((8, count), f32),
        ],
        scratch_shapes=[
            pltpu.VMEM((heads, QB, 128), bf16),
            pltpu.VMEM((8, QB), f32),
            pltpu.VMEM((heads, 128, QB), f32),
        ],
        cost_estimate=cost(heads * count * count * 512, 4 * count * q_cols),
        name="attend",
    )(queries, keys, values_t)


def attend_back_kernel(
    heads,
    q_ref,
    do_ref,
    o_ref,
    lse_ref,
    k_ref,
    kt_ref,
    v_ref,
    table_ref,
    out_ref,
    qs_ref,
    ds_ref,
    delta_ref,
    dq_ref,
    dk_ref,
    dv_ref,
):
    block = pl.program_id(0)
    blocks = pl.num_programs(0)
    q_cols = heads * HD

    @pl.when(block == 0)
    def _():
        dk_ref[...] = jnp.zeros(dk_ref.shape, f32)
        dv_ref[...] = jnp.zeros(dv_ref.shape, f32)

    rows = q_ref[...]
    grads = do_ref[...]
    product = (grads.astype(f32) * o_ref[...].astype(f32)).T
    for head in range(heads):
        qs_ref[head] = head_slab(rows, head, 1.0)
        ds_ref[head] = head_slab(grads, head, 0.0)
        delta_ref[head : head + 1, :] = jnp.sum(
            product[head * HD : (head + 1) * HD, :], axis=0, keepdims=True
        )
    dq_ref[...] = jnp.zeros(dq_ref.shape, f32)

    def step(start, diagonal):
        here = pl.ds(start, QB)
        keys = k_ref[here, :]
        keys_t = kt_ref[:, here]
        values = v_ref[here, :]
        dk = dk_ref[here, :]
        dv = dv_ref[here, :]

        def products(head):
            return (mm(keys, qs_ref[head], NT), mm(values, ds_ref[head], NT))

        ready = products(0)
        for head in range(heads):
            score, prob_grad = ready
            if head + 1 < heads:
                ready = products(head + 1)
            probs = jnp.exp(score - lse_ref[head : head + 1, :])
            if diagonal:
                probs = jnp.where(causal(QB, QB), probs, 0.0)
            dv = dv + mm(probs.astype(bf16), ds_ref[head], NN)
            score_grad = (probs * (prob_grad - delta_ref[head : head + 1, :])).astype(bf16)
            dk = dk + mm(score_grad, qs_ref[head], NN)
            dq_ref[head] = dq_ref[head] + mm(keys_t, score_grad, NN)
        dk_ref[here, :] = dk
        dv_ref[here, :] = dv

    def body(index, carry):
        step(pl.multiple_of(index * QB, QB), False)
        return carry

    lax.fori_loop(0, block, body, 0)
    step(pl.multiple_of(block * QB, QB), True)
    dq = jnp.concatenate([dq_ref[head, :HD, :] for head in range(heads)], 0).T * ATTN_SCALE
    here = pl.ds(pl.multiple_of(block * QB, QB), QB)
    out_ref[here, :q_cols] = unrotate(dq, *turn_at(table_ref, block)).astype(bf16)

    @pl.when(block == blocks - 1)
    def _():
        def finish(index, carry):
            there = pl.ds(pl.multiple_of(index * QB, QB), QB)
            dk = dk_ref[there, :]
            lane = lax.broadcasted_iota(jnp.int32, dk.shape, 1)
            dk = unrotate(jnp.where(lane < HD, dk, 0.0), *turn_at(table_ref, index))
            dv = dv_ref[there, :]
            out_ref[there, q_cols:] = jnp.concatenate([dk[:, :HD], dv[:, :HD]], 1).astype(bf16)
            return carry

        lax.fori_loop(0, blocks, finish, 0)


def attend_back(queries, out_grads, attended, lse, keys, keys_t, values, table):
    count, q_cols = queries.shape
    heads = q_cols // HD
    row = lambda i: (i, 0)
    whole = lambda i: (0, 0)
    return pl.pallas_call(
        functools.partial(attend_back_kernel, heads),
        grid=(count // QB,),
        in_specs=[
            pl.BlockSpec((QB, q_cols), row),
            pl.BlockSpec((QB, q_cols), row),
            pl.BlockSpec((QB, q_cols), row),
            pl.BlockSpec((8, QB), lambda i: (0, i)),
            pl.BlockSpec((count, 128), whole),
            pl.BlockSpec((128, count), whole),
            pl.BlockSpec((count, 128), whole),
            pl.BlockSpec(table.shape, whole),
        ],
        out_specs=pl.BlockSpec((count, q_cols + 128), whole),
        out_shape=jax.ShapeDtypeStruct((count, q_cols + 128), bf16),
        scratch_shapes=[
            pltpu.VMEM((heads, QB, 128), bf16),
            pltpu.VMEM((heads, QB, 128), bf16),
            pltpu.VMEM((8, QB), f32),
            pltpu.VMEM((heads, 128, QB), f32),
            pltpu.VMEM((count, 128), f32),
            pltpu.VMEM((count, 128), f32),
        ],
        cost_estimate=cost(heads * count * count * 1280, 10 * count * q_cols),
        name="attend_back",
    )(queries, out_grads, attended, lse, keys, keys_t, values, table)


def column_block(ref, width):
    return pl.ds(pl.multiple_of(pl.program_id(0) * width, width), width)


def out_norm_kernel(ids_ref, o_ref, w_ref, rows_ref, gain_ref, middle_ref, normed_ref):
    here = column_block(middle_ref, w_ref.shape[1])
    groups, _, q_cols = o_ref.shape
    total = mm(o_ref[0], w_ref[:q_cols, :], NN)
    for group in range(1, groups):
        total += mm(o_ref[group], w_ref[group * q_cols : (group + 1) * q_cols, :], NN)
    middle_ref[:, here] = rows_ref[:, here].astype(f32) + RESID * total

    @pl.when(pl.program_id(0) == pl.num_programs(0) - 1)
    def _():
        middle = middle_ref[...]
        row_scale = lax.rsqrt(jnp.mean(middle * middle, axis=-1, keepdims=True) + EPSILON)
        normed_ref[...] = (middle * row_scale * gain_ref[...]).astype(bf16)


def out_norm(ids, attended, w_out, hidden, gain):
    groups, share, q_cols = attended.shape
    width = hidden.shape[1]
    whole = lambda j, s: (0, 0)
    return pl.pallas_call(
        out_norm_kernel,
        grid_spec=pltpu.PrefetchScalarGridSpec(
            num_scalar_prefetch=1,
            grid=(width // WIDE,),
            in_specs=[
                pl.BlockSpec((groups, share, q_cols), lambda j, s: (0, 0, 0)),
                pl.BlockSpec((groups * q_cols, WIDE), lambda j, s: (0, j)),
                pl.BlockSpec((share, width), lambda j, s: (s[0], 0)),
                pl.BlockSpec((1, width), whole),
            ],
            out_specs=[pl.BlockSpec((share, width), whole), pl.BlockSpec((share, width), whole)],
        ),
        out_shape=[
            jax.ShapeDtypeStruct((share, width), f32),
            jax.ShapeDtypeStruct((share, width), bf16),
        ],
        cost_estimate=cost(2 * groups * share * q_cols * width, 2 * groups * q_cols * width),
        name="out_project_and_norm",
    )(ids, attended, w_out, hidden, gain)


def norm_back_kernel(
    parts,
    ids_ref,
    *refs,
):
    part_refs = refs[:parts]
    middle_ref, gain_ref, cotangent_ref, w_ref, dh_ref, da_ref, gain_grad_ref, do_ref = refs[parts:]

    @pl.when(pl.program_id(0) == 0)
    def _():
        incoming = part_refs[0][...].astype(f32)
        for ref in part_refs[1:]:
            incoming = incoming + ref[...].astype(f32)
        middle = middle_ref[...]
        row_scale = lax.rsqrt(jnp.mean(middle * middle, axis=-1, keepdims=True) + EPSILON)
        normed = middle * row_scale
        gain_grad_ref[...] = jnp.sum(incoming * normed, axis=0, keepdims=True)
        scaled = incoming * gain_ref[...]
        branch = row_scale * (scaled - normed * jnp.mean(scaled * normed, axis=-1, keepdims=True))
        share = middle.shape[0]
        position = ids_ref[0] * share + lax.broadcasted_iota(jnp.int32, (share, 1), 0)
        direct = jnp.where(position < ids_ref[1], cotangent_ref[...].astype(f32), 0.0)
        dh = direct + branch
        dh_ref[...] = dh
        da_ref[...] = (RESID * dh).astype(bf16)

    per_step, _, q_cols = do_ref.shape
    for index in range(per_step):
        rows = w_ref[index * q_cols : (index + 1) * q_cols, :]
        do_ref[index] = mm(da_ref[...], rows, NT).astype(bf16)


def norm_back(ids, parts, middle, gain, cotangent, w_out, q_cols):
    share, width = middle.shape
    groups = w_out.shape[0] // q_cols
    per_step = WIDE // q_cols
    whole = lambda t, s: (0, 0)
    return pl.pallas_call(
        functools.partial(norm_back_kernel, len(parts)),
        grid_spec=pltpu.PrefetchScalarGridSpec(
            num_scalar_prefetch=1,
            grid=(groups // per_step,),
            in_specs=[pl.BlockSpec((share, width), whole)] * len(parts)
            + [
                pl.BlockSpec((share, width), whole),
                pl.BlockSpec((1, width), whole),
                pl.BlockSpec((share, width), lambda t, s: (s[0], 0)),
                pl.BlockSpec((WIDE, width), lambda t, s: (t, 0)),
            ],
            out_specs=[
                pl.BlockSpec((share, width), whole),
                pl.BlockSpec((share, width), whole),
                pl.BlockSpec((1, width), whole),
                pl.BlockSpec((per_step, share, q_cols), lambda t, s: (t, 0, 0)),
            ],
        ),
        out_shape=[
            jax.ShapeDtypeStruct((share, width), f32),
            jax.ShapeDtypeStruct((share, width), bf16),
            jax.ShapeDtypeStruct((1, width), f32),
            jax.ShapeDtypeStruct((groups, share, q_cols), bf16),
        ],
        cost_estimate=cost(2 * groups * share * q_cols * width, 2 * groups * q_cols * width),
        name="norm_back_and_project",
    )(ids, *parts, middle, gain, cotangent, w_out)


def in_grad_kernel(ids_ref, d_ref, w_ref, rows_ref, gain_ref, dh_ref, out_ref):
    here = column_block(out_ref, w_ref.shape[1])
    total = mm(d_ref[0], w_ref[0], NT)
    for group in range(1, d_ref.shape[0]):
        total += mm(d_ref[group], w_ref[group], NT)
    out_ref[:, here] = total

    @pl.when(pl.program_id(0) == pl.num_programs(0) - 1)
    def _():
        rows = rows_ref[...].astype(f32)
        row_scale = lax.rsqrt(jnp.mean(rows * rows, axis=-1, keepdims=True) + EPSILON)
        normed = rows * row_scale
        scaled = out_ref[...] * gain_ref[...]
        branch = row_scale * (scaled - normed * jnp.mean(scaled * normed, axis=-1, keepdims=True))
        out_ref[...] = dh_ref[...] + branch


def in_grad(ids, grads, w_qkv, hidden, gain, dh):
    groups, share, cols = grads.shape
    width = hidden.shape[1]
    whole = lambda j, s: (0, 0)
    return pl.pallas_call(
        in_grad_kernel,
        grid_spec=pltpu.PrefetchScalarGridSpec(
            num_scalar_prefetch=1,
            grid=(width // WIDE,),
            in_specs=[
                pl.BlockSpec((groups, share, cols), lambda j, s: (0, 0, 0)),
                pl.BlockSpec((groups, WIDE, cols), lambda j, s: (0, j, 0)),
                pl.BlockSpec((share, width), lambda j, s: (s[0], 0)),
                pl.BlockSpec((1, width), whole),
                pl.BlockSpec((share, width), whole),
            ],
            out_specs=pl.BlockSpec((share, width), whole),
        ),
        out_shape=jax.ShapeDtypeStruct((share, width), f32),
        cost_estimate=cost(2 * groups * share * cols * width, 2 * groups * cols * width),
        name="input_grad",
    )(ids, grads, w_qkv, hidden, gain, dh)


def out_wgrad_kernel(core_ref, o_ref, da_ref, send_ref, keep_ref):
    step = pl.program_id(0)
    groups, _, q_cols = o_ref.shape

    def store(ref):
        for group in range(groups):
            part = mm(o_ref[group], da_ref[...], TN)
            ref[0, group * q_cols : (group + 1) * q_cols, :] = part.astype(bf16)

    half = pl.num_programs(0) // 2
    pl.when(step < half)(lambda: store(send_ref))
    pl.when(step >= half)(lambda: store(keep_ref))


def out_wgrad_parts(core, attended, branch_grad, replicas):
    groups, share, q_cols = attended.shape
    width = branch_grad.shape[1]
    cols = width // replicas
    chips = replicas // 2
    column = lambda i, s: jnp.where(i < chips, 2 * i + 1 - s[0], 2 * (i - chips) + s[0])
    out = jax.ShapeDtypeStruct((chips, groups * q_cols, cols), bf16)
    block = (1, groups * q_cols, cols)
    return pl.pallas_call(
        out_wgrad_kernel,
        grid_spec=pltpu.PrefetchScalarGridSpec(
            num_scalar_prefetch=1,
            grid=(replicas,),
            in_specs=[
                pl.BlockSpec((groups, share, q_cols), lambda i, s: (0, 0, 0)),
                pl.BlockSpec((share, cols), lambda i, s: (0, column(i, s))),
            ],
            out_specs=[
                pl.BlockSpec(block, lambda i, s: (jnp.minimum(i, chips - 1), 0, 0)),
                pl.BlockSpec(block, lambda i, s: (jnp.maximum(i - chips, 0), 0, 0)),
            ],
        ),
        out_shape=[out, out],
        cost_estimate=cost(2 * groups * share * q_cols * width, 2 * groups * q_cols * width),
        name="out_weight_grad",
    )(core, attended, branch_grad)


def swiglu(normed, down_in, w_gate, w_up, w_down):
    gate = mm(normed, w_gate, NN)
    up = mm(normed, w_up, NN)
    act_grad = mm(down_in, w_down, NT)
    sg = jax.nn.sigmoid(gate)
    silu = gate * sg
    act = (silu * up).astype(bf16)
    gate_grad = (act_grad * up * sg * (1.0 + gate * (1.0 - sg))).astype(bf16)
    up_grad = (act_grad * silu).astype(bf16)
    normed_grad = (mm(gate_grad, w_gate, NT) + mm(up_grad, w_up, NT)).astype(bf16)
    return act, gate_grad, up_grad, normed_grad


def ring_order(count):
    inner = 2 if count <= 8 else 4
    outer = count // inner
    cells = [(0, 0)]
    for row in range(outer):
        cells += [(row, c) for c in (range(1, inner) if row % 2 == 0 else range(inner - 1, 0, -1))]
    cells += [(row, 0) for row in range(outer - 1, 0, -1)]
    return [row * inner + c for row, c in cells]


def add_low(left, right):
    return (left.astype(f32) + right.astype(f32)).astype(bf16)


def tie(*values):
    return lax.optimization_barrier(values)


def split_by_core(parts):
    replicas = parts.shape[0]
    core = lax.axis_index("dp") % 2
    by_core = parts.reshape((replicas // 2, 2) + parts.shape[1:])
    take = lambda i: lax.dynamic_index_in_dim(by_core, i, 1, keepdims=False)
    return take(1 - core), take(core)


def over_dp(send, keep):
    chips = send.shape[0]
    replicas = 2 * chips
    chip = lax.axis_index("dp") // 2
    take = lambda a, i: lax.dynamic_index_in_dim(a, i, 0, keepdims=False)
    got = lax.ppermute(send, "dp", [(i, i ^ 1) for i in range(replicas)])
    total = take(keep, chip).astype(f32) + take(got, chip).astype(f32)
    for step in range(1, chips):
        there = (chip + step) % chips
        term = take(keep, there).astype(f32) + take(got, there).astype(f32)
        moved = lax.ppermute(
            term.astype(send.dtype),
            "dp",
            [(i, ((i // 2 + step) % chips) * 2 + i % 2) for i in range(replicas)],
        )
        total = total + moved.astype(f32)
    return total


def local(
    hidden_in,
    seq_lengths,
    out_grad,
    attn_gain,
    mlp_gain,
    w_query,
    w_key,
    w_value,
    w_out,
    w_gate,
    w_up,
    w_down,
):
    rows_total, width = hidden_in.shape
    q_cols = w_query.shape[1]
    heads_here = q_cols // HD
    groups = lax.axis_size("tensor")
    replicas = lax.axis_size("dp")
    member = lax.axis_index("tensor")
    replica = lax.axis_index("dp")
    share = rows_total // groups
    order = ring_order(groups)
    place = [order.index(i) for i in range(groups)]
    ahead = [(order[i], order[(i + 1) % groups]) for i in range(groups)]
    behind = [(b, a) for a, b in ahead]
    half_way = groups // 2
    chunks = [
        [order[(place[i] + d) % groups] for d in range(-half_way + 1, half_way + 1)]
        for i in range(groups)
    ]
    near = jnp.asarray(chunks, jnp.int32)[member]
    at = lambda d: near[d + half_way - 1]
    length = seq_lengths[0]
    own_id = jnp.stack([member, length])
    table = rope_tables(rows_total)
    gain_one = attn_gain[None, :]
    gain_two = mlp_gain[None, :]
    half = share // 2

    def quarter(array):
        count = array.shape[0] // replicas
        return lax.dynamic_slice_in_dim(array, replica * count, count, 0)

    def exchange(array):
        return lax.all_to_all(array, "tensor", 0, 0, tiled=True)

    w_out_all = lax.all_gather(quarter(w_out), ("tensor", "dp"), axis=0, tiled=True)
    kv_of = [i * heads_here // (H // KVH) for i in range(groups)]
    w_kv = exchange(pick_heads(w_key, w_value, kv_of)).reshape(width, 2 * HD)
    normed_one, queries = front(hidden_in, gain_one, w_query, table)
    w_kv, normed_one = tie(w_kv, normed_one)
    w_qkv = jnp.concatenate([w_query, w_kv], 1)
    w_qkv_all = lax.all_gather(quarter(w_qkv), ("tensor", "dp"), axis=0, tiled=True)
    w_qkv_all = w_qkv_all.reshape(groups, width, q_cols + 2 * HD)
    keys, keys_t, values, values_t = keys_values(seq_lengths, normed_one, w_kv, table)
    attended, lse = attend(queries, keys, values_t)
    attended_rows = exchange(attended.reshape(groups, share, q_cols))
    positions = jnp.arange(rows_total, dtype=jnp.int32)[:, None]
    down_in = (jnp.where(positions < length, out_grad.astype(f32), 0.0) * RESID).astype(bf16)
    attended_rows, down_in = tie(attended_rows, down_in)
    middle, normed_two = out_norm(own_id, attended_rows, w_out_all, hidden_in, gain_two)
    normed_two, down_in = tie(normed_two, down_in)

    weights = (w_gate, w_up, w_down)
    chunk = lambda i: lax.dynamic_slice_in_dim(down_in, i * share, share, 0)
    ring_rows, ring_down, done = [normed_two], [chunk(member)], []
    from_behind = from_ahead = normed_two
    for distance in range(1, half_way + 1):
        if distance < half_way:
            from_behind = lax.ppermute(from_behind, "tensor", ahead)
            from_ahead = lax.ppermute(from_ahead, "tensor", behind)
        else:
            from_behind = lax.ppermute(from_behind[:half], "tensor", ahead)
            from_ahead = lax.ppermute(from_ahead[half:], "tensor", behind)
        units = swiglu(ring_rows[-1], ring_down[-1], *weights)
        from_behind, from_ahead, *units = tie(from_behind, from_ahead, *units)
        done.append(units)
        ring_rows.append(jnp.concatenate([from_behind, from_ahead], 0))
        if distance < half_way:
            ring_down.append(jnp.concatenate([chunk(at(-distance)), chunk(at(distance))], 0))
        else:
            ring_down.append(chunk(at(half_way)))
    done.append(swiglu(ring_rows[-1], ring_down[-1], *weights))
    act, gate_grad, up_grad = (jnp.concatenate([d[i] for d in done], 0) for i in range(3))
    normed_ring = jnp.concatenate(ring_rows, 0)
    down_ring = jnp.concatenate(ring_down, 0)

    def first_hop(far):
        return (
            lax.ppermute(far[:half], "tensor", ahead),
            lax.ppermute(far[half:], "tensor", behind),
        )

    def next_hop(pair, got, first):
        down, up = pair[:share], pair[share:]
        if first:
            up = jnp.concatenate([add_low(up[:half], got[0]), up[half:]], 0)
            down = jnp.concatenate([down[:half], add_low(down[half:], got[1])], 0)
        else:
            up, down = add_low(up, got[0]), add_low(down, got[1])
        return lax.ppermute(up, "tensor", ahead), lax.ppermute(down, "tensor", behind)

    grads = [d[3] for d in done]
    got = first_hop(grads[-1])
    mlp = mm(act, w_down, NN).astype(bf16)
    got, mlp = tie(got, mlp)
    fillers = [
        lambda: mm(act, down_ring, TN).astype(bf16),
        lambda: mm(normed_ring, gate_grad, TN).astype(bf16),
        lambda: mm(normed_ring, up_grad, TN).astype(bf16),
    ]
    filled = []
    for hop, pair in enumerate(reversed(grads[1:-1])):
        got = next_hop(pair, got, hop == 0)
        if hop < len(fillers):
            got, value = tie(got, fillers[hop]())
            filled.append(value)
    down_wgrad, gate_wgrad, up_wgrad = filled
    scatter = lambda a, d: lax.psum_scatter(a, "dp", scatter_dimension=d, tiled=True)
    down_wgrad = scatter(down_wgrad, 1)
    gate_wgrad = scatter(gate_wgrad, 0)
    up_wgrad = scatter(up_wgrad, 0)

    bounds = [0, share] + [share + 2 * share * d for d in range(1, half_way)] + [rows_total]
    mlp = [mlp[a:b] for a, b in zip(bounds[:-1], bounds[1:])]
    mlp_own, mlp_far, mlp_pairs = mlp[0], mlp[-1], list(reversed(mlp[1:-1]))
    got, mlp_far = tie(got, mlp_far)
    mlp_got = first_hop(mlp_far)
    middle_grad, branch_grad, mlp_gain_part, do_send = norm_back(
        own_id, [grads[0], *got], middle, gain_two, out_grad, w_out_all, q_cols
    )
    mlp_got, do_send, branch_grad = tie(mlp_got, do_send, branch_grad)
    attended_grad = exchange(do_send).reshape(rows_total, q_cols)
    core_id = (replica % 2)[None]
    out_parts = out_wgrad_parts(core_id, attended_rows, branch_grad, replicas)
    mlp_got = next_hop(mlp_pairs[0], mlp_got, True)
    attended_grad, mlp_got, *out_parts = tie(attended_grad, mlp_got, *out_parts)
    out_wgrad = over_dp(*out_parts).astype(bf16)
    mlp_got = next_hop(mlp_pairs[1], mlp_got, False)
    qkv_grad = attend_back(
        queries, attended_grad, attended, lse, keys, keys_t, values, table
    )
    mlp_got, qkv_grad, down_wgrad = tie(mlp_got, qkv_grad, down_wgrad)
    qkv_rows = exchange(qkv_grad.reshape(groups, share, q_cols + 2 * HD))

    qkv_wgrad = mm(normed_one, qkv_grad, TN)
    qkv_rows, qkv_wgrad, gate_wgrad = tie(qkv_rows, qkv_wgrad, gate_wgrad)
    attn_gain_part = jnp.sum(qkv_wgrad * w_qkv.astype(f32), axis=1) / attn_gain
    small = jnp.concatenate(
        [
            qkv_wgrad[:, q_cols:],
            attn_gain_part[:, None],
            mlp_gain_part[0][:, None],
            jnp.zeros((width, 126), f32),
        ],
        1,
    )
    small = over_dp(*split_by_core(small.reshape(replicas, -1, 256)))
    query_wgrad = qkv_wgrad[:, :q_cols].astype(bf16).reshape(replicas, -1, q_cols)
    query_wgrad = over_dp(*split_by_core(query_wgrad))
    pieces = exchange(small.reshape(groups, small.shape[0] // groups, 256))
    input_grad = in_grad(own_id, qkv_rows, w_qkv_all, hidden_in, gain_one, middle_grad)
    for pair in mlp_pairs[2:]:
        mlp_got = next_hop(pair, mlp_got, False)
    layer_out = (
        middle
        + RESID * (mlp_own.astype(f32) + mlp_got[0].astype(f32) + mlp_got[1].astype(f32))
    ).astype(bf16)
    gains = jnp.sum(pieces[:, :, 128:130], axis=0)
    kv = pieces[:, :, :128].reshape(KVH, groups // KVH, -1, 128).sum(axis=1)
    kv = jnp.swapaxes(kv, 0, 1)
    key_wgrad = kv[:, :, :HD].reshape(-1, KVH * HD)
    value_wgrad = kv[:, :, HD:].reshape(-1, KVH * HD)
    out_wgrad = lax.psum_scatter(out_wgrad, "tensor", scatter_dimension=0, tiled=True).astype(f32)
    return (
        layer_out,
        input_grad,
        gains[:, 0],
        gains[:, 1],
        query_wgrad,
        key_wgrad,
        value_wgrad,
        out_wgrad,
        gate_wgrad.astype(f32),
        up_wgrad.astype(f32),
        down_wgrad.astype(f32),
    )


def solution(mesh):
    placed = (
        P("dp", None),
        P("dp"),
        P("dp", None),
        P(),
        P(),
        P(None, "tensor"),
        P("tensor", None),
        P("tensor", None),
        P("tensor", None),
        P(None, "tensor"),
        P(None, "tensor"),
        P("tensor", None),
    )
    return jax.shard_map(
        local,
        mesh=mesh,
        in_specs=placed,
        out_specs=(
            P(("dp", "tensor"), None),
            P(("dp", "tensor"), None),
            P(("dp", "tensor")),
            P(("dp", "tensor")),
            P("dp", "tensor"),
            P(("dp", "tensor"), None),
            P(("dp", "tensor"), None),
            P("tensor", "dp"),
            P("dp", "tensor"),
            P("dp", "tensor"),
            P("tensor", "dp"),
        ),
        check_vma=False,
    )
```

```python
import functools
import math

import jax
import jax.numpy as jnp
from jax import lax
from jax.experimental import pallas as pl
from jax.experimental.pallas import tpu as pltpu
from jax.sharding import PartitionSpec as P

H = 32
KVH = 8
HD = 64
SEQ_LEN = 2048
QB = 256
WIDE = 512

RESID = 0.22
ATTN_SCALE = 0.015625
EPSILON = 1e-05
THETA_LOG = math.log(10000000.0)
MASKED = -1e30

f32 = jnp.float32
bf16 = jnp.bfloat16
NN = (((1,), (0,)), ((), ()))
NT = (((1,), (1,)), ((), ()))
TN = (((0,), (0,)), ((), ()))


def mm(left, right, dims):
    return lax.dot_general(left, right, dims, preferred_element_type=f32)


def grant(mib):
    return pltpu.CompilerParams(vmem_limit_bytes=mib * 1024 * 1024)


def cost(flops, nbytes):
    return pl.CostEstimate(flops=int(flops), bytes_accessed=int(nbytes), transcendentals=0)


def rope_tables(count):
    lane = jnp.arange(128, dtype=jnp.int32) % (HD // 2)
    freqs = jnp.exp(-THETA_LOG * (2 * lane).astype(f32) / HD)[None, :]
    fine = jnp.arange(QB, dtype=jnp.int32)
    coarse = jnp.arange(count // QB * 8, dtype=jnp.int32) // 8 * QB
    angle_rows = jnp.concatenate([fine, coarse]).astype(f32)[:, None] * freqs
    return jnp.concatenate([jnp.cos(angle_rows), jnp.sin(angle_rows)], 1)


def turn_at(table_ref, block):
    fine = table_ref[:QB, :]
    coarse = table_ref[pl.ds(pl.multiple_of(QB + block * 8, 8), 8), :][:1, :]
    cos_f, sin_f, cos_c, sin_c = fine[:, :128], fine[:, 128:], coarse[:, :128], coarse[:, 128:]
    return cos_f * cos_c - sin_f * sin_c, sin_f * cos_c + cos_f * sin_c


def widen(table, count):
    return table if count == 128 else jnp.concatenate([table] * (count // 128), 1)


def swap_halves(rows):
    count = rows.shape[1]
    lane = lax.broadcasted_iota(jnp.int32, rows.shape, 1)
    ahead = pltpu.roll(rows, count - HD // 2, 1)
    behind = pltpu.roll(rows, HD // 2, 1)
    return jnp.where(lane % HD < HD // 2, ahead, behind)


def half_sign(shape):
    lane = lax.broadcasted_iota(jnp.int32, shape, 1)
    return jnp.where(lane % HD < HD // 2, -1.0, 1.0)


def rotate(rows, cosines, sines):
    count = rows.shape[1]
    turned = swap_halves(rows) * half_sign(rows.shape)
    return rows * widen(cosines, count) + turned * widen(sines, count)


def unrotate(rows, cosines, sines):
    count = rows.shape[1]
    turned = swap_halves(rows * widen(sines, count)) * half_sign(rows.shape)
    return rows * widen(cosines, count) - turned


def front_kernel(rows_ref, gain_ref, wq_ref, table_ref, normed_ref, q_ref):
    rows = rows_ref[...].astype(f32)
    row_scale = lax.rsqrt(jnp.mean(rows * rows, axis=-1, keepdims=True) + EPSILON)
    normed_ref[...] = (rows * row_scale * gain_ref[...]).astype(bf16)
    q_raw = mm(normed_ref[...], wq_ref[...], NN)
    turned = rotate(q_raw, *turn_at(table_ref, pl.program_id(0)))
    q_ref[...] = (turned.astype(bf16).astype(f32) * ATTN_SCALE).astype(bf16)


def front(hidden, gain, w_query, table):
    count, width = hidden.shape
    q_cols = w_query.shape[1]
    row = lambda i: (i, 0)
    whole = lambda i: (0, 0)
    return pl.pallas_call(
        front_kernel,
        grid=(count // QB,),
        in_specs=[
            pl.BlockSpec((QB, width), row),
            pl.BlockSpec((1, width), whole),
            pl.BlockSpec((width, q_cols), whole),
            pl.BlockSpec(table.shape, whole),
        ],
        out_specs=[pl.BlockSpec((QB, width), row), pl.BlockSpec((QB, q_cols), row)],
        out_shape=[
            jax.ShapeDtypeStruct((count, width), bf16),
            jax.ShapeDtypeStruct((count, q_cols), bf16),
        ],
        cost_estimate=cost(2 * count * width * q_cols, 5 * count * width),
        name="norm_and_query",
    )(hidden, gain, w_query, table)


def keys_kernel(length_ref, normed_ref, wkv_ref, table_ref, k_ref, kt_ref, v_ref, vt_ref):
    kv_raw = mm(normed_ref[...], wkv_ref[...], NN)
    lane = lax.broadcasted_iota(jnp.int32, kv_raw.shape, 1)
    position = pl.program_id(0) * WIDE + lax.broadcasted_iota(jnp.int32, kv_raw.shape, 0)
    blocks = [turn_at(table_ref, pl.program_id(0) * (WIDE // QB) + i) for i in range(WIDE // QB)]
    cosines, sines = (jnp.concatenate([b[i] for b in blocks], 0) for i in range(2))
    turned = rotate(kv_raw, cosines, sines)
    keys = jnp.where(lane < HD, turned, 0.0)
    blocked = jnp.where((lane == HD) & (position >= length_ref[0]), MASKED, 0.0)
    k_ref[...] = (keys + blocked).astype(bf16)
    kt_ref[...] = keys.T.astype(bf16)
    values = jnp.concatenate([kv_raw[:, HD:], kv_raw[:, :HD]], 1)
    values = jnp.where(lane < HD, values, 1.0)
    v_ref[...] = values.astype(bf16)
    vt_ref[...] = values.T.astype(bf16)


def keys_values(length, normed, w_kv, table):
    count, width = normed.shape
    row = lambda i, s: (i, 0)
    col = lambda i, s: (0, i)
    return pl.pallas_call(
        keys_kernel,
        grid_spec=pltpu.PrefetchScalarGridSpec(
            num_scalar_prefetch=1,
            grid=(count // WIDE,),
            in_specs=[
                pl.BlockSpec((WIDE, width), row),
                pl.BlockSpec((width, 128), lambda i, s: (0, 0)),
                pl.BlockSpec(table.shape, lambda i, s: (0, 0)),
            ],
            out_specs=[
                pl.BlockSpec((WIDE, 128), row),
                pl.BlockSpec((128, WIDE), col),
                pl.BlockSpec((WIDE, 128), row),
                pl.BlockSpec((128, WIDE), col),
            ],
        ),
        out_shape=[
            jax.ShapeDtypeStruct((count, 128), bf16),
            jax.ShapeDtypeStruct((128, count), bf16),
            jax.ShapeDtypeStruct((count, 128), bf16),
            jax.ShapeDtypeStruct((128, count), bf16),
        ],
        cost_estimate=cost(2 * count * width * 128, 2 * count * width),
        name="keys_and_values",
    )(length, normed, w_kv, table)


def pick_kernel(picks, k_ref, v_ref, out_ref):
    for index, head in enumerate(picks):
        both = [ref[:, 128 * (head // 2) : 128 * (head // 2) + 128] for ref in (k_ref, v_ref)]
        at = head % 2 * HD
        out_ref[index] = jnp.concatenate([b[:, at : at + HD] for b in both], 1)


def pick_heads(w_key, w_value, picks):
    return pl.pallas_call(
        functools.partial(pick_kernel, picks),
        out_shape=jax.ShapeDtypeStruct((len(picks), w_key.shape[0], 2 * HD), bf16),
        name="pick_heads",
    )(w_key, w_value)


def head_slab(rows, head, fill):
    pair = rows[:, 128 * (head // 2) : 128 * (head // 2) + 128]
    if head % 2:
        pair = jnp.concatenate([pair[:, HD:], pair[:, :HD]], 1)
    lane = lax.broadcasted_iota(jnp.int32, pair.shape, 1)
    other = jnp.where(lane == HD, jnp.full(pair.shape, fill, f32), 0.0).astype(pair.dtype)
    return jnp.where(lane < HD, pair, other)


def causal(keys_count, rows_count):
    key = lax.broadcasted_iota(jnp.int32, (keys_count, rows_count), 0)
    return key <= lax.broadcasted_iota(jnp.int32, (keys_count, rows_count), 1)


def attend_kernel(heads, q_ref, k_ref, vt_ref, o_ref, lse_ref, slab_ref, high_ref, total_ref):
    block = pl.program_id(0)
    rows = q_ref[...]
    for head in range(heads):
        slab_ref[head] = head_slab(rows, head, 1.0)
    high_ref[...] = jnp.full(high_ref.shape, MASKED, f32)
    total_ref[...] = jnp.zeros(total_ref.shape, f32)

    def step(start, width, diagonal):
        keys = k_ref[pl.ds(start, width), :]
        values = vt_ref[:, pl.ds(start, width)]
        scores = [mm(keys, slab_ref[head], NT) for head in range(heads)]
        for head in range(heads):
            score = scores[head]
            if diagonal:
                score = jnp.where(causal(width, QB), score, MASKED)
            old = high_ref[head : head + 1, :]
            new = jnp.maximum(old, jnp.max(score, axis=0, keepdims=True))
            probs = jnp.exp(score - new).astype(bf16)
            high_ref[head : head + 1, :] = new
            total_ref[head] = total_ref[head] * jnp.exp(old - new) + mm(values, probs, NN)

    def body(index, carry):
        step(pl.multiple_of(index * WIDE, WIDE), WIDE, False)
        return carry

    lax.fori_loop(0, block // 2, body, 0)

    @pl.when(block % 2 == 1)
    def _():
        step(pl.multiple_of((block - 1) * QB, QB), QB, False)

    step(pl.multiple_of(block * QB, QB), QB, True)
    outs = []
    for head in range(heads):
        total = total_ref[head]
        mass = total[HD : HD + 1, :]
        lse_ref[head : head + 1, :] = high_ref[head : head + 1, :] + jnp.log(mass)
        outs.append(total[:HD, :] * (1.0 / mass))
    o_ref[...] = jnp.concatenate(outs, 0).T.astype(bf16)


def attend(queries, keys, values_t):
    count, q_cols = queries.shape
    heads = q_cols // HD
    return pl.pallas_call(
        functools.partial(attend_kernel, heads),
        grid=(count // QB,),
        in_specs=[
            pl.BlockSpec((QB, q_cols), lambda i: (i, 0)),
            pl.BlockSpec((count, 128), lambda i: (0, 0)),
            pl.BlockSpec((128, count), lambda i: (0, 0)),
        ],
        out_specs=[
            pl.BlockSpec((QB, q_cols), lambda i: (i, 0)),
            pl.BlockSpec((8, QB), lambda i: (0, i)),
        ],
        out_shape=[
            jax.ShapeDtypeStruct((count, q_cols), bf16),
            jax.ShapeDtypeStruct((8, count), f32),
        ],
        scratch_shapes=[
            pltpu.VMEM((heads, QB, 128), bf16),
            pltpu.VMEM((8, QB), f32),
            pltpu.VMEM((heads, 128, QB), f32),
        ],
        cost_estimate=cost(heads * count * count * 512, 4 * count * q_cols),
        name="attend",
    )(queries, keys, values_t)


def attend_back_kernel(
    heads,
    first,
    q_ref,
    do_ref,
    o_ref,
    lse_ref,
    k_ref,
    kt_ref,
    v_ref,
    table_ref,
    *refs,
):
    carried = refs[:3] if first else ()
    outs = refs[len(carried) : -6]
    qs_ref, ds_ref, delta_ref, dq_ref, dk_ref, dv_ref = refs[-6:]
    step_id = pl.program_id(0)
    block = first + step_id
    last = pl.num_programs(0) - 1
    q_cols = heads * HD

    @pl.when(step_id == 0)
    def _():
        dk_ref[...] = carried[1][...] if first else jnp.zeros(dk_ref.shape, f32)
        dv_ref[...] = carried[2][...] if first else jnp.zeros(dv_ref.shape, f32)
        if first:
            outs[0][: first * QB, :q_cols] = carried[0][...]

    rows = q_ref[...]
    grads = do_ref[...]
    product = (grads.astype(f32) * o_ref[...].astype(f32)).T
    for head in range(heads):
        qs_ref[head] = head_slab(rows, head, 1.0)
        ds_ref[head] = head_slab(grads, head, 0.0)
        delta_ref[head : head + 1, :] = jnp.sum(
            product[head * HD : (head + 1) * HD, :], axis=0, keepdims=True
        )
    dq_ref[...] = jnp.zeros(dq_ref.shape, f32)

    def step(start, diagonal):
        here = pl.ds(start, QB)
        keys = k_ref[here, :]
        keys_t = kt_ref[:, here]
        values = v_ref[here, :]
        dk = dk_ref[here, :]
        dv = dv_ref[here, :]

        def products(head):
            return (mm(keys, qs_ref[head], NT), mm(values, ds_ref[head], NT))

        ready = products(0)
        for head in range(heads):
            score, prob_grad = ready
            if head + 1 < heads:
                ready = products(head + 1)
            probs = jnp.exp(score - lse_ref[head : head + 1, :])
            if diagonal:
                probs = jnp.where(causal(QB, QB), probs, 0.0)
            dv = dv + mm(probs.astype(bf16), ds_ref[head], NN)
            score_grad = (probs * (prob_grad - delta_ref[head : head + 1, :])).astype(bf16)
            dk = dk + mm(score_grad, qs_ref[head], NN)
            dq_ref[head] = dq_ref[head] + mm(keys_t, score_grad, NN)
        dk_ref[here, :] = dk
        dv_ref[here, :] = dv

    def body(index, carry):
        step(pl.multiple_of(index * QB, QB), False)
        return carry

    lax.fori_loop(0, block, body, 0)
    step(pl.multiple_of(block * QB, QB), True)
    dq = jnp.concatenate([dq_ref[head, :HD, :] for head in range(heads)], 0).T * ATTN_SCALE
    here = pl.ds(pl.multiple_of(block * QB, QB), QB)
    dq = unrotate(dq, *turn_at(table_ref, block)).astype(bf16)
    if first:
        outs[0][here, :q_cols] = dq
    else:
        outs[0][...] = dq

    @pl.when(step_id == last)
    def _():
        if not first:
            outs[1][...] = dk_ref[...]
            outs[2][...] = dv_ref[...]
            return

        def finish(index, carry):
            there = pl.ds(pl.multiple_of(index * QB, QB), QB)
            dk = dk_ref[there, :]
            lane = lax.broadcasted_iota(jnp.int32, dk.shape, 1)
            dk = unrotate(jnp.where(lane < HD, dk, 0.0), *turn_at(table_ref, index))
            dv = dv_ref[there, :]
            outs[0][there, q_cols:] = jnp.concatenate([dk[:, :HD], dv[:, :HD]], 1).astype(bf16)
            return carry

        lax.fori_loop(0, dk_ref.shape[0] // QB, finish, 0)


def attend_back(first, queries, out_grads, attended, lse, keys, keys_t, values, table, carried):
    count, q_cols = queries.shape
    heads = q_cols // HD
    blocks = count // QB
    split = blocks * 5 // 8
    steps = blocks - split if first else split
    start = split if first else 0
    row = lambda i: (start + i, 0)
    whole = lambda i: (0, 0)
    total = pl.BlockSpec((count, 128), whole)
    total_shape = jax.ShapeDtypeStruct((count, 128), f32)
    early = (split * QB, q_cols)
    if first:
        out_specs = pl.BlockSpec((count, q_cols + 128), whole)
        out_shape = jax.ShapeDtypeStruct((count, q_cols + 128), bf16)
    else:
        out_specs = [pl.BlockSpec((QB, q_cols), row), total, total]
        out_shape = [jax.ShapeDtypeStruct(early, bf16), total_shape, total_shape]
    return pl.pallas_call(
        functools.partial(attend_back_kernel, heads, start),
        grid=(steps,),
        in_specs=[
            pl.BlockSpec((QB, q_cols), row),
            pl.BlockSpec((QB, q_cols), row),
            pl.BlockSpec((QB, q_cols), row),
            pl.BlockSpec((8, QB), lambda i: (0, start + i)),
            total,
            pl.BlockSpec((128, count), whole),
            total,
            pl.BlockSpec(table.shape, whole),
        ]
        + ([pl.BlockSpec(early, whole), total, total] if first else []),
        out_specs=out_specs,
        out_shape=out_shape,
        scratch_shapes=[
            pltpu.VMEM((heads, QB, 128), bf16),
            pltpu.VMEM((heads, QB, 128), bf16),
            pltpu.VMEM((8, QB), f32),
            pltpu.VMEM((heads, 128, QB), f32),
            pltpu.VMEM((count, 128), f32),
            pltpu.VMEM((count, 128), f32),
        ],
        cost_estimate=cost(heads * count * count * 640, 10 * count * q_cols),
        name="attend_back",
    )(queries, out_grads, attended, lse, keys, keys_t, values, table, *carried)


LENGTH, CORE, RING = 0, 1, 2


def out_norm_kernel(ids_ref, o_ref, mine_ref, other_ref, rows_ref, gain_ref, middle_ref, normed_ref):
    step = pl.program_id(0)
    steps = pl.num_programs(0)
    groups, _, q_cols = o_ref.shape
    cols = mine_ref.shape[1]

    def work(w_ref, core, index):
        total = None
        for place in range(groups):
            term = mm(
                o_ref[ids_ref[RING + place]], w_ref[place * q_cols : (place + 1) * q_cols, :], NN
            )
            total = term if total is None else total + term
        first = core * (steps // 2) + index
        here = pl.ds(pl.multiple_of(first * cols, cols), cols)
        middle_ref[:, here] = rows_ref[:, here].astype(f32) + RESID * total

    core = ids_ref[CORE]
    pl.when(step < steps // 2)(lambda: work(mine_ref, core, step))
    pl.when(step >= steps // 2)(lambda: work(other_ref, 1 - core, step - steps // 2))

    @pl.when(step == steps - 1)
    def _():
        middle = middle_ref[...]
        row_scale = lax.rsqrt(jnp.mean(middle * middle, axis=-1, keepdims=True) + EPSILON)
        normed_ref[...] = (middle * row_scale * gain_ref[...]).astype(bf16)


def out_norm(ids, attended, w_mine, w_other, hidden, gain):
    groups, share, q_cols = attended.shape
    width = hidden.shape[1]
    whole = lambda j, s: (0, 0)
    steps = 2
    return pl.pallas_call(
        out_norm_kernel,
        grid_spec=pltpu.PrefetchScalarGridSpec(
            num_scalar_prefetch=1,
            grid=(steps,),
            in_specs=[
                pl.BlockSpec((groups, share, q_cols), lambda j, s: (0, 0, 0)),
                pl.BlockSpec(
                    (groups * q_cols, width // steps), lambda j, s: (0, jnp.minimum(j, steps // 2 - 1))
                ),
                pl.BlockSpec(
                    (groups * q_cols, width // steps), lambda j, s: (0, jnp.maximum(j - steps // 2, 0))
                ),
                pl.BlockSpec((share, width), lambda j, s: (s[RING], 0)),
                pl.BlockSpec((1, width), whole),
            ],
            out_specs=[pl.BlockSpec((share, width), whole), pl.BlockSpec((share, width), whole)],
        ),
        out_shape=[
            jax.ShapeDtypeStruct((share, width), f32),
            jax.ShapeDtypeStruct((share, width), bf16),
        ],
        cost_estimate=cost(2 * groups * share * q_cols * width, 2 * groups * q_cols * width),
        name="out_project_and_norm",
    )(ids, attended, w_mine, w_other, hidden, gain)


def norm_back_kernel(
    ids_ref,
    own_ref,
    up_ref,
    down_ref,
    middle_ref,
    gain_ref,
    cotangent_ref,
    mine_ref,
    other_ref,
    dh_ref,
    da_ref,
    gain_grad_ref,
    do_ref,
):
    step = pl.program_id(0)

    @pl.when(step == 0)
    def _():
        incoming = own_ref[...].astype(f32) + up_ref[...].astype(f32) + down_ref[...].astype(f32)
        middle = middle_ref[...]
        row_scale = lax.rsqrt(jnp.mean(middle * middle, axis=-1, keepdims=True) + EPSILON)
        normed = middle * row_scale
        gain_grad_ref[...] = jnp.sum(incoming * normed, axis=0, keepdims=True)
        scaled = incoming * gain_ref[...]
        branch = row_scale * (scaled - normed * jnp.mean(scaled * normed, axis=-1, keepdims=True))
        share = middle.shape[0]
        position = ids_ref[RING] * share + lax.broadcasted_iota(jnp.int32, (share, 1), 0)
        direct = jnp.where(position < ids_ref[LENGTH], cotangent_ref[...].astype(f32), 0.0)
        dh = direct + branch
        dh_ref[...] = dh
        da_ref[...] = (RESID * dh).astype(bf16)

    rows, cols = mine_ref.shape
    q_cols = do_ref.shape[2]
    core = ids_ref[CORE]
    mine = da_ref[:, pl.ds(pl.multiple_of(core * cols, cols), cols)]
    other = da_ref[:, pl.ds(pl.multiple_of((1 - core) * cols, cols), cols)]
    per_step = rows // q_cols
    for index in range(per_step):
        here = slice(index * q_cols, (index + 1) * q_cols)
        grad = mm(mine, mine_ref[here, :], NT) + mm(other, other_ref[here, :], NT)
        do_ref[ids_ref[RING + step * per_step + index]] = grad.astype(bf16)


def norm_back(ids, parts, middle, gain, cotangent, w_mine, w_other, q_cols):
    share, width = middle.shape
    groups = w_mine.shape[0] // q_cols
    whole = lambda t, s: (0, 0)
    weight = pl.BlockSpec((groups * q_cols // 2, width // 2), lambda t, s: (t, 0))
    return pl.pallas_call(
        norm_back_kernel,
        grid_spec=pltpu.PrefetchScalarGridSpec(
            num_scalar_prefetch=1,
            grid=(2,),
            in_specs=[pl.BlockSpec((share, width), whole)] * 4
            + [
                pl.BlockSpec((1, width), whole),
                pl.BlockSpec((share, width), lambda t, s: (s[RING], 0)),
                weight,
                weight,
            ],
            out_specs=[
                pl.BlockSpec((share, width), whole),
                pl.BlockSpec((share, width), whole),
                pl.BlockSpec((1, width), whole),
                pl.BlockSpec((groups, share, q_cols), lambda t, s: (0, 0, 0)),
            ],
        ),
        out_shape=[
            jax.ShapeDtypeStruct((share, width), f32),
            jax.ShapeDtypeStruct((share, width), bf16),
            jax.ShapeDtypeStruct((1, width), f32),
            jax.ShapeDtypeStruct((groups, share, q_cols), bf16),
        ],
        cost_estimate=cost(2 * groups * share * q_cols * width, 2 * groups * q_cols * width),
        name="norm_back_and_project",
    )(ids, *parts, middle, gain, cotangent, w_mine, w_other)


def in_grad_kernel(ids_ref, own_ref, up_ref, down_ref, rows_ref, gain_ref, dh_ref, out_ref):
    incoming = own_ref[...].astype(f32) + up_ref[...].astype(f32) + down_ref[...].astype(f32)
    rows = rows_ref[...].astype(f32)
    row_scale = lax.rsqrt(jnp.mean(rows * rows, axis=-1, keepdims=True) + EPSILON)
    normed = rows * row_scale
    scaled = incoming * gain_ref[...]
    branch = row_scale * (scaled - normed * jnp.mean(scaled * normed, axis=-1, keepdims=True))
    out_ref[...] = dh_ref[...] + branch


def in_grad(ids, terms, got, hidden, gain, dh):
    share, width = dh.shape
    steps = 4
    rows = share // steps
    row = lambda j, s: (j, 0)
    own = lambda j, s: (steps * s[RING] + j, 0)
    return pl.pallas_call(
        in_grad_kernel,
        grid_spec=pltpu.PrefetchScalarGridSpec(
            num_scalar_prefetch=1,
            grid=(steps,),
            in_specs=[
                pl.BlockSpec((rows, width), own),
                pl.BlockSpec((rows, width), row),
                pl.BlockSpec((rows, width), row),
                pl.BlockSpec((rows, width), own),
                pl.BlockSpec((1, width), lambda j, s: (0, 0)),
                pl.BlockSpec((rows, width), row),
            ],
            out_specs=pl.BlockSpec((rows, width), row),
        ),
        out_shape=jax.ShapeDtypeStruct((share, width), f32),
        cost_estimate=cost(20 * share * width, 16 * share * width),
        name="input_grad",
    )(ids, terms, *got, hidden, gain, dh)


def core_halves(chips):
    piece = lambda i, s: jnp.where(i < chips, 2 * i + 1 - s[CORE], 2 * (i - chips) + s[CORE])
    sent = lambda i: jnp.minimum(i, chips - 1)
    kept = lambda i: jnp.maximum(i - chips, 0)
    return piece, sent, kept


def out_wgrad_kernel(ids_ref, o_ref, da_ref, send_ref, keep_ref):
    step = pl.program_id(0)
    groups, _, q_cols = o_ref.shape

    def store(ref):
        for group in range(groups):
            part = mm(o_ref[group], da_ref[...], TN)
            ref[0, group * q_cols : (group + 1) * q_cols, :] = part.astype(bf16)

    half = pl.num_programs(0) // 2
    pl.when(step < half)(lambda: store(send_ref))
    pl.when(step >= half)(lambda: store(keep_ref))


def out_wgrad_parts(ids, attended, branch_grad, replicas):
    groups, share, q_cols = attended.shape
    width = branch_grad.shape[1]
    cols = width // replicas
    chips = replicas // 2
    piece, sent, kept = core_halves(chips)
    out = jax.ShapeDtypeStruct((chips, groups * q_cols, cols), bf16)
    block = (1, groups * q_cols, cols)
    return pl.pallas_call(
        out_wgrad_kernel,
        grid_spec=pltpu.PrefetchScalarGridSpec(
            num_scalar_prefetch=1,
            grid=(replicas,),
            in_specs=[
                pl.BlockSpec((groups, share, q_cols), lambda i, s: (0, 0, 0)),
                pl.BlockSpec((share, cols), lambda i, s: (0, piece(i, s))),
            ],
            out_specs=[
                pl.BlockSpec(block, lambda i, s: (sent(i), 0, 0)),
                pl.BlockSpec(block, lambda i, s: (kept(i), 0, 0)),
            ],
        ),
        out_shape=[out, out],
        cost_estimate=cost(2 * groups * share * q_cols * width, 2 * groups * q_cols * width),
        name="out_weight_grad",
    )(ids, attended, branch_grad)


def qkv_wgrad_kernel(
    ids_ref,
    normed_ref,
    grad_ref,
    w_ref,
    gain_ref,
    other_gain_ref,
    q_send_ref,
    q_keep_ref,
    s_send_ref,
    s_keep_ref,
):
    step = pl.program_id(0)
    cols = normed_ref.shape[1]
    q_cols = q_send_ref.shape[2]

    def store(q_ref, s_ref):
        grad = mm(normed_ref[...], grad_ref[...], TN)
        q_ref[0] = grad[:, :q_cols].astype(bf16)
        s_ref[0, :, : 2 * HD] = grad[:, q_cols:]
        gain = jnp.sum(grad * w_ref[...].astype(f32), axis=1, keepdims=True)
        lane = lax.broadcasted_iota(jnp.int32, (cols, 128), 1)
        first = jnp.where(lane == 0, gain / gain_ref[...], 0.0)
        s_ref[0, :, 2 * HD :] = jnp.where(lane == 1, other_gain_ref[...], first)

    half = pl.num_programs(0) // 2
    pl.when(step < half)(lambda: store(q_send_ref, s_send_ref))
    pl.when(step >= half)(lambda: store(q_keep_ref, s_keep_ref))


def qkv_wgrad_parts(ids, normed, grads, w_qkv, gain, other_gain, replicas):
    count, width = normed.shape
    all_cols = grads.shape[1]
    q_cols = all_cols - 2 * HD
    chips = replicas // 2
    cols = width // replicas
    piece, sent, kept = core_halves(chips)
    down = lambda n: pl.BlockSpec((cols, n), lambda i, s: (piece(i, s), 0))
    out = lambda n, where: pl.BlockSpec((1, cols, n), lambda i, s: (where(i), 0, 0))
    shape = lambda n, kind: jax.ShapeDtypeStruct((chips, cols, n), kind)
    return pl.pallas_call(
        qkv_wgrad_kernel,
        grid_spec=pltpu.PrefetchScalarGridSpec(
            num_scalar_prefetch=1,
            grid=(replicas,),
            in_specs=[
                pl.BlockSpec((count, cols), lambda i, s: (0, piece(i, s))),
                pl.BlockSpec((count, all_cols), lambda i, s: (0, 0)),
                down(all_cols),
                down(1),
                down(1),
            ],
            out_specs=[out(q_cols, sent), out(q_cols, kept), out(256, sent), out(256, kept)],
        ),
        out_shape=[shape(q_cols, bf16)] * 2 + [shape(256, f32)] * 2,
        cost_estimate=cost(2 * count * width * all_cols, 3 * count * width),
        name="projection_weight_grads",
    )(ids, normed, grads, w_qkv, gain, other_gain)


def layer_out_kernel(middle_ref, own_ref, up_ref, down_ref, out_ref):
    total = own_ref[...].astype(f32) + up_ref[...].astype(f32) + down_ref[...].astype(f32)
    out_ref[...] = (middle_ref[...] + RESID * total).astype(bf16)


def layer_output(middle, own, own_row, got):
    share, width = middle.shape
    spec = lambda row: pl.BlockSpec((share, WIDE), lambda j: (row, j))
    return pl.pallas_call(
        layer_out_kernel,
        grid=(width // WIDE,),
        in_specs=[spec(0), spec(own_row), spec(0), spec(0)],
        out_specs=spec(0),
        out_shape=jax.ShapeDtypeStruct((share, width), bf16),
        cost_estimate=cost(5 * share * width, 12 * share * width),
        name="layer_output",
    )(middle, own, *got)


def ring_add_kernel(first, ids_ref, term_ref, got_ref, out_ref):
    rows = got_ref.shape[0]
    if rows < out_ref.shape[0]:
        out_ref[...] = term_ref[...]
    here = slice(first, first + rows)
    out_ref[here, :] = (term_ref[here, :].astype(f32) + got_ref[...].astype(f32)).astype(bf16)


def ring_add(ids, terms, block, place, got, first, share):
    width = terms.shape[1]
    cols = width // 2
    which = lambda j, s: (s[RING + place] if block is None else block, j)
    column = lambda j, s: (0, j)
    return pl.pallas_call(
        functools.partial(ring_add_kernel, first),
        grid_spec=pltpu.PrefetchScalarGridSpec(
            num_scalar_prefetch=1,
            grid=(2,),
            in_specs=[
                pl.BlockSpec((share, cols), which),
                pl.BlockSpec((got.shape[0], cols), column),
            ],
            out_specs=pl.BlockSpec((share, cols), column),
        ),
        out_shape=jax.ShapeDtypeStruct((share, width), bf16),
        cost_estimate=cost(2 * share * width, 6 * share * width),
        name="ring_add",
    )(ids, terms, got)


def swiglu_kernel(pieces, members, row, ids_ref, *refs):
    piece_refs = refs[:pieces]
    cot_ref, gate_ref, up_ref, down_ref = refs[pieces : pieces + 4]
    outs = refs[-19:-13]
    x, dm, wg, wu, wd, act, dgate, dup, in_sem, gate_sem, up_sem, down_sem, out_sem = refs[-13:]
    kept, dn_ref = outs[:5], outs[5]
    rows = x.shape[0]
    share = rows // len(members)
    width, units = wg.shape
    blocks = gate_sem.shape[0]
    block = units // blocks
    part = width // blocks
    arrivals = []
    at = 0
    for ref in piece_refs:
        count = ref.shape[0]
        arrivals.append((ref, x.at[at : at + count, :]))
        at += count
    for index, place in enumerate(members):
        first = pl.multiple_of(ids_ref[RING + place] * share, share)
        here = slice(index * share, (index + 1) * share)
        arrivals.append((cot_ref.at[pl.ds(first, share), :], dm.at[here, :]))
    arrivals = [pltpu.make_async_copy(*pair, in_sem.at[i]) for i, pair in enumerate(arrivals)]

    def weights(u):
        here = pl.ds(pl.multiple_of(u * block, block), block)
        return (
            pltpu.make_async_copy(gate_ref.at[:, here], wg.at[:, here], gate_sem.at[u]),
            pltpu.make_async_copy(up_ref.at[:, here], wu.at[:, here], up_sem.at[u]),
            pltpu.make_async_copy(down_ref.at[here, :], wd.at[here, :], down_sem.at[u]),
        )

    for copy in arrivals[:pieces]:
        copy.start()
    for copy in weights(0):
        copy.start()
    for copy in arrivals[pieces:]:
        copy.start()
    for u in range(1, blocks):
        for copy in weights(u):
            copy.start()
    for copy in arrivals:
        copy.wait()
    for index, place in enumerate(members):
        here = slice(index * share, (index + 1) * share)
        position = ids_ref[RING + place] * share + lax.broadcasted_iota(jnp.int32, (share, 1), 0)
        scaled = dm[here, :].astype(f32) * RESID
        dm[here, :] = jnp.where(position < ids_ref[LENGTH], scaled, 0.0).astype(bf16)

    def one_block(u, carry):
        for copy in weights(u):
            copy.wait()
        here = pl.ds(pl.multiple_of(u * block, block), block)
        gate = mm(x[...], wg[:, here], NN)
        up = mm(x[...], wu[:, here], NN)
        grad = mm(dm[...], wd[here, :], NT)
        sg = jax.nn.sigmoid(gate)
        silu = gate * sg
        act[:, here] = (silu * up).astype(bf16)
        dgate[:, here] = (grad * up * sg * (1.0 + gate * (1.0 - sg))).astype(bf16)
        dup[:, here] = (grad * silu).astype(bf16)
        return carry

    lax.fori_loop(0, blocks, one_block, 0)

    def one_part(n, carry):
        here = pl.ds(pl.multiple_of(n * part, part), part)
        grad = mm(dgate[...], wg[here, :], NT) + mm(dup[...], wu[here, :], NT)
        dn_ref[:, here] = grad.astype(bf16)
        return carry

    one_part(0, 0)
    leaving = [
        pltpu.make_async_copy(src, dst.at[pl.ds(row, rows), :], out_sem.at[i])
        for i, (src, dst) in enumerate(zip((x, dm, act, dgate, dup), kept))
    ]
    for copy in leaving:
        copy.start()
    lax.fori_loop(1, blocks, one_part, 0)
    for copy in leaving:
        copy.wait()


def swiglu(ids, pieces, members, cotangent, weights, row, buffers, total_rows):
    w_gate, w_up, w_down = weights
    width, units = w_gate.shape
    rows = sum(piece.shape[0] for piece in pieces)
    blocks = 2
    hbm = pl.BlockSpec(memory_space=pl.ANY)
    operands = [*pieces, cotangent, *weights, *buffers]
    aliases = {5 + len(pieces) + index: index for index in range(len(buffers))}
    collected = lambda n: jax.ShapeDtypeStruct((total_rows, n), bf16)
    held = lambda *shape: pltpu.VMEM(shape, bf16)
    copies = lambda n: pltpu.SemaphoreType.DMA((n,))
    return pl.pallas_call(
        functools.partial(swiglu_kernel, len(pieces), tuple(members), row),
        grid_spec=pltpu.PrefetchScalarGridSpec(
            num_scalar_prefetch=1,
            grid=(1,),
            in_specs=[hbm] * len(operands),
            out_specs=[hbm] * 5 + [pl.BlockSpec((rows, width), lambda i, s: (0, 0))],
            scratch_shapes=[held(rows, width)] * 2
            + [held(width, units), held(width, units), held(units, width)]
            + [held(rows, units)] * 3
            + [copies(len(pieces) + len(members)), *([copies(blocks)] * 3), copies(5)],
        ),
        out_shape=[collected(width)] * 2
        + [collected(units)] * 3
        + [jax.ShapeDtypeStruct((rows, width), bf16)],
        input_output_aliases=aliases,
        compiler_params=grant(58),
        cost_estimate=cost(12 * rows * width * units, 6 * width * units + 16 * rows * width),
        name="swiglu_rows",
    )(ids, *operands)


def ring_order(count):
    inner = 2 if count <= 8 else 4
    outer = count // inner
    cells = [(0, 0)]
    for row in range(outer):
        cells += [(row, c) for c in (range(1, inner) if row % 2 == 0 else range(inner - 1, 0, -1))]
    cells += [(row, 0) for row in range(outer - 1, 0, -1)]
    return [row * inner + c for row, c in cells]


def tie(*values):
    return lax.optimization_barrier(values)


def over_cores(send, keep):
    chips = send.shape[0]
    chip = lax.axis_index("dp") // 2
    take = lambda a, i: lax.dynamic_index_in_dim(a, i, 0, keepdims=False)
    got = lax.ppermute(send, "dp", [(i, i ^ 1) for i in range(2 * chips)])
    stay = [take(keep, chip), take(got, chip)]
    go = []
    for step in range(1, chips):
        there = (chip + step) % chips
        term = take(keep, there).astype(f32) + take(got, there).astype(f32)
        go.append(term.astype(send.dtype))
    return stay, go


def over_chips(stay, go):
    chips = len(go) + 1
    terms = list(stay)
    for step in range(1, chips):
        to = [(i, ((i // 2 + step) % chips) * 2 + i % 2) for i in range(2 * chips)]
        terms.append(lax.ppermute(go[step - 1], "dp", to))
    return terms


def total_of(terms):
    total = terms[0].astype(f32)
    for term in terms[1:]:
        total = total + term.astype(f32)
    return total


def local(
    hidden_in,
    seq_lengths,
    out_grad,
    attn_gain,
    mlp_gain,
    w_query,
    w_key,
    w_value,
    w_out,
    w_gate,
    w_up,
    w_down,
):
    rows_total, width = hidden_in.shape
    q_cols = w_query.shape[1]
    heads_here = q_cols // HD
    groups = lax.axis_size("tensor")
    replicas = lax.axis_size("dp")
    member = lax.axis_index("tensor")
    replica = lax.axis_index("dp")
    core = replica % 2
    share = rows_total // groups
    half = share // 2
    order = ring_order(groups)
    spot = [order.index(i) for i in range(groups)]
    ahead = [(order[i], order[(i + 1) % groups]) for i in range(groups)]
    behind = [(b, a) for a, b in ahead]
    half_way = groups // 2
    apart = [0]
    for d in range(1, half_way):
        apart += [-d, d]
    apart.append(half_way)
    ring = [[order[(spot[i] + d) % groups] for d in apart] for i in range(groups)]
    ids = jnp.concatenate(
        [seq_lengths, core[None].astype(jnp.int32), jnp.asarray(ring, jnp.int32)[member]]
    )
    table = rope_tables(rows_total)
    gain_one = attn_gain[None, :]
    gain_two = mlp_gain[None, :]

    def exchange(array):
        return lax.all_to_all(array, "tensor", 0, 0, tiled=True)

    def onward(array):
        return lax.ppermute(array, "tensor", ahead)

    def back(array):
        return lax.ppermute(array, "tensor", behind)

    w_own = lax.dynamic_slice_in_dim(w_out, core * (width // 2), width // 2, 1)
    w_hop = onward(w_own), back(w_own)
    w_mine = [w_own]

    def w_next():
        w_mine.extend(w_hop)
        if len(w_mine) < groups - 1:
            return onward(w_hop[0]), back(w_hop[1])
        return onward(w_hop[0][: q_cols // 2]), back(w_hop[1][q_cols // 2 :])

    kv_of = [i * heads_here // (H // KVH) for i in range(groups)]
    w_kv = pick_heads(w_key, w_value, kv_of)
    w_kv = exchange(w_kv).reshape(width, 2 * HD)
    normed_one, queries = front(hidden_in, gain_one, w_query, table)
    *w_hop, w_kv, normed_one, queries = tie(*w_hop, w_kv, normed_one, queries)
    for _ in range(half_way - 3):
        w_hop = w_next()
    keys, keys_t, values, values_t = keys_values(seq_lengths, normed_one, w_kv, table)
    *w_hop, keys = tie(*w_hop, keys)
    w_hop = w_next()
    attended, lse = attend(queries, keys, values_t)
    *w_hop, attended = tie(*w_hop, attended)
    attended_rows = exchange(attended.reshape(groups, share, q_cols))
    w_hop = w_next()
    w_mine = jnp.concatenate([*w_mine, *w_hop], 0)
    w_other = lax.ppermute(w_mine, "dp", [(i, i ^ 1) for i in range(replicas)])
    w_qkv = jnp.concatenate([w_query, w_kv], 1)
    middle, normed_two = out_norm(ids, attended_rows, w_mine, w_other, hidden_in, gain_two)

    weights = (w_gate, w_up, w_down)
    grads = []
    buffers = []

    def run(pieces, members, row):
        nonlocal buffers
        *buffers, grad = swiglu(
            ids, pieces, members, out_grad, weights, row, buffers, rows_total
        )
        grads.append(grad)

    pieces, members, row = [normed_two], [0], rows_total - 2 * share
    hop = [normed_two, normed_two]
    for d in range(1, half_way + 1):
        if d < half_way:
            hop = [onward(hop[0]), back(hop[1])]
        else:
            hop = [onward(hop[0][:half]), back(hop[1][half:])]
        run(pieces, members, row)
        hop, grads[-1], buffers = tie(hop, grads[-1], buffers)
        pieces = hop
        if d < half_way:
            members, row = [2 * d - 1, 2 * d], 2 * share * (d - 1)
        else:
            members, row = [groups - 1], rows_total - share
    run(pieces, members, row)
    normed_ring, down_ring, act, dgate, dup = buffers

    def first_hop(far):
        return onward(far[:half]), back(far[half:])

    def next_hop(terms, block, got):
        down = ring_add(ids, terms, block, None, got[1], share - got[1].shape[0], share)
        up = ring_add(ids, terms, block + 1, None, got[0], 0, share)
        return onward(up), back(down)

    def natural_hop(terms, distance, got):
        first = share - got[1].shape[0]
        down = ring_add(ids, terms, None, 2 * distance - 1, got[1], first, share)
        up = ring_add(ids, terms, None, 2 * distance, got[0], 0, share)
        return onward(up), back(down)

    got = first_hop(grads[-1])
    mlp = mm(act, w_down, NN).astype(bf16)
    *got, mlp = tie(*got, mlp)
    fillers = [
        lambda: mm(act, down_ring, TN).astype(bf16),
        lambda: mm(normed_ring, dgate, TN).astype(bf16),
        lambda: mm(normed_ring, dup, TN).astype(bf16),
    ]
    filled = []
    for d in range(half_way - 1, 0, -1):
        got = next_hop(grads[d], 0, got)
        if len(filled) < 3:
            *got, value = tie(*got, fillers[len(filled)]())
            filled.append(value)
    down_wgrad, gate_wgrad, up_wgrad = filled
    scatter = lambda a, d: lax.psum_scatter(a, "dp", scatter_dimension=d, tiled=True)
    down_wgrad = scatter(down_wgrad, 1)
    gate_wgrad = scatter(gate_wgrad, 0)
    up_wgrad = scatter(up_wgrad, 0)

    *got, mlp = tie(*got, mlp)
    out_got = first_hop(mlp[rows_total - share :])
    dh, da, gain_part, do_send = norm_back(
        ids, [grads[0], *got], middle, gain_two, out_grad, w_mine, w_other, q_cols
    )
    *out_got, do_send, da = tie(*out_got, do_send, da)
    do = exchange(do_send).reshape(rows_total, q_cols)
    out_parts = out_wgrad_parts(ids, attended_rows, da, replicas)
    do, out_parts = tie(do, out_parts)
    out_got = next_hop(mlp, 2 * half_way - 4, out_got)
    out_parts = over_cores(*out_parts)
    operands = [queries, do, attended, lse, keys, keys_t, values, table]
    carried = attend_back(0, *operands, [])
    out_got, carried, down_wgrad, out_parts = tie(out_got, carried, down_wgrad, out_parts)
    out_terms = over_chips(*out_parts)
    for d in range(half_way - 2, 1, -1):
        out_got = next_hop(mlp, 2 * d - 2, out_got)
    qkv_grad = attend_back(1, *operands, carried)
    out_got, qkv_grad = tie(out_got, qkv_grad)

    first_grad = mm(qkv_grad, w_qkv, NT).astype(bf16)
    far = lax.dynamic_slice_in_dim(first_grad, ids[RING + groups - 1] * share, share, 0)
    in_got = first_hop(far)
    out_got = next_hop(mlp, 0, out_got)
    q_send, q_keep, s_send, s_keep = qkv_wgrad_parts(
        ids,
        normed_one,
        qkv_grad,
        w_qkv,
        attn_gain[:, None],
        gain_part.reshape(width, 1),
        replicas,
    )
    in_got, out_got, q_send, s_send, gate_wgrad, out_terms = tie(
        in_got, out_got, q_send, s_send, gate_wgrad, out_terms
    )
    out_wgrad = total_of(out_terms).astype(bf16)
    out_wgrad = lax.psum_scatter(out_wgrad, "tensor", scatter_dimension=0, tiled=True)
    small = over_cores(s_send, s_keep)
    query_wgrad = over_cores(q_send, q_keep)
    for d in range(half_way - 1, 0, -1):
        in_got = natural_hop(first_grad, d, in_got)
        if d == half_way - 1:
            small = over_chips(*small)
            query_wgrad = over_chips(*query_wgrad)
            in_got, small, query_wgrad = tie(in_got, small, query_wgrad)
            small, query_wgrad = total_of(small), total_of(query_wgrad)
            layer_out = layer_output(middle, mlp, groups - 2, out_got)
        elif d == half_way - 2:
            in_got, layer_out, up_wgrad = tie(in_got, layer_out, up_wgrad)
    pieces = exchange(small.reshape(groups, small.shape[0] // groups, 256))
    input_grad = in_grad(ids, first_grad, in_got, hidden_in, gain_one, dh)
    gains = jnp.sum(pieces[:, :, 128:130], axis=0)
    kv = pieces[:, :, :128].reshape(KVH, groups // KVH, -1, 128).sum(axis=1)
    kv = jnp.swapaxes(kv, 0, 1)
    key_wgrad = kv[:, :, :HD].reshape(-1, KVH * HD)
    value_wgrad = kv[:, :, HD:].reshape(-1, KVH * HD)
    return (
        layer_out,
        input_grad,
        gains[:, 0],
        gains[:, 1],
        query_wgrad,
        key_wgrad,
        value_wgrad,
        out_wgrad.astype(f32),
        gate_wgrad.astype(f32),
        up_wgrad.astype(f32),
        down_wgrad.astype(f32),
    )


def solution(mesh):
    placed = (
        P("dp", None),
        P("dp"),
        P("dp", None),
        P(),
        P(),
        P(None, "tensor"),
        P("tensor", None),
        P("tensor", None),
        P("tensor", None),
        P(None, "tensor"),
        P(None, "tensor"),
        P("tensor", None),
    )
    return jax.shard_map(
        local,
        mesh=mesh,
        in_specs=placed,
        out_specs=(
            P(("dp", "tensor"), None),
            P(("dp", "tensor"), None),
            P(("dp", "tensor")),
            P(("dp", "tensor")),
            P("dp", "tensor"),
            P(("dp", "tensor"), None),
            P(("dp", "tensor"), None),
            P("tensor", "dp"),
            P("dp", "tensor"),
            P("dp", "tensor"),
            P("tensor", "dp"),
        ),
        check_vma=False,
    )
```

```python
import functools
import math

import jax
import jax.numpy as jnp
from jax import lax
from jax.experimental import pallas as pl
from jax.experimental.pallas import tpu as pltpu
from jax.sharding import PartitionSpec as P

H = 32
KVH = 8
HD = 64
SEQ_LEN = 2048
QB = 256
WIDE = 512

RESID = 0.22
ATTN_SCALE = 0.015625
EPSILON = 1e-05
THETA_LOG = math.log(10000000.0)
MASKED = -1e30

f32 = jnp.float32
bf16 = jnp.bfloat16
NN = (((1,), (0,)), ((), ()))
NT = (((1,), (1,)), ((), ()))
TN = (((0,), (0,)), ((), ()))


def mm(left, right, dims):
    return lax.dot_general(left, right, dims, preferred_element_type=f32)


def grant(mib):
    return pltpu.CompilerParams(vmem_limit_bytes=mib * 1024 * 1024)


def cost(flops, nbytes):
    return pl.CostEstimate(flops=int(flops), bytes_accessed=int(nbytes), transcendentals=0)


def rope_tables(count):
    lane = jnp.arange(128, dtype=jnp.int32) % (HD // 2)
    freqs = jnp.exp(-THETA_LOG * (2 * lane).astype(f32) / HD)[None, :]
    fine = jnp.arange(QB, dtype=jnp.int32)
    coarse = jnp.arange(count // QB * 8, dtype=jnp.int32) // 8 * QB
    angle_rows = jnp.concatenate([fine, coarse]).astype(f32)[:, None] * freqs
    return jnp.concatenate([jnp.cos(angle_rows), jnp.sin(angle_rows)], 1)


def turn_at(table_ref, block):
    fine = table_ref[:QB, :]
    coarse = table_ref[pl.ds(pl.multiple_of(QB + block * 8, 8), 8), :][:1, :]
    cos_f, sin_f, cos_c, sin_c = fine[:, :128], fine[:, 128:], coarse[:, :128], coarse[:, 128:]
    return cos_f * cos_c - sin_f * sin_c, sin_f * cos_c + cos_f * sin_c


def widen(table, count):
    return table if count == 128 else jnp.concatenate([table] * (count // 128), 1)


def swap_halves(rows):
    count = rows.shape[1]
    lane = lax.broadcasted_iota(jnp.int32, rows.shape, 1)
    ahead = pltpu.roll(rows, count - HD // 2, 1)
    behind = pltpu.roll(rows, HD // 2, 1)
    return jnp.where(lane % HD < HD // 2, ahead, behind)


def half_sign(shape):
    lane = lax.broadcasted_iota(jnp.int32, shape, 1)
    return jnp.where(lane % HD < HD // 2, -1.0, 1.0)


def rotate(rows, cosines, sines):
    count = rows.shape[1]
    turned = swap_halves(rows) * half_sign(rows.shape)
    return rows * widen(cosines, count) + turned * widen(sines, count)


def unrotate(rows, cosines, sines):
    count = rows.shape[1]
    turned = swap_halves(rows * widen(sines, count)) * half_sign(rows.shape)
    return rows * widen(cosines, count) - turned


def front_kernel(start, rows_ref, gain_ref, wq_ref, table_ref, *refs):
    normed_ref, q_ref = refs[-2:]
    rows = rows_ref[...].astype(f32)
    row_scale = lax.rsqrt(jnp.mean(rows * rows, axis=-1, keepdims=True) + EPSILON)
    normed_ref[...] = (rows * row_scale * gain_ref[...]).astype(bf16)
    q_raw = mm(normed_ref[...], wq_ref[...], NN)
    turned = rotate(q_raw, *turn_at(table_ref, start + pl.program_id(0)))
    q_ref[...] = (turned.astype(bf16).astype(f32) * ATTN_SCALE).astype(bf16)


def front(first, hidden, gain, w_query, table, carried):
    count, width = hidden.shape
    q_cols = w_query.shape[1]
    steps = count // QB // 2
    start = steps if first else 0
    row = lambda i: (start + i, 0)
    whole = lambda i: (0, 0)
    return pl.pallas_call(
        functools.partial(front_kernel, start),
        grid=(steps,),
        in_specs=[
            pl.BlockSpec((QB, width), row),
            pl.BlockSpec((1, width), whole),
            pl.BlockSpec((width, q_cols), whole),
            pl.BlockSpec(table.shape, whole),
        ]
        + [pl.BlockSpec(memory_space=pl.ANY)] * len(carried),
        out_specs=[pl.BlockSpec((QB, width), row), pl.BlockSpec((QB, q_cols), row)],
        out_shape=[
            jax.ShapeDtypeStruct((count, width), bf16),
            jax.ShapeDtypeStruct((count, q_cols), bf16),
        ],
        input_output_aliases={4 + index: index for index in range(len(carried))},
        cost_estimate=cost(count * width * q_cols, 3 * count * width),
        name="norm_and_query",
    )(hidden, gain, w_query, table, *carried)


def keys_kernel(length_ref, normed_ref, wkv_ref, table_ref, k_ref, kt_ref, v_ref, vt_ref):
    kv_raw = mm(normed_ref[...], wkv_ref[...], NN)
    lane = lax.broadcasted_iota(jnp.int32, kv_raw.shape, 1)
    position = pl.program_id(0) * WIDE + lax.broadcasted_iota(jnp.int32, kv_raw.shape, 0)
    blocks = [turn_at(table_ref, pl.program_id(0) * (WIDE // QB) + i) for i in range(WIDE // QB)]
    cosines, sines = (jnp.concatenate([b[i] for b in blocks], 0) for i in range(2))
    turned = rotate(kv_raw, cosines, sines)
    keys = jnp.where(lane < HD, turned, 0.0)
    blocked = jnp.where((lane == HD) & (position >= length_ref[0]), MASKED, 0.0)
    k_ref[...] = (keys + blocked).astype(bf16)
    kt_ref[...] = keys.T.astype(bf16)
    values = jnp.concatenate([kv_raw[:, HD:], kv_raw[:, :HD]], 1)
    values = jnp.where(lane < HD, values, 1.0)
    v_ref[...] = values.astype(bf16)
    vt_ref[...] = values.T.astype(bf16)


def keys_values(length, normed, w_kv, table):
    count, width = normed.shape
    row = lambda i, s: (i, 0)
    col = lambda i, s: (0, i)
    return pl.pallas_call(
        keys_kernel,
        grid_spec=pltpu.PrefetchScalarGridSpec(
            num_scalar_prefetch=1,
            grid=(count // WIDE,),
            in_specs=[
                pl.BlockSpec((WIDE, width), row),
                pl.BlockSpec((width, 128), lambda i, s: (0, 0)),
                pl.BlockSpec(table.shape, lambda i, s: (0, 0)),
            ],
            out_specs=[
                pl.BlockSpec((WIDE, 128), row),
                pl.BlockSpec((128, WIDE), col),
                pl.BlockSpec((WIDE, 128), row),
                pl.BlockSpec((128, WIDE), col),
            ],
        ),
        out_shape=[
            jax.ShapeDtypeStruct((count, 128), bf16),
            jax.ShapeDtypeStruct((128, count), bf16),
            jax.ShapeDtypeStruct((count, 128), bf16),
            jax.ShapeDtypeStruct((128, count), bf16),
        ],
        cost_estimate=cost(2 * count * width * 128, 2 * count * width),
        name="keys_and_values",
    )(length, normed, w_kv, table)


def pick_kernel(picks, k_ref, v_ref, out_ref):
    for index, head in enumerate(picks):
        both = [ref[:, 128 * (head // 2) : 128 * (head // 2) + 128] for ref in (k_ref, v_ref)]
        at = head % 2 * HD
        out_ref[index] = jnp.concatenate([b[:, at : at + HD] for b in both], 1)


def pick_heads(w_key, w_value, picks):
    return pl.pallas_call(
        functools.partial(pick_kernel, picks),
        out_shape=jax.ShapeDtypeStruct((len(picks), w_key.shape[0], 2 * HD), bf16),
        name="pick_heads",
    )(w_key, w_value)


def head_slab(rows, head, fill):
    pair = rows[:, 128 * (head // 2) : 128 * (head // 2) + 128]
    if head % 2:
        pair = jnp.concatenate([pair[:, HD:], pair[:, :HD]], 1)
    lane = lax.broadcasted_iota(jnp.int32, pair.shape, 1)
    other = jnp.where(lane == HD, jnp.full(pair.shape, fill, f32), 0.0).astype(pair.dtype)
    return jnp.where(lane < HD, pair, other)


def causal(keys_count, rows_count):
    key = lax.broadcasted_iota(jnp.int32, (keys_count, rows_count), 0)
    return key <= lax.broadcasted_iota(jnp.int32, (keys_count, rows_count), 1)


def attend_kernel(heads, start, q_ref, k_ref, vt_ref, *refs):
    o_ref, lse_ref, slab_ref, high_ref, total_ref = refs[-5:]
    block = start + pl.program_id(0)
    rows = q_ref[...]
    for head in range(heads):
        slab_ref[head] = head_slab(rows, head, 1.0)
    high_ref[...] = jnp.full(high_ref.shape, MASKED, f32)
    total_ref[...] = jnp.zeros(total_ref.shape, f32)

    def step(start, width, diagonal):
        keys = k_ref[pl.ds(start, width), :]
        values = vt_ref[:, pl.ds(start, width)]
        scores = [mm(keys, slab_ref[head], NT) for head in range(heads)]
        for head in range(heads):
            score = scores[head]
            if diagonal:
                score = jnp.where(causal(width, QB), score, MASKED)
            old = high_ref[head : head + 1, :]
            new = jnp.maximum(old, jnp.max(score, axis=0, keepdims=True))
            probs = jnp.exp(score - new).astype(bf16)
            high_ref[head : head + 1, :] = new
            total_ref[head] = total_ref[head] * jnp.exp(old - new) + mm(values, probs, NN)

    def body(index, carry):
        step(pl.multiple_of(index * WIDE, WIDE), WIDE, False)
        return carry

    lax.fori_loop(0, block // 2, body, 0)

    @pl.when(block % 2 == 1)
    def _():
        step(pl.multiple_of((block - 1) * QB, QB), QB, False)

    step(pl.multiple_of(block * QB, QB), QB, True)
    outs = []
    for head in range(heads):
        total = total_ref[head]
        mass = total[HD : HD + 1, :]
        lse_ref[head : head + 1, :] = high_ref[head : head + 1, :] + jnp.log(mass)
        outs.append(total[:HD, :] * (1.0 / mass))
    o_ref[...] = jnp.concatenate(outs, 0).T.astype(bf16)


def attend(first, queries, keys, values_t, carried):
    count, q_cols = queries.shape
    heads = q_cols // HD
    blocks = count // QB
    split = blocks * 5 // 8
    start = split if first else 0
    return pl.pallas_call(
        functools.partial(attend_kernel, heads, start),
        grid=(blocks - split if first else split,),
        in_specs=[
            pl.BlockSpec((QB, q_cols), lambda i: (start + i, 0)),
            pl.BlockSpec((count, 128), lambda i: (0, 0)),
            pl.BlockSpec((128, count), lambda i: (0, 0)),
        ]
        + [pl.BlockSpec(memory_space=pl.ANY)] * len(carried),
        out_specs=[
            pl.BlockSpec((QB, q_cols), lambda i: (start + i, 0)),
            pl.BlockSpec((8, QB), lambda i: (0, start + i)),
        ],
        out_shape=[
            jax.ShapeDtypeStruct((count, q_cols), bf16),
            jax.ShapeDtypeStruct((8, count), f32),
        ],
        scratch_shapes=[
            pltpu.VMEM((heads, QB, 128), bf16),
            pltpu.VMEM((8, QB), f32),
            pltpu.VMEM((heads, 128, QB), f32),
        ],
        input_output_aliases={3 + index: index for index in range(len(carried))},
        cost_estimate=cost(heads * count * count * 256, 2 * count * q_cols),
        name="attend",
    )(queries, keys, values_t, *carried)


def attend_back_kernel(
    heads,
    first,
    q_ref,
    do_ref,
    o_ref,
    lse_ref,
    k_ref,
    kt_ref,
    v_ref,
    table_ref,
    *refs,
):
    carried = refs[:3] if first else ()
    outs = refs[len(carried) : -6]
    qs_ref, ds_ref, delta_ref, dq_ref, dk_ref, dv_ref = refs[-6:]
    step_id = pl.program_id(0)
    block = first + step_id
    last = pl.num_programs(0) - 1
    q_cols = heads * HD

    @pl.when(step_id == 0)
    def _():
        dk_ref[...] = carried[1][...] if first else jnp.zeros(dk_ref.shape, f32)
        dv_ref[...] = carried[2][...] if first else jnp.zeros(dv_ref.shape, f32)
        if first:
            outs[0][: first * QB, :q_cols] = carried[0][...]

    rows = q_ref[...]
    grads = do_ref[...]
    product = (grads.astype(f32) * o_ref[...].astype(f32)).T
    for head in range(heads):
        qs_ref[head] = head_slab(rows, head, 1.0)
        ds_ref[head] = head_slab(grads, head, 0.0)
        delta_ref[head : head + 1, :] = jnp.sum(
            product[head * HD : (head + 1) * HD, :], axis=0, keepdims=True
        )
    dq_ref[...] = jnp.zeros(dq_ref.shape, f32)

    def step(start, diagonal):
        here = pl.ds(start, QB)
        keys = k_ref[here, :]
        keys_t = kt_ref[:, here]
        values = v_ref[here, :]
        dk = dk_ref[here, :]
        dv = dv_ref[here, :]

        def products(head):
            return (mm(keys, qs_ref[head], NT), mm(values, ds_ref[head], NT))

        ready = products(0)
        for head in range(heads):
            score, prob_grad = ready
            if head + 1 < heads:
                ready = products(head + 1)
            probs = jnp.exp(score - lse_ref[head : head + 1, :])
            if diagonal:
                probs = jnp.where(causal(QB, QB), probs, 0.0)
            dv = dv + mm(probs.astype(bf16), ds_ref[head], NN)
            score_grad = (probs * (prob_grad - delta_ref[head : head + 1, :])).astype(bf16)
            dk = dk + mm(score_grad, qs_ref[head], NN)
            dq_ref[head] = dq_ref[head] + mm(keys_t, score_grad, NN)
        dk_ref[here, :] = dk
        dv_ref[here, :] = dv

    def body(index, carry):
        step(pl.multiple_of(index * QB, QB), False)
        return carry

    lax.fori_loop(0, block, body, 0)
    step(pl.multiple_of(block * QB, QB), True)
    dq = jnp.concatenate([dq_ref[head, :HD, :] for head in range(heads)], 0).T * ATTN_SCALE
    here = pl.ds(pl.multiple_of(block * QB, QB), QB)
    dq = unrotate(dq, *turn_at(table_ref, block)).astype(bf16)
    if first:
        outs[0][here, :q_cols] = dq
    else:
        outs[0][...] = dq

    @pl.when(step_id == last)
    def _():
        if not first:
            outs[1][...] = dk_ref[...]
            outs[2][...] = dv_ref[...]
            return

        def finish(index, carry):
            there = pl.ds(pl.multiple_of(index * QB, QB), QB)
            dk = dk_ref[there, :]
            lane = lax.broadcasted_iota(jnp.int32, dk.shape, 1)
            dk = unrotate(jnp.where(lane < HD, dk, 0.0), *turn_at(table_ref, index))
            dv = dv_ref[there, :]
            outs[0][there, q_cols:] = jnp.concatenate([dk[:, :HD], dv[:, :HD]], 1).astype(bf16)
            return carry

        lax.fori_loop(0, dk_ref.shape[0] // QB, finish, 0)


def attend_back(first, queries, out_grads, attended, lse, keys, keys_t, values, table, carried):
    count, q_cols = queries.shape
    heads = q_cols // HD
    blocks = count // QB
    split = blocks * 5 // 8
    steps = blocks - split if first else split
    start = split if first else 0
    row = lambda i: (start + i, 0)
    whole = lambda i: (0, 0)
    total = pl.BlockSpec((count, 128), whole)
    total_shape = jax.ShapeDtypeStruct((count, 128), f32)
    early = (split * QB, q_cols)
    if first:
        out_specs = pl.BlockSpec((count, q_cols + 128), whole)
        out_shape = jax.ShapeDtypeStruct((count, q_cols + 128), bf16)
    else:
        out_specs = [pl.BlockSpec((QB, q_cols), row), total, total]
        out_shape = [jax.ShapeDtypeStruct(early, bf16), total_shape, total_shape]
    return pl.pallas_call(
        functools.partial(attend_back_kernel, heads, start),
        grid=(steps,),
        in_specs=[
            pl.BlockSpec((QB, q_cols), row),
            pl.BlockSpec((QB, q_cols), row),
            pl.BlockSpec((QB, q_cols), row),
            pl.BlockSpec((8, QB), lambda i: (0, start + i)),
            total,
            pl.BlockSpec((128, count), whole),
            total,
            pl.BlockSpec(table.shape, whole),
        ]
        + ([pl.BlockSpec(early, whole), total, total] if first else []),
        out_specs=out_specs,
        out_shape=out_shape,
        scratch_shapes=[
            pltpu.VMEM((heads, QB, 128), bf16),
            pltpu.VMEM((heads, QB, 128), bf16),
            pltpu.VMEM((8, QB), f32),
            pltpu.VMEM((heads, 128, QB), f32),
            pltpu.VMEM((count, 128), f32),
            pltpu.VMEM((count, 128), f32),
        ],
        cost_estimate=cost(heads * count * count * 640, 10 * count * q_cols),
        name="attend_back",
    )(queries, out_grads, attended, lse, keys, keys_t, values, table, *carried)


LENGTH, CORE, CHIP, RING = 0, 1, 2, 3


def out_norm_kernel(ids_ref, o_ref, mine_ref, other_ref, rows_ref, gain_ref, middle_ref, normed_ref):
    step = pl.program_id(0)
    steps = pl.num_programs(0)
    groups, _, q_cols = o_ref.shape
    cols = mine_ref.shape[1]

    def work(w_ref, core, index):
        total = None
        for place in range(groups):
            term = mm(
                o_ref[ids_ref[RING + place]], w_ref[place * q_cols : (place + 1) * q_cols, :], NN
            )
            total = term if total is None else total + term
        first = core * (steps // 2) + index
        here = pl.ds(pl.multiple_of(first * cols, cols), cols)
        middle_ref[:, here] = rows_ref[:, here].astype(f32) + RESID * total

    core = ids_ref[CORE]
    pl.when(step < steps // 2)(lambda: work(mine_ref, core, step))
    pl.when(step >= steps // 2)(lambda: work(other_ref, 1 - core, step - steps // 2))

    @pl.when(step == steps - 1)
    def _():
        middle = middle_ref[...]
        row_scale = lax.rsqrt(jnp.mean(middle * middle, axis=-1, keepdims=True) + EPSILON)
        normed_ref[...] = (middle * row_scale * gain_ref[...]).astype(bf16)


def out_norm(ids, attended, w_mine, w_other, hidden, gain):
    groups, share, q_cols = attended.shape
    width = hidden.shape[1]
    whole = lambda j, s: (0, 0)
    steps = 2
    return pl.pallas_call(
        out_norm_kernel,
        grid_spec=pltpu.PrefetchScalarGridSpec(
            num_scalar_prefetch=1,
            grid=(steps,),
            in_specs=[
                pl.BlockSpec((groups, share, q_cols), lambda j, s: (0, 0, 0)),
                pl.BlockSpec(
                    (groups * q_cols, width // steps), lambda j, s: (0, jnp.minimum(j, steps // 2 - 1))
                ),
                pl.BlockSpec(
                    (groups * q_cols, width // steps), lambda j, s: (0, jnp.maximum(j - steps // 2, 0))
                ),
                pl.BlockSpec((share, width), lambda j, s: (s[RING], 0)),
                pl.BlockSpec((1, width), whole),
            ],
            out_specs=[pl.BlockSpec((share, width), whole), pl.BlockSpec((share, width), whole)],
        ),
        out_shape=[
            jax.ShapeDtypeStruct((share, width), f32),
            jax.ShapeDtypeStruct((share, width), bf16),
        ],
        cost_estimate=cost(2 * groups * share * q_cols * width, 2 * groups * q_cols * width),
        name="out_project_and_norm",
    )(ids, attended, w_mine, w_other, hidden, gain)


def norm_back_kernel(
    ids_ref,
    own_ref,
    up_ref,
    down_ref,
    middle_ref,
    gain_ref,
    cotangent_ref,
    mine_ref,
    other_ref,
    dh_ref,
    da_ref,
    gain_grad_ref,
    do_ref,
):
    step = pl.program_id(0)

    @pl.when(step == 0)
    def _():
        incoming = own_ref[...].astype(f32) + up_ref[...].astype(f32) + down_ref[...].astype(f32)
        middle = middle_ref[...]
        row_scale = lax.rsqrt(jnp.mean(middle * middle, axis=-1, keepdims=True) + EPSILON)
        normed = middle * row_scale
        gain_grad_ref[...] = jnp.sum(incoming * normed, axis=0, keepdims=True)
        scaled = incoming * gain_ref[...]
        branch = row_scale * (scaled - normed * jnp.mean(scaled * normed, axis=-1, keepdims=True))
        share = middle.shape[0]
        position = ids_ref[RING] * share + lax.broadcasted_iota(jnp.int32, (share, 1), 0)
        direct = jnp.where(position < ids_ref[LENGTH], cotangent_ref[...].astype(f32), 0.0)
        dh = direct + branch
        dh_ref[...] = dh
        da_ref[...] = (RESID * dh).astype(bf16)

    rows, cols = mine_ref.shape
    q_cols = do_ref.shape[2]
    core = ids_ref[CORE]
    mine = da_ref[:, pl.ds(pl.multiple_of(core * cols, cols), cols)]
    other = da_ref[:, pl.ds(pl.multiple_of((1 - core) * cols, cols), cols)]
    per_step = rows // q_cols
    for index in range(per_step):
        here = slice(index * q_cols, (index + 1) * q_cols)
        grad = mm(mine, mine_ref[here, :], NT) + mm(other, other_ref[here, :], NT)
        do_ref[ids_ref[RING + step * per_step + index]] = grad.astype(bf16)


def norm_back(ids, parts, middle, gain, cotangent, w_mine, w_other, q_cols):
    share, width = middle.shape
    groups = w_mine.shape[0] // q_cols
    whole = lambda t, s: (0, 0)
    weight = pl.BlockSpec((groups * q_cols // 2, width // 2), lambda t, s: (t, 0))
    return pl.pallas_call(
        norm_back_kernel,
        grid_spec=pltpu.PrefetchScalarGridSpec(
            num_scalar_prefetch=1,
            grid=(2,),
            in_specs=[pl.BlockSpec((share, width), whole)] * 4
            + [
                pl.BlockSpec((1, width), whole),
                pl.BlockSpec((share, width), lambda t, s: (s[RING], 0)),
                weight,
                weight,
            ],
            out_specs=[
                pl.BlockSpec((share, width), whole),
                pl.BlockSpec((share, width), whole),
                pl.BlockSpec((1, width), whole),
                pl.BlockSpec((groups, share, q_cols), lambda t, s: (0, 0, 0)),
            ],
        ),
        out_shape=[
            jax.ShapeDtypeStruct((share, width), f32),
            jax.ShapeDtypeStruct((share, width), bf16),
            jax.ShapeDtypeStruct((1, width), f32),
            jax.ShapeDtypeStruct((groups, share, q_cols), bf16),
        ],
        cost_estimate=cost(2 * groups * share * q_cols * width, 2 * groups * q_cols * width),
        name="norm_back_and_project",
    )(ids, *parts, middle, gain, cotangent, w_mine, w_other)


def in_grad_kernel(ids_ref, own_ref, up_ref, down_ref, rows_ref, gain_ref, dh_ref, out_ref):
    incoming = own_ref[...].astype(f32) + up_ref[...].astype(f32) + down_ref[...].astype(f32)
    rows = rows_ref[...].astype(f32)
    row_scale = lax.rsqrt(jnp.mean(rows * rows, axis=-1, keepdims=True) + EPSILON)
    normed = rows * row_scale
    scaled = incoming * gain_ref[...]
    branch = row_scale * (scaled - normed * jnp.mean(scaled * normed, axis=-1, keepdims=True))
    out_ref[...] = dh_ref[...] + branch


def in_grad(ids, terms, got, hidden, gain, dh):
    share, width = dh.shape
    steps = 4
    rows = share // steps
    row = lambda j, s: (j, 0)
    own = lambda j, s: (steps * s[RING] + j, 0)
    return pl.pallas_call(
        in_grad_kernel,
        grid_spec=pltpu.PrefetchScalarGridSpec(
            num_scalar_prefetch=1,
            grid=(steps,),
            in_specs=[
                pl.BlockSpec((rows, width), own),
                pl.BlockSpec((rows, width), row),
                pl.BlockSpec((rows, width), row),
                pl.BlockSpec((rows, width), own),
                pl.BlockSpec((1, width), lambda j, s: (0, 0)),
                pl.BlockSpec((rows, width), row),
            ],
            out_specs=pl.BlockSpec((rows, width), row),
        ),
        out_shape=jax.ShapeDtypeStruct((share, width), f32),
        cost_estimate=cost(20 * share * width, 16 * share * width),
        name="input_grad",
    )(ids, terms, *got, hidden, gain, dh)


def core_halves(chips):
    def piece(i, s):
        chip = (s[CHIP] + i) % chips
        return 2 * chip + jnp.where(i < chips, 1 - s[CORE], s[CORE])

    sent = lambda i: jnp.minimum(i, chips - 1)
    kept = lambda i: jnp.maximum(i - chips, 0)
    return piece, sent, kept


def out_wgrad_kernel(ids_ref, o_ref, da_ref, send_ref, keep_ref):
    step = pl.program_id(0)
    groups, _, q_cols = o_ref.shape

    def store(ref):
        for group in range(groups):
            part = mm(o_ref[group], da_ref[...], TN)
            ref[0, group * q_cols : (group + 1) * q_cols, :] = part.astype(bf16)

    half = pl.num_programs(0) // 2
    pl.when(step < half)(lambda: store(send_ref))
    pl.when(step >= half)(lambda: store(keep_ref))


def out_wgrad_parts(ids, attended, branch_grad, replicas):
    groups, share, q_cols = attended.shape
    width = branch_grad.shape[1]
    cols = width // replicas
    chips = replicas // 2
    piece, sent, kept = core_halves(chips)
    out = jax.ShapeDtypeStruct((chips, groups * q_cols, cols), bf16)
    block = (1, groups * q_cols, cols)
    return pl.pallas_call(
        out_wgrad_kernel,
        grid_spec=pltpu.PrefetchScalarGridSpec(
            num_scalar_prefetch=1,
            grid=(replicas,),
            in_specs=[
                pl.BlockSpec((groups, share, q_cols), lambda i, s: (0, 0, 0)),
                pl.BlockSpec((share, cols), lambda i, s: (0, piece(i, s))),
            ],
            out_specs=[
                pl.BlockSpec(block, lambda i, s: (sent(i), 0, 0)),
                pl.BlockSpec(block, lambda i, s: (kept(i), 0, 0)),
            ],
        ),
        out_shape=[out, out],
        cost_estimate=cost(2 * groups * share * q_cols * width, 2 * groups * q_cols * width),
        name="out_weight_grad",
    )(ids, attended, branch_grad)


def qkv_wgrad_kernel(
    ids_ref,
    normed_ref,
    grad_ref,
    w_ref,
    gain_ref,
    other_gain_ref,
    q_send_ref,
    q_keep_ref,
    s_send_ref,
    s_keep_ref,
):
    step = pl.program_id(0)
    cols = normed_ref.shape[1]
    q_cols = q_send_ref.shape[2]

    def store(q_ref, s_ref):
        grad = mm(normed_ref[...], grad_ref[...], TN)
        q_ref[0] = grad[:, :q_cols].astype(bf16)
        s_ref[0, :, : 2 * HD] = grad[:, q_cols:]
        gain = jnp.sum(grad * w_ref[...].astype(f32), axis=1, keepdims=True)
        lane = lax.broadcasted_iota(jnp.int32, (cols, 128), 1)
        first = jnp.where(lane == 0, gain / gain_ref[...], 0.0)
        s_ref[0, :, 2 * HD :] = jnp.where(lane == 1, other_gain_ref[...], first)

    half = pl.num_programs(0) // 2
    pl.when(step < half)(lambda: store(q_send_ref, s_send_ref))
    pl.when(step >= half)(lambda: store(q_keep_ref, s_keep_ref))


def qkv_wgrad_parts(ids, normed, grads, w_qkv, gain, other_gain, replicas):
    count, width = normed.shape
    all_cols = grads.shape[1]
    q_cols = all_cols - 2 * HD
    chips = replicas // 2
    cols = width // replicas
    piece, sent, kept = core_halves(chips)
    down = lambda n: pl.BlockSpec((cols, n), lambda i, s: (piece(i, s), 0))
    out = lambda n, where: pl.BlockSpec((1, cols, n), lambda i, s: (where(i), 0, 0))
    shape = lambda n, kind: jax.ShapeDtypeStruct((chips, cols, n), kind)
    return pl.pallas_call(
        qkv_wgrad_kernel,
        grid_spec=pltpu.PrefetchScalarGridSpec(
            num_scalar_prefetch=1,
            grid=(replicas,),
            in_specs=[
                pl.BlockSpec((count, cols), lambda i, s: (0, piece(i, s))),
                pl.BlockSpec((count, all_cols), lambda i, s: (0, 0)),
                down(all_cols),
                down(1),
                down(1),
            ],
            out_specs=[out(q_cols, sent), out(q_cols, kept), out(256, sent), out(256, kept)],
        ),
        out_shape=[shape(q_cols, bf16)] * 2 + [shape(256, f32)] * 2,
        cost_estimate=cost(2 * count * width * all_cols, 3 * count * width),
        name="projection_weight_grads",
    )(ids, normed, grads, w_qkv, gain, other_gain)


def layer_out_kernel(middle_ref, own_ref, up_ref, down_ref, out_ref):
    total = own_ref[...].astype(f32) + up_ref[...].astype(f32) + down_ref[...].astype(f32)
    out_ref[...] = (middle_ref[...] + RESID * total).astype(bf16)


def layer_output(middle, own, own_row, got):
    share, width = middle.shape
    spec = lambda row: pl.BlockSpec((share, WIDE), lambda j: (row, j))
    return pl.pallas_call(
        layer_out_kernel,
        grid=(width // WIDE,),
        in_specs=[spec(0), spec(own_row), spec(0), spec(0)],
        out_specs=spec(0),
        out_shape=jax.ShapeDtypeStruct((share, width), bf16),
        cost_estimate=cost(5 * share * width, 12 * share * width),
        name="layer_output",
    )(middle, own, *got)


def ring_add_kernel(first, ids_ref, term_ref, got_ref, out_ref):
    rows = got_ref.shape[0]
    if rows < out_ref.shape[0]:
        out_ref[...] = term_ref[...]
    here = slice(first, first + rows)
    out_ref[here, :] = (term_ref[here, :].astype(f32) + got_ref[...].astype(f32)).astype(bf16)


def ring_add(ids, terms, block, place, got, first, share):
    width = terms.shape[1]
    cols = width // 2
    which = lambda j, s: (s[RING + place] if block is None else block, j)
    column = lambda j, s: (0, j)
    return pl.pallas_call(
        functools.partial(ring_add_kernel, first),
        grid_spec=pltpu.PrefetchScalarGridSpec(
            num_scalar_prefetch=1,
            grid=(2,),
            in_specs=[
                pl.BlockSpec((share, cols), which),
                pl.BlockSpec((got.shape[0], cols), column),
            ],
            out_specs=pl.BlockSpec((share, cols), column),
        ),
        out_shape=jax.ShapeDtypeStruct((share, width), bf16),
        cost_estimate=cost(2 * share * width, 6 * share * width),
        name="ring_add",
    )(ids, terms, got)


def swiglu_kernel(pieces, members, row, ids_ref, *refs):
    piece_refs = refs[:pieces]
    cot_ref, gate_ref, up_ref, down_ref = refs[pieces : pieces + 4]
    outs = refs[-19:-13]
    x, dm, wg, wu, wd, act, dgate, dup, in_sem, gate_sem, up_sem, down_sem, out_sem = refs[-13:]
    kept, dn_ref = outs[:5], outs[5]
    rows = x.shape[0]
    share = rows // len(members)
    width, units = wg.shape
    blocks = gate_sem.shape[0]
    block = units // blocks
    part = width // blocks
    arrivals = []
    at = 0
    for ref in piece_refs:
        count = ref.shape[0]
        arrivals.append((ref, x.at[at : at + count, :]))
        at += count
    for index, place in enumerate(members):
        first = pl.multiple_of(ids_ref[RING + place] * share, share)
        here = slice(index * share, (index + 1) * share)
        arrivals.append((cot_ref.at[pl.ds(first, share), :], dm.at[here, :]))
    arrivals = [pltpu.make_async_copy(*pair, in_sem.at[i]) for i, pair in enumerate(arrivals)]

    def weights(u):
        here = pl.ds(pl.multiple_of(u * block, block), block)
        return (
            pltpu.make_async_copy(gate_ref.at[:, here], wg.at[:, here], gate_sem.at[u]),
            pltpu.make_async_copy(up_ref.at[:, here], wu.at[:, here], up_sem.at[u]),
            pltpu.make_async_copy(down_ref.at[here, :], wd.at[here, :], down_sem.at[u]),
        )

    for copy in arrivals[:pieces]:
        copy.start()
    for copy in weights(0):
        copy.start()
    for copy in arrivals[pieces:]:
        copy.start()
    for u in range(1, blocks):
        for copy in weights(u):
            copy.start()
    for copy in arrivals:
        copy.wait()
    for index, place in enumerate(members):
        here = slice(index * share, (index + 1) * share)
        position = ids_ref[RING + place] * share + lax.broadcasted_iota(jnp.int32, (share, 1), 0)
        scaled = dm[here, :].astype(f32) * RESID
        dm[here, :] = jnp.where(position < ids_ref[LENGTH], scaled, 0.0).astype(bf16)

    def one_block(u, carry):
        for copy in weights(u):
            copy.wait()
        here = pl.ds(pl.multiple_of(u * block, block), block)
        gate = mm(x[...], wg[:, here], NN)
        up = mm(x[...], wu[:, here], NN)
        grad = mm(dm[...], wd[here, :], NT)
        sg = jax.nn.sigmoid(gate)
        silu = gate * sg
        act[:, here] = (silu * up).astype(bf16)
        dgate[:, here] = (grad * up * sg * (1.0 + gate * (1.0 - sg))).astype(bf16)
        dup[:, here] = (grad * silu).astype(bf16)
        return carry

    lax.fori_loop(0, blocks, one_block, 0)

    def one_part(n, carry):
        here = pl.ds(pl.multiple_of(n * part, part), part)
        grad = mm(dgate[...], wg[here, :], NT) + mm(dup[...], wu[here, :], NT)
        dn_ref[:, here] = grad.astype(bf16)
        return carry

    one_part(0, 0)
    leaving = [
        pltpu.make_async_copy(src, dst.at[pl.ds(row, rows), :], out_sem.at[i])
        for i, (src, dst) in enumerate(zip((x, dm, act, dgate, dup), kept))
    ]
    for copy in leaving:
        copy.start()
    lax.fori_loop(1, blocks, one_part, 0)
    for copy in leaving:
        copy.wait()


def swiglu(ids, pieces, members, cotangent, weights, row, buffers, total_rows):
    w_gate, w_up, w_down = weights
    width, units = w_gate.shape
    rows = sum(piece.shape[0] for piece in pieces)
    blocks = 2
    hbm = pl.BlockSpec(memory_space=pl.ANY)
    operands = [*pieces, cotangent, *weights, *buffers]
    aliases = {5 + len(pieces) + index: index for index in range(len(buffers))}
    collected = lambda n: jax.ShapeDtypeStruct((total_rows, n), bf16)
    held = lambda *shape: pltpu.VMEM(shape, bf16)
    copies = lambda n: pltpu.SemaphoreType.DMA((n,))
    return pl.pallas_call(
        functools.partial(swiglu_kernel, len(pieces), tuple(members), row),
        grid_spec=pltpu.PrefetchScalarGridSpec(
            num_scalar_prefetch=1,
            grid=(1,),
            in_specs=[hbm] * len(operands),
            out_specs=[hbm] * 5 + [pl.BlockSpec((rows, width), lambda i, s: (0, 0))],
            scratch_shapes=[held(rows, width)] * 2
            + [held(width, units), held(width, units), held(units, width)]
            + [held(rows, units)] * 3
            + [copies(len(pieces) + len(members)), *([copies(blocks)] * 3), copies(5)],
        ),
        out_shape=[collected(width)] * 2
        + [collected(units)] * 3
        + [jax.ShapeDtypeStruct((rows, width), bf16)],
        input_output_aliases=aliases,
        compiler_params=grant(58),
        cost_estimate=cost(12 * rows * width * units, 6 * width * units + 16 * rows * width),
        name="swiglu_rows",
    )(ids, *operands)


def ring_order(count):
    inner = 2 if count <= 8 else 4
    outer = count // inner
    cells = [(0, 0)]
    for row in range(outer):
        cells += [(row, c) for c in (range(1, inner) if row % 2 == 0 else range(inner - 1, 0, -1))]
    cells += [(row, 0) for row in range(outer - 1, 0, -1)]
    return [row * inner + c for row, c in cells]


def tie(*values):
    return lax.optimization_barrier(values)


def over_cores(send, keep):
    chips = send.shape[0]
    got = lax.ppermute(send, "dp", [(i, i ^ 1) for i in range(2 * chips)])
    go = [
        (keep[step].astype(f32) + got[step].astype(f32)).astype(send.dtype)
        for step in range(1, chips)
    ]
    return keep, got, go


def over_chips(keep, got, go):
    chips = len(go) + 1
    arriving = []
    for step in range(1, chips):
        to = [(i, ((i // 2 + step) % chips) * 2 + i % 2) for i in range(2 * chips)]
        arriving.append(lax.ppermute(go[step - 1], "dp", to))
    return keep, got, arriving


def total_of(keep, got, arriving):
    total = keep[0].astype(f32) + got[0].astype(f32)
    for term in arriving:
        total = total + term.astype(f32)
    return total


def local(
    hidden_in,
    seq_lengths,
    out_grad,
    attn_gain,
    mlp_gain,
    w_query,
    w_key,
    w_value,
    w_out,
    w_gate,
    w_up,
    w_down,
):
    rows_total, width = hidden_in.shape
    q_cols = w_query.shape[1]
    heads_here = q_cols // HD
    groups = lax.axis_size("tensor")
    replicas = lax.axis_size("dp")
    member = lax.axis_index("tensor")
    replica = lax.axis_index("dp")
    core = replica % 2
    share = rows_total // groups
    half = share // 2
    order = ring_order(groups)
    spot = [order.index(i) for i in range(groups)]
    ahead = [(order[i], order[(i + 1) % groups]) for i in range(groups)]
    behind = [(b, a) for a, b in ahead]
    half_way = groups // 2
    apart = [0]
    for d in range(1, half_way):
        apart += [-d, d]
    apart.append(half_way)
    ring = [[order[(spot[i] + d) % groups] for d in apart] for i in range(groups)]
    ids = jnp.concatenate(
        [
            seq_lengths,
            jnp.stack([core, replica // 2]).astype(jnp.int32),
            jnp.asarray(ring, jnp.int32)[member],
        ]
    )
    table = rope_tables(rows_total)
    gain_one = attn_gain[None, :]
    gain_two = mlp_gain[None, :]

    def exchange(array):
        return lax.all_to_all(array, "tensor", 0, 0, tiled=True)

    def onward(array):
        return lax.ppermute(array, "tensor", ahead)

    def back(array):
        return lax.ppermute(array, "tensor", behind)

    w_own = lax.dynamic_slice_in_dim(w_out, core * (width // 2), width // 2, 1)
    w_hop = onward(w_own), back(w_own)
    w_mine = [w_own]

    def w_next():
        w_mine.extend(w_hop)
        if len(w_mine) < groups - 1:
            return onward(w_hop[0]), back(w_hop[1])
        return onward(w_hop[0][: q_cols // 2]), back(w_hop[1][q_cols // 2 :])

    kv_of = [i * heads_here // (H // KVH) for i in range(groups)]
    w_kv = pick_heads(w_key, w_value, kv_of)
    w_kv = exchange(w_kv).reshape(width, 2 * HD)
    carried = front(0, hidden_in, gain_one, w_query, table, [])
    w_hop, carried = tie(w_hop, carried)
    for _ in range(half_way - 3):
        w_hop = w_next()
    normed_one, queries = front(1, hidden_in, gain_one, w_query, table, carried)
    keys, keys_t, values, values_t = keys_values(seq_lengths, normed_one, w_kv, table)
    w_hop, keys = tie(w_hop, keys)
    w_hop = w_next()
    carried = attend(0, queries, keys, values_t, [])
    w_hop, carried = tie(w_hop, carried)
    w_hop = w_next()
    attended, lse = attend(1, queries, keys, values_t, carried)
    w_hop, attended = tie(w_hop, attended)
    attended_rows = exchange(attended.reshape(groups, share, q_cols))
    w_mine = jnp.concatenate([*w_mine, *w_hop], 0)
    w_other = lax.ppermute(w_mine, "dp", [(i, i ^ 1) for i in range(replicas)])
    w_qkv = jnp.concatenate([w_query, w_kv], 1)
    middle, normed_two = out_norm(ids, attended_rows, w_mine, w_other, hidden_in, gain_two)

    weights = (w_gate, w_up, w_down)
    grads = []
    buffers = []

    def run(pieces, members, row):
        nonlocal buffers
        *buffers, grad = swiglu(
            ids, pieces, members, out_grad, weights, row, buffers, rows_total
        )
        grads.append(grad)

    pieces, members, row = [normed_two], [0], rows_total - 2 * share
    hop = [normed_two, normed_two]
    for d in range(1, half_way + 1):
        if d < half_way:
            hop = [onward(hop[0]), back(hop[1])]
        else:
            hop = [onward(hop[0][:half]), back(hop[1][half:])]
        run(pieces, members, row)
        hop, grads[-1], buffers = tie(hop, grads[-1], buffers)
        pieces = hop
        if d < half_way:
            members, row = [2 * d - 1, 2 * d], 2 * share * (d - 1)
        else:
            members, row = [groups - 1], rows_total - share
    run(pieces, members, row)
    normed_ring, down_ring, act, dgate, dup = buffers

    def first_hop(far):
        return onward(far[:half]), back(far[half:])

    def hop_sums(terms, block, got):
        down = ring_add(ids, terms, block, None, got[1], share - got[1].shape[0], share)
        up = ring_add(ids, terms, block + 1, None, got[0], 0, share)
        return up, down

    def send_on(sums):
        return onward(sums[0]), back(sums[1])

    def next_hop(terms, block, got):
        return send_on(hop_sums(terms, block, got))

    def natural_sums(terms, distance, got):
        first = share - got[1].shape[0]
        down = ring_add(ids, terms, None, 2 * distance - 1, got[1], first, share)
        up = ring_add(ids, terms, None, 2 * distance, got[0], 0, share)
        return up, down

    got = first_hop(grads[-1])
    mlp = mm(act, w_down, NN).astype(bf16)
    mlp_far = [mlp[rows_total - share : rows_total - half], mlp[rows_total - half :]]
    got, mlp, mlp_far = tie(got, mlp, mlp_far)
    fillers = [
        lambda: mm(act, down_ring, TN).astype(bf16),
        lambda: mm(normed_ring, dgate, TN).astype(bf16),
        lambda: mm(normed_ring, dup, TN).astype(bf16),
    ]
    filled = []
    for d in range(half_way - 1, 0, -1):
        got = next_hop(grads[d], 0, got)
        if len(filled) < 3:
            *got, value = tie(*got, fillers[len(filled)]())
            filled.append(value)
    down_wgrad, gate_wgrad, up_wgrad = filled
    scatter = lambda a, d: lax.psum_scatter(a, "dp", scatter_dimension=d, tiled=True)
    down_wgrad = scatter(down_wgrad, 1)
    gate_wgrad = scatter(gate_wgrad, 0)
    up_wgrad = scatter(up_wgrad, 0)

    got, mlp_far = tie(got, mlp_far)
    out_got = send_on(mlp_far)
    dh, da, gain_part, do_send = norm_back(
        ids, [grads[0], *got], middle, gain_two, out_grad, w_mine, w_other, q_cols
    )
    *out_got, do_send, da = tie(*out_got, do_send, da)
    do = exchange(do_send).reshape(rows_total, q_cols)
    out_parts = out_wgrad_parts(ids, attended_rows, da, replicas)
    out_sums = hop_sums(mlp, 2 * half_way - 4, out_got)
    do, out_parts, out_sums = tie(do, out_parts, out_sums)
    out_got = send_on(out_sums)
    out_parts = over_cores(*out_parts)
    operands = [queries, do, attended, lse, keys, keys_t, values, table]
    carried = attend_back(0, *operands, [])
    out_got, carried, down_wgrad, out_parts = tie(out_got, carried, down_wgrad, out_parts)
    out_terms = over_chips(*out_parts)
    for d in range(half_way - 2, 1, -1):
        out_got = next_hop(mlp, 2 * d - 2, out_got)
    qkv_grad = attend_back(1, *operands, carried)
    out_got, qkv_grad = tie(out_got, qkv_grad)

    far = lax.dynamic_slice_in_dim(qkv_grad, ids[RING + groups - 1] * share, share, 0)
    far = mm(far, w_qkv, NT).astype(bf16)
    in_got = first_hop(far)
    qkv_grad, far, out_got = tie(qkv_grad, far, out_got)
    out_got = next_hop(mlp, 0, out_got)
    first_grad = mm(qkv_grad, w_qkv, NT).astype(bf16)
    q_send, q_keep, s_send, s_keep = qkv_wgrad_parts(
        ids,
        normed_one,
        qkv_grad,
        w_qkv,
        attn_gain[:, None],
        gain_part.reshape(width, 1),
        replicas,
    )
    in_got, out_got, q_send, s_send, gate_wgrad, first_grad = tie(
        in_got, out_got, q_send, s_send, gate_wgrad, first_grad
    )
    small = over_cores(s_send, s_keep)
    query_wgrad = over_cores(q_send, q_keep)
    for d in range(half_way - 1, 0, -1):
        in_sums = natural_sums(first_grad, d, in_got)
        if d == half_way - 1:
            in_got = send_on(in_sums)
            small = over_chips(*small)
            query_wgrad = over_chips(*query_wgrad)
            in_got, small, query_wgrad, out_terms = tie(in_got, small, query_wgrad, out_terms)
            out_wgrad = total_of(*out_terms).astype(bf16)
            out_wgrad = lax.psum_scatter(out_wgrad, "tensor", scatter_dimension=0, tiled=True)
            small, query_wgrad = total_of(*small), total_of(*query_wgrad)
            layer_out = layer_output(middle, mlp, groups - 2, out_got)
            continue
        in_got = send_on(in_sums)
        if d == half_way - 2:
            in_got, layer_out, up_wgrad = tie(in_got, layer_out, up_wgrad)
    pieces = exchange(small.reshape(groups, small.shape[0] // groups, 256))
    input_grad = in_grad(ids, first_grad, in_got, hidden_in, gain_one, dh)
    gains = jnp.sum(pieces[:, :, 128:130], axis=0)
    kv = pieces[:, :, :128].reshape(KVH, groups // KVH, -1, 128).sum(axis=1)
    kv = jnp.swapaxes(kv, 0, 1)
    key_wgrad = kv[:, :, :HD].reshape(-1, KVH * HD)
    value_wgrad = kv[:, :, HD:].reshape(-1, KVH * HD)
    return (
        layer_out,
        input_grad,
        gains[:, 0],
        gains[:, 1],
        query_wgrad,
        key_wgrad,
        value_wgrad,
        out_wgrad.astype(f32),
        gate_wgrad.astype(f32),
        up_wgrad.astype(f32),
        down_wgrad.astype(f32),
    )


def solution(mesh):
    placed = (
        P("dp", None),
        P("dp"),
        P("dp", None),
        P(),
        P(),
        P(None, "tensor"),
        P("tensor", None),
        P("tensor", None),
        P("tensor", None),
        P(None, "tensor"),
        P(None, "tensor"),
        P("tensor", None),
    )
    return jax.shard_map(
        local,
        mesh=mesh,
        in_specs=placed,
        out_specs=(
            P(("dp", "tensor"), None),
            P(("dp", "tensor"), None),
            P(("dp", "tensor")),
            P(("dp", "tensor")),
            P("dp", "tensor"),
            P(("dp", "tensor"), None),
            P(("dp", "tensor"), None),
            P("tensor", "dp"),
            P("dp", "tensor"),
            P("dp", "tensor"),
            P("tensor", "dp"),
        ),
        check_vma=False,
    )
```

```python
import functools
import math

import jax
import jax.numpy as jnp
from jax import lax
from jax.experimental import pallas as pl
from jax.experimental.pallas import tpu as pltpu
from jax.sharding import PartitionSpec as P

H = 32
KVH = 8
HD = 64
SEQ_LEN = 2048
QB = 256
WIDE = 512

RESID = 0.22
ATTN_SCALE = 0.015625
EPSILON = 1e-05
THETA_LOG = math.log(10000000.0)
MASKED = -1e30

f32 = jnp.float32
bf16 = jnp.bfloat16
NN = (((1,), (0,)), ((), ()))
NT = (((1,), (1,)), ((), ()))
TN = (((0,), (0,)), ((), ()))


def mm(left, right, dims):
    return lax.dot_general(left, right, dims, preferred_element_type=f32)


def grant(mib):
    return pltpu.CompilerParams(vmem_limit_bytes=mib * 1024 * 1024)


def cost(flops, nbytes):
    return pl.CostEstimate(flops=int(flops), bytes_accessed=int(nbytes), transcendentals=0)


def rope_tables(count):
    lane = jnp.arange(128, dtype=jnp.int32) % (HD // 2)
    freqs = jnp.exp(-THETA_LOG * (2 * lane).astype(f32) / HD)[None, :]
    fine = jnp.arange(QB, dtype=jnp.int32)
    coarse = jnp.arange(count // QB * 8, dtype=jnp.int32) // 8 * QB
    angle_rows = jnp.concatenate([fine, coarse]).astype(f32)[:, None] * freqs
    return jnp.concatenate([jnp.cos(angle_rows), jnp.sin(angle_rows)], 1)


def turn_at(table_ref, block):
    fine = table_ref[:QB, :]
    coarse = table_ref[pl.ds(pl.multiple_of(QB + block * 8, 8), 8), :][:1, :]
    cos_f, sin_f, cos_c, sin_c = fine[:, :128], fine[:, 128:], coarse[:, :128], coarse[:, 128:]
    return cos_f * cos_c - sin_f * sin_c, sin_f * cos_c + cos_f * sin_c


def widen(table, count):
    return table if count == 128 else jnp.concatenate([table] * (count // 128), 1)


def swap_halves(rows):
    count = rows.shape[1]
    lane = lax.broadcasted_iota(jnp.int32, rows.shape, 1)
    ahead = pltpu.roll(rows, count - HD // 2, 1)
    behind = pltpu.roll(rows, HD // 2, 1)
    return jnp.where(lane % HD < HD // 2, ahead, behind)


def half_sign(shape):
    lane = lax.broadcasted_iota(jnp.int32, shape, 1)
    return jnp.where(lane % HD < HD // 2, -1.0, 1.0)


def rotate(rows, cosines, sines):
    count = rows.shape[1]
    turned = swap_halves(rows) * half_sign(rows.shape)
    return rows * widen(cosines, count) + turned * widen(sines, count)


def unrotate(rows, cosines, sines):
    count = rows.shape[1]
    turned = swap_halves(rows * widen(sines, count)) * half_sign(rows.shape)
    return rows * widen(cosines, count) - turned


def front_kernel(start, rows_ref, gain_ref, wq_ref, table_ref, *refs):
    normed_ref, q_ref = refs[-2:]
    rows = rows_ref[...].astype(f32)
    row_scale = lax.rsqrt(jnp.mean(rows * rows, axis=-1, keepdims=True) + EPSILON)
    normed_ref[...] = (rows * row_scale * gain_ref[...]).astype(bf16)
    q_raw = mm(normed_ref[...], wq_ref[...], NN)
    turned = rotate(q_raw, *turn_at(table_ref, start + pl.program_id(0)))
    q_ref[...] = (turned.astype(bf16).astype(f32) * ATTN_SCALE).astype(bf16)


def front(first, hidden, gain, w_query, table, carried):
    count, width = hidden.shape
    q_cols = w_query.shape[1]
    steps = count // QB // 2
    start = steps if first else 0
    row = lambda i: (start + i, 0)
    whole = lambda i: (0, 0)
    return pl.pallas_call(
        functools.partial(front_kernel, start),
        grid=(steps,),
        in_specs=[
            pl.BlockSpec((QB, width), row),
            pl.BlockSpec((1, width), whole),
            pl.BlockSpec((width, q_cols), whole),
            pl.BlockSpec(table.shape, whole),
        ]
        + [pl.BlockSpec(memory_space=pl.ANY)] * len(carried),
        out_specs=[pl.BlockSpec((QB, width), row), pl.BlockSpec((QB, q_cols), row)],
        out_shape=[
            jax.ShapeDtypeStruct((count, width), bf16),
            jax.ShapeDtypeStruct((count, q_cols), bf16),
        ],
        input_output_aliases={4 + index: index for index in range(len(carried))},
        cost_estimate=cost(count * width * q_cols, 3 * count * width),
        name="norm_and_query",
    )(hidden, gain, w_query, table, *carried)


def keys_kernel(length_ref, normed_ref, wkv_ref, table_ref, k_ref, kt_ref, v_ref, vt_ref):
    kv_raw = mm(normed_ref[...], wkv_ref[...], NN)
    lane = lax.broadcasted_iota(jnp.int32, kv_raw.shape, 1)
    position = pl.program_id(0) * WIDE + lax.broadcasted_iota(jnp.int32, kv_raw.shape, 0)
    blocks = [turn_at(table_ref, pl.program_id(0) * (WIDE // QB) + i) for i in range(WIDE // QB)]
    cosines, sines = (jnp.concatenate([b[i] for b in blocks], 0) for i in range(2))
    turned = rotate(kv_raw, cosines, sines)
    keys = jnp.where(lane < HD, turned, 0.0)
    blocked = jnp.where((lane == HD) & (position >= length_ref[0]), MASKED, 0.0)
    k_ref[...] = (keys + blocked).astype(bf16)
    kt_ref[...] = keys.T.astype(bf16)
    values = jnp.concatenate([kv_raw[:, HD:], kv_raw[:, :HD]], 1)
    values = jnp.where(lane < HD, values, 1.0)
    v_ref[...] = values.astype(bf16)
    vt_ref[...] = values.T.astype(bf16)


def keys_values(length, normed, w_kv, table):
    count, width = normed.shape
    row = lambda i, s: (i, 0)
    col = lambda i, s: (0, i)
    return pl.pallas_call(
        keys_kernel,
        grid_spec=pltpu.PrefetchScalarGridSpec(
            num_scalar_prefetch=1,
            grid=(count // WIDE,),
            in_specs=[
                pl.BlockSpec((WIDE, width), row),
                pl.BlockSpec((width, 128), lambda i, s: (0, 0)),
                pl.BlockSpec(table.shape, lambda i, s: (0, 0)),
            ],
            out_specs=[
                pl.BlockSpec((WIDE, 128), row),
                pl.BlockSpec((128, WIDE), col),
                pl.BlockSpec((WIDE, 128), row),
                pl.BlockSpec((128, WIDE), col),
            ],
        ),
        out_shape=[
            jax.ShapeDtypeStruct((count, 128), bf16),
            jax.ShapeDtypeStruct((128, count), bf16),
            jax.ShapeDtypeStruct((count, 128), bf16),
            jax.ShapeDtypeStruct((128, count), bf16),
        ],
        cost_estimate=cost(2 * count * width * 128, 2 * count * width),
        name="keys_and_values",
    )(length, normed, w_kv, table)


def pick_kernel(picks, k_ref, v_ref, out_ref):
    for index, head in enumerate(picks):
        both = [ref[:, 128 * (head // 2) : 128 * (head // 2) + 128] for ref in (k_ref, v_ref)]
        at = head % 2 * HD
        out_ref[index] = jnp.concatenate([b[:, at : at + HD] for b in both], 1)


def pick_heads(w_key, w_value, picks):
    return pl.pallas_call(
        functools.partial(pick_kernel, picks),
        out_shape=jax.ShapeDtypeStruct((len(picks), w_key.shape[0], 2 * HD), bf16),
        name="pick_heads",
    )(w_key, w_value)


def head_slab(rows, head, fill):
    pair = rows[:, 128 * (head // 2) : 128 * (head // 2) + 128]
    if head % 2:
        pair = jnp.concatenate([pair[:, HD:], pair[:, :HD]], 1)
    lane = lax.broadcasted_iota(jnp.int32, pair.shape, 1)
    other = jnp.where(lane == HD, jnp.full(pair.shape, fill, f32), 0.0).astype(pair.dtype)
    return jnp.where(lane < HD, pair, other)


def causal(keys_count, rows_count):
    key = lax.broadcasted_iota(jnp.int32, (keys_count, rows_count), 0)
    return key <= lax.broadcasted_iota(jnp.int32, (keys_count, rows_count), 1)


def attend_kernel(heads, start, q_ref, k_ref, vt_ref, *refs):
    o_ref, lse_ref, slab_ref, high_ref, total_ref = refs[-5:]
    block = start + pl.program_id(0)
    rows = q_ref[...]
    for head in range(heads):
        slab_ref[head] = head_slab(rows, head, 1.0)
    high_ref[...] = jnp.full(high_ref.shape, MASKED, f32)
    total_ref[...] = jnp.zeros(total_ref.shape, f32)

    def step(start, width, diagonal):
        keys = k_ref[pl.ds(start, width), :]
        values = vt_ref[:, pl.ds(start, width)]
        scores = [mm(keys, slab_ref[head], NT) for head in range(heads)]
        for head in range(heads):
            score = scores[head]
            if diagonal:
                score = jnp.where(causal(width, QB), score, MASKED)
            old = high_ref[head : head + 1, :]
            new = jnp.maximum(old, jnp.max(score, axis=0, keepdims=True))
            probs = jnp.exp(score - new).astype(bf16)
            high_ref[head : head + 1, :] = new
            total_ref[head] = total_ref[head] * jnp.exp(old - new) + mm(values, probs, NN)

    def body(index, carry):
        step(pl.multiple_of(index * WIDE, WIDE), WIDE, False)
        return carry

    lax.fori_loop(0, block // 2, body, 0)

    @pl.when(block % 2 == 1)
    def _():
        step(pl.multiple_of((block - 1) * QB, QB), QB, False)

    step(pl.multiple_of(block * QB, QB), QB, True)
    outs = []
    for head in range(heads):
        total = total_ref[head]
        mass = total[HD : HD + 1, :]
        lse_ref[head : head + 1, :] = high_ref[head : head + 1, :] + jnp.log(mass)
        outs.append(total[:HD, :] * (1.0 / mass))
    o_ref[...] = jnp.concatenate(outs, 0).T.astype(bf16)


def attend(first, queries, keys, values_t, carried):
    count, q_cols = queries.shape
    heads = q_cols // HD
    blocks = count // QB
    split = blocks * 5 // 8
    start = split if first else 0
    return pl.pallas_call(
        functools.partial(attend_kernel, heads, start),
        grid=(blocks - split if first else split,),
        in_specs=[
            pl.BlockSpec((QB, q_cols), lambda i: (start + i, 0)),
            pl.BlockSpec((count, 128), lambda i: (0, 0)),
            pl.BlockSpec((128, count), lambda i: (0, 0)),
        ]
        + [pl.BlockSpec(memory_space=pl.ANY)] * len(carried),
        out_specs=[
            pl.BlockSpec((QB, q_cols), lambda i: (start + i, 0)),
            pl.BlockSpec((8, QB), lambda i: (0, start + i)),
        ],
        out_shape=[
            jax.ShapeDtypeStruct((count, q_cols), bf16),
            jax.ShapeDtypeStruct((8, count), f32),
        ],
        scratch_shapes=[
            pltpu.VMEM((heads, QB, 128), bf16),
            pltpu.VMEM((8, QB), f32),
            pltpu.VMEM((heads, 128, QB), f32),
        ],
        input_output_aliases={3 + index: index for index in range(len(carried))},
        cost_estimate=cost(heads * count * count * 256, 2 * count * q_cols),
        name="attend",
    )(queries, keys, values_t, *carried)


def attend_back_kernel(
    heads,
    first,
    q_ref,
    do_ref,
    o_ref,
    lse_ref,
    k_ref,
    kt_ref,
    v_ref,
    table_ref,
    *refs,
):
    carried = refs[:3] if first else ()
    outs = refs[len(carried) : -6]
    qs_ref, ds_ref, delta_ref, dq_ref, dk_ref, dv_ref = refs[-6:]
    step_id = pl.program_id(0)
    block = first + step_id
    last = pl.num_programs(0) - 1
    q_cols = heads * HD

    @pl.when(step_id == 0)
    def _():
        dk_ref[...] = carried[1][...] if first else jnp.zeros(dk_ref.shape, f32)
        dv_ref[...] = carried[2][...] if first else jnp.zeros(dv_ref.shape, f32)
        if first:
            outs[0][: first * QB, :q_cols] = carried[0][...]

    rows = q_ref[...]
    grads = do_ref[...]
    product = (grads.astype(f32) * o_ref[...].astype(f32)).T
    for head in range(heads):
        qs_ref[head] = head_slab(rows, head, 1.0)
        ds_ref[head] = head_slab(grads, head, 0.0)
        delta_ref[head : head + 1, :] = jnp.sum(
            product[head * HD : (head + 1) * HD, :], axis=0, keepdims=True
        )
    dq_ref[...] = jnp.zeros(dq_ref.shape, f32)

    def step(start, diagonal):
        here = pl.ds(start, QB)
        keys = k_ref[here, :]
        keys_t = kt_ref[:, here]
        values = v_ref[here, :]
        dk = dk_ref[here, :]
        dv = dv_ref[here, :]

        def products(head):
            return (mm(keys, qs_ref[head], NT), mm(values, ds_ref[head], NT))

        ready = products(0)
        for head in range(heads):
            score, prob_grad = ready
            if head + 1 < heads:
                ready = products(head + 1)
            probs = jnp.exp(score - lse_ref[head : head + 1, :])
            if diagonal:
                probs = jnp.where(causal(QB, QB), probs, 0.0)
            dv = dv + mm(probs.astype(bf16), ds_ref[head], NN)
            score_grad = (probs * (prob_grad - delta_ref[head : head + 1, :])).astype(bf16)
            dk = dk + mm(score_grad, qs_ref[head], NN)
            dq_ref[head] = dq_ref[head] + mm(keys_t, score_grad, NN)
        dk_ref[here, :] = dk
        dv_ref[here, :] = dv

    def body(index, carry):
        step(pl.multiple_of(index * QB, QB), False)
        return carry

    lax.fori_loop(0, block, body, 0)
    step(pl.multiple_of(block * QB, QB), True)
    dq = jnp.concatenate([dq_ref[head, :HD, :] for head in range(heads)], 0).T * ATTN_SCALE
    here = pl.ds(pl.multiple_of(block * QB, QB), QB)
    dq = unrotate(dq, *turn_at(table_ref, block)).astype(bf16)
    if first:
        outs[0][here, :q_cols] = dq
    else:
        outs[0][...] = dq

    @pl.when(step_id == last)
    def _():
        if not first:
            outs[1][...] = dk_ref[...]
            outs[2][...] = dv_ref[...]
            return

        def finish(index, carry):
            there = pl.ds(pl.multiple_of(index * QB, QB), QB)
            dk = dk_ref[there, :]
            lane = lax.broadcasted_iota(jnp.int32, dk.shape, 1)
            dk = unrotate(jnp.where(lane < HD, dk, 0.0), *turn_at(table_ref, index))
            dv = dv_ref[there, :]
            outs[0][there, q_cols:] = jnp.concatenate([dk[:, :HD], dv[:, :HD]], 1).astype(bf16)
            return carry

        lax.fori_loop(0, dk_ref.shape[0] // QB, finish, 0)


def attend_back(first, queries, out_grads, attended, lse, keys, keys_t, values, table, carried):
    count, q_cols = queries.shape
    heads = q_cols // HD
    blocks = count // QB
    split = blocks * 5 // 8
    steps = blocks - split if first else split
    start = split if first else 0
    row = lambda i: (start + i, 0)
    whole = lambda i: (0, 0)
    total = pl.BlockSpec((count, 128), whole)
    total_shape = jax.ShapeDtypeStruct((count, 128), f32)
    early = (split * QB, q_cols)
    if first:
        out_specs = pl.BlockSpec((count, q_cols + 128), whole)
        out_shape = jax.ShapeDtypeStruct((count, q_cols + 128), bf16)
    else:
        out_specs = [pl.BlockSpec((QB, q_cols), row), total, total]
        out_shape = [jax.ShapeDtypeStruct(early, bf16), total_shape, total_shape]
    return pl.pallas_call(
        functools.partial(attend_back_kernel, heads, start),
        grid=(steps,),
        in_specs=[
            pl.BlockSpec((QB, q_cols), row),
            pl.BlockSpec((QB, q_cols), row),
            pl.BlockSpec((QB, q_cols), row),
            pl.BlockSpec((8, QB), lambda i: (0, start + i)),
            total,
            pl.BlockSpec((128, count), whole),
            total,
            pl.BlockSpec(table.shape, whole),
        ]
        + ([pl.BlockSpec(early, whole), total, total] if first else []),
        out_specs=out_specs,
        out_shape=out_shape,
        scratch_shapes=[
            pltpu.VMEM((heads, QB, 128), bf16),
            pltpu.VMEM((heads, QB, 128), bf16),
            pltpu.VMEM((8, QB), f32),
            pltpu.VMEM((heads, 128, QB), f32),
            pltpu.VMEM((count, 128), f32),
            pltpu.VMEM((count, 128), f32),
        ],
        cost_estimate=cost(heads * count * count * 640, 10 * count * q_cols),
        name="attend_back",
    )(queries, out_grads, attended, lse, keys, keys_t, values, table, *carried)


LENGTH, CORE, CHIP, RING = 0, 1, 2, 3


def out_norm_kernel(ids_ref, o_ref, mine_ref, other_ref, rows_ref, gain_ref, middle_ref, normed_ref):
    step = pl.program_id(0)
    steps = pl.num_programs(0)
    groups, _, q_cols = o_ref.shape
    cols = mine_ref.shape[1]

    def work(w_ref, core, index):
        total = None
        for place in range(groups):
            term = mm(
                o_ref[ids_ref[RING + place]], w_ref[place * q_cols : (place + 1) * q_cols, :], NN
            )
            total = term if total is None else total + term
        first = core * (steps // 2) + index
        here = pl.ds(pl.multiple_of(first * cols, cols), cols)
        middle_ref[:, here] = rows_ref[:, here].astype(f32) + RESID * total

    core = ids_ref[CORE]
    pl.when(step < steps // 2)(lambda: work(mine_ref, core, step))
    pl.when(step >= steps // 2)(lambda: work(other_ref, 1 - core, step - steps // 2))

    @pl.when(step == steps - 1)
    def _():
        middle = middle_ref[...]
        row_scale = lax.rsqrt(jnp.mean(middle * middle, axis=-1, keepdims=True) + EPSILON)
        normed_ref[...] = (middle * row_scale * gain_ref[...]).astype(bf16)


def out_norm(ids, attended, w_mine, w_other, hidden, gain):
    groups, share, q_cols = attended.shape
    width = hidden.shape[1]
    whole = lambda j, s: (0, 0)
    steps = 2
    return pl.pallas_call(
        out_norm_kernel,
        grid_spec=pltpu.PrefetchScalarGridSpec(
            num_scalar_prefetch=1,
            grid=(steps,),
            in_specs=[
                pl.BlockSpec((groups, share, q_cols), lambda j, s: (0, 0, 0)),
                pl.BlockSpec(
                    (groups * q_cols, width // steps), lambda j, s: (0, jnp.minimum(j, steps // 2 - 1))
                ),
                pl.BlockSpec(
                    (groups * q_cols, width // steps), lambda j, s: (0, jnp.maximum(j - steps // 2, 0))
                ),
                pl.BlockSpec((share, width), lambda j, s: (s[RING], 0)),
                pl.BlockSpec((1, width), whole),
            ],
            out_specs=[pl.BlockSpec((share, width), whole), pl.BlockSpec((share, width), whole)],
        ),
        out_shape=[
            jax.ShapeDtypeStruct((share, width), f32),
            jax.ShapeDtypeStruct((share, width), bf16),
        ],
        cost_estimate=cost(2 * groups * share * q_cols * width, 2 * groups * q_cols * width),
        name="out_project_and_norm",
    )(ids, attended, w_mine, w_other, hidden, gain)


def norm_back_kernel(
    ids_ref,
    own_ref,
    up_ref,
    down_ref,
    middle_ref,
    gain_ref,
    cotangent_ref,
    mine_ref,
    other_ref,
    dh_ref,
    da_ref,
    gain_grad_ref,
    do_ref,
):
    step = pl.program_id(0)

    @pl.when(step == 0)
    def _():
        incoming = own_ref[...].astype(f32) + up_ref[...].astype(f32) + down_ref[...].astype(f32)
        middle = middle_ref[...]
        row_scale = lax.rsqrt(jnp.mean(middle * middle, axis=-1, keepdims=True) + EPSILON)
        normed = middle * row_scale
        gain_grad_ref[...] = jnp.sum(incoming * normed, axis=0, keepdims=True)
        scaled = incoming * gain_ref[...]
        branch = row_scale * (scaled - normed * jnp.mean(scaled * normed, axis=-1, keepdims=True))
        share = middle.shape[0]
        position = ids_ref[RING] * share + lax.broadcasted_iota(jnp.int32, (share, 1), 0)
        direct = jnp.where(position < ids_ref[LENGTH], cotangent_ref[...].astype(f32), 0.0)
        dh = direct + branch
        dh_ref[...] = dh
        da_ref[...] = (RESID * dh).astype(bf16)

    rows, cols = mine_ref.shape
    q_cols = do_ref.shape[2]
    core = ids_ref[CORE]
    mine = da_ref[:, pl.ds(pl.multiple_of(core * cols, cols), cols)]
    other = da_ref[:, pl.ds(pl.multiple_of((1 - core) * cols, cols), cols)]
    per_step = rows // q_cols
    for index in range(per_step):
        here = slice(index * q_cols, (index + 1) * q_cols)
        grad = mm(mine, mine_ref[here, :], NT) + mm(other, other_ref[here, :], NT)
        do_ref[ids_ref[RING + step * per_step + index]] = grad.astype(bf16)


def norm_back(ids, parts, middle, gain, cotangent, w_mine, w_other, q_cols):
    share, width = middle.shape
    groups = w_mine.shape[0] // q_cols
    whole = lambda t, s: (0, 0)
    weight = pl.BlockSpec((groups * q_cols // 2, width // 2), lambda t, s: (t, 0))
    return pl.pallas_call(
        norm_back_kernel,
        grid_spec=pltpu.PrefetchScalarGridSpec(
            num_scalar_prefetch=1,
            grid=(2,),
            in_specs=[pl.BlockSpec((share, width), whole)] * 4
            + [
                pl.BlockSpec((1, width), whole),
                pl.BlockSpec((share, width), lambda t, s: (s[RING], 0)),
                weight,
                weight,
            ],
            out_specs=[
                pl.BlockSpec((share, width), whole),
                pl.BlockSpec((share, width), whole),
                pl.BlockSpec((1, width), whole),
                pl.BlockSpec((groups, share, q_cols), lambda t, s: (0, 0, 0)),
            ],
        ),
        out_shape=[
            jax.ShapeDtypeStruct((share, width), f32),
            jax.ShapeDtypeStruct((share, width), bf16),
            jax.ShapeDtypeStruct((1, width), f32),
            jax.ShapeDtypeStruct((groups, share, q_cols), bf16),
        ],
        cost_estimate=cost(2 * groups * share * q_cols * width, 2 * groups * q_cols * width),
        name="norm_back_and_project",
    )(ids, *parts, middle, gain, cotangent, w_mine, w_other)


def in_grad_kernel(ids_ref, own_ref, up_ref, down_ref, rows_ref, gain_ref, dh_ref, out_ref):
    incoming = own_ref[...].astype(f32) + up_ref[...].astype(f32) + down_ref[...].astype(f32)
    rows = rows_ref[...].astype(f32)
    row_scale = lax.rsqrt(jnp.mean(rows * rows, axis=-1, keepdims=True) + EPSILON)
    normed = rows * row_scale
    scaled = incoming * gain_ref[...]
    branch = row_scale * (scaled - normed * jnp.mean(scaled * normed, axis=-1, keepdims=True))
    out_ref[...] = dh_ref[...] + branch


def in_grad(ids, terms, got, hidden, gain, dh):
    share, width = dh.shape
    steps = 4
    rows = share // steps
    row = lambda j, s: (j, 0)
    own = lambda j, s: (steps * s[RING] + j, 0)
    return pl.pallas_call(
        in_grad_kernel,
        grid_spec=pltpu.PrefetchScalarGridSpec(
            num_scalar_prefetch=1,
            grid=(steps,),
            in_specs=[
                pl.BlockSpec((rows, width), own),
                pl.BlockSpec((rows, width), row),
                pl.BlockSpec((rows, width), row),
                pl.BlockSpec((rows, width), own),
                pl.BlockSpec((1, width), lambda j, s: (0, 0)),
                pl.BlockSpec((rows, width), row),
            ],
            out_specs=pl.BlockSpec((rows, width), row),
        ),
        out_shape=jax.ShapeDtypeStruct((share, width), f32),
        cost_estimate=cost(20 * share * width, 16 * share * width),
        name="input_grad",
    )(ids, terms, *got, hidden, gain, dh)


def core_halves(chips):
    def piece(i, s):
        chip = (s[CHIP] + i) % chips
        return 2 * chip + jnp.where(i < chips, 1 - s[CORE], s[CORE])

    sent = lambda i: jnp.minimum(i, chips - 1)
    kept = lambda i: jnp.maximum(i - chips, 0)
    return piece, sent, kept


def out_wgrad_kernel(ids_ref, o_ref, da_ref, send_ref, keep_ref):
    step = pl.program_id(0)
    groups, _, q_cols = o_ref.shape

    def store(ref):
        for group in range(groups):
            part = mm(o_ref[group], da_ref[...], TN)
            ref[0, group * q_cols : (group + 1) * q_cols, :] = part.astype(bf16)

    half = pl.num_programs(0) // 2
    pl.when(step < half)(lambda: store(send_ref))
    pl.when(step >= half)(lambda: store(keep_ref))


def out_wgrad_parts(ids, attended, branch_grad, replicas):
    groups, share, q_cols = attended.shape
    width = branch_grad.shape[1]
    cols = width // replicas
    chips = replicas // 2
    piece, sent, kept = core_halves(chips)
    out = jax.ShapeDtypeStruct((chips, groups * q_cols, cols), bf16)
    block = (1, groups * q_cols, cols)
    return pl.pallas_call(
        out_wgrad_kernel,
        grid_spec=pltpu.PrefetchScalarGridSpec(
            num_scalar_prefetch=1,
            grid=(replicas,),
            in_specs=[
                pl.BlockSpec((groups, share, q_cols), lambda i, s: (0, 0, 0)),
                pl.BlockSpec((share, cols), lambda i, s: (0, piece(i, s))),
            ],
            out_specs=[
                pl.BlockSpec(block, lambda i, s: (sent(i), 0, 0)),
                pl.BlockSpec(block, lambda i, s: (kept(i), 0, 0)),
            ],
        ),
        out_shape=[out, out],
        cost_estimate=cost(2 * groups * share * q_cols * width, 2 * groups * q_cols * width),
        name="out_weight_grad",
    )(ids, attended, branch_grad)


def qkv_wgrad_kernel(
    ids_ref,
    normed_ref,
    grad_ref,
    w_ref,
    gain_ref,
    other_gain_ref,
    q_send_ref,
    q_keep_ref,
    s_send_ref,
    s_keep_ref,
):
    step = pl.program_id(0)
    cols = normed_ref.shape[1]
    q_cols = q_send_ref.shape[2]

    def store(q_ref, s_ref):
        grad = mm(normed_ref[...], grad_ref[...], TN)
        q_ref[0] = grad[:, :q_cols].astype(bf16)
        s_ref[0, :, : 2 * HD] = grad[:, q_cols:]
        gain = jnp.sum(grad * w_ref[...].astype(f32), axis=1, keepdims=True)
        lane = lax.broadcasted_iota(jnp.int32, (cols, 128), 1)
        first = jnp.where(lane == 0, gain / gain_ref[...], 0.0)
        s_ref[0, :, 2 * HD :] = jnp.where(lane == 1, other_gain_ref[...], first)

    half = pl.num_programs(0) // 2
    pl.when(step < half)(lambda: store(q_send_ref, s_send_ref))
    pl.when(step >= half)(lambda: store(q_keep_ref, s_keep_ref))


def qkv_wgrad_parts(ids, normed, grads, w_qkv, gain, other_gain, replicas):
    count, width = normed.shape
    all_cols = grads.shape[1]
    q_cols = all_cols - 2 * HD
    chips = replicas // 2
    cols = width // replicas
    piece, sent, kept = core_halves(chips)
    down = lambda n: pl.BlockSpec((cols, n), lambda i, s: (piece(i, s), 0))
    out = lambda n, where: pl.BlockSpec((1, cols, n), lambda i, s: (where(i), 0, 0))
    shape = lambda n, kind: jax.ShapeDtypeStruct((chips, cols, n), kind)
    return pl.pallas_call(
        qkv_wgrad_kernel,
        grid_spec=pltpu.PrefetchScalarGridSpec(
            num_scalar_prefetch=1,
            grid=(replicas,),
            in_specs=[
                pl.BlockSpec((count, cols), lambda i, s: (0, piece(i, s))),
                pl.BlockSpec((count, all_cols), lambda i, s: (0, 0)),
                down(all_cols),
                down(1),
                down(1),
            ],
            out_specs=[out(q_cols, sent), out(q_cols, kept), out(256, sent), out(256, kept)],
        ),
        out_shape=[shape(q_cols, bf16)] * 2 + [shape(256, f32)] * 2,
        cost_estimate=cost(2 * count * width * all_cols, 3 * count * width),
        name="projection_weight_grads",
    )(ids, normed, grads, w_qkv, gain, other_gain)


def layer_out_kernel(middle_ref, own_ref, up_ref, down_ref, out_ref):
    total = own_ref[...].astype(f32) + up_ref[...].astype(f32) + down_ref[...].astype(f32)
    out_ref[...] = (middle_ref[...] + RESID * total).astype(bf16)


def layer_output(middle, own, own_row, got):
    share, width = middle.shape
    spec = lambda row: pl.BlockSpec((share, WIDE), lambda j: (row, j))
    return pl.pallas_call(
        layer_out_kernel,
        grid=(width // WIDE,),
        in_specs=[spec(0), spec(own_row), spec(0), spec(0)],
        out_specs=spec(0),
        out_shape=jax.ShapeDtypeStruct((share, width), bf16),
        cost_estimate=cost(5 * share * width, 12 * share * width),
        name="layer_output",
    )(middle, own, *got)


def ring_add_kernel(first, ids_ref, term_ref, got_ref, out_ref):
    rows = got_ref.shape[0]
    if rows < out_ref.shape[0]:
        out_ref[...] = term_ref[...]
    here = slice(first, first + rows)
    out_ref[here, :] = (term_ref[here, :].astype(f32) + got_ref[...].astype(f32)).astype(bf16)


def ring_add(ids, terms, block, place, got, first, share):
    width = terms.shape[1]
    cols = width // 2
    which = lambda j, s: (s[RING + place] if block is None else block, j)
    column = lambda j, s: (0, j)
    return pl.pallas_call(
        functools.partial(ring_add_kernel, first),
        grid_spec=pltpu.PrefetchScalarGridSpec(
            num_scalar_prefetch=1,
            grid=(2,),
            in_specs=[
                pl.BlockSpec((share, cols), which),
                pl.BlockSpec((got.shape[0], cols), column),
            ],
            out_specs=pl.BlockSpec((share, cols), column),
        ),
        out_shape=jax.ShapeDtypeStruct((share, width), bf16),
        cost_estimate=cost(2 * share * width, 6 * share * width),
        name="ring_add",
    )(ids, terms, got)


def swiglu_kernel(pieces, members, row, ids_ref, *refs):
    piece_refs = refs[:pieces]
    cot_ref, gate_ref, up_ref, down_ref = refs[pieces : pieces + 4]
    outs = refs[-19:-13]
    x, dm, wg, wu, wd, act, dgate, dup, in_sem, gate_sem, up_sem, down_sem, out_sem = refs[-13:]
    kept, dn_ref = outs[:5], outs[5]
    rows = x.shape[0]
    share = rows // len(members)
    width, units = wg.shape
    blocks = gate_sem.shape[0]
    block = units // blocks
    part = width // blocks
    arrivals = []
    at = 0
    for ref in piece_refs:
        count = ref.shape[0]
        arrivals.append((ref, x.at[at : at + count, :]))
        at += count
    for index, place in enumerate(members):
        first = pl.multiple_of(ids_ref[RING + place] * share, share)
        here = slice(index * share, (index + 1) * share)
        arrivals.append((cot_ref.at[pl.ds(first, share), :], dm.at[here, :]))
    arrivals = [pltpu.make_async_copy(*pair, in_sem.at[i]) for i, pair in enumerate(arrivals)]

    def weights(u):
        here = pl.ds(pl.multiple_of(u * block, block), block)
        return (
            pltpu.make_async_copy(gate_ref.at[:, here], wg.at[:, here], gate_sem.at[u]),
            pltpu.make_async_copy(up_ref.at[:, here], wu.at[:, here], up_sem.at[u]),
            pltpu.make_async_copy(down_ref.at[here, :], wd.at[here, :], down_sem.at[u]),
        )

    for copy in arrivals[:pieces]:
        copy.start()
    for copy in weights(0):
        copy.start()
    for copy in arrivals[pieces:]:
        copy.start()
    for u in range(1, blocks):
        for copy in weights(u):
            copy.start()
    for copy in arrivals:
        copy.wait()
    for index, place in enumerate(members):
        here = slice(index * share, (index + 1) * share)
        position = ids_ref[RING + place] * share + lax.broadcasted_iota(jnp.int32, (share, 1), 0)
        scaled = dm[here, :].astype(f32) * RESID
        dm[here, :] = jnp.where(position < ids_ref[LENGTH], scaled, 0.0).astype(bf16)

    def one_block(u, carry):
        for copy in weights(u):
            copy.wait()
        here = pl.ds(pl.multiple_of(u * block, block), block)
        gate = mm(x[...], wg[:, here], NN)
        up = mm(x[...], wu[:, here], NN)
        grad = mm(dm[...], wd[here, :], NT)
        sg = jax.nn.sigmoid(gate)
        silu = gate * sg
        act[:, here] = (silu * up).astype(bf16)
        dgate[:, here] = (grad * up * sg * (1.0 + gate * (1.0 - sg))).astype(bf16)
        dup[:, here] = (grad * silu).astype(bf16)
        return carry

    lax.fori_loop(0, blocks, one_block, 0)

    def one_part(n, carry):
        here = pl.ds(pl.multiple_of(n * part, part), part)
        grad = mm(dgate[...], wg[here, :], NT) + mm(dup[...], wu[here, :], NT)
        dn_ref[:, here] = grad.astype(bf16)
        return carry

    one_part(0, 0)
    leaving = [
        pltpu.make_async_copy(src, dst.at[pl.ds(row, rows), :], out_sem.at[i])
        for i, (src, dst) in enumerate(zip((x, dm, act, dgate, dup), kept))
    ]
    for copy in leaving:
        copy.start()
    lax.fori_loop(1, blocks, one_part, 0)
    for copy in leaving:
        copy.wait()


def swiglu(ids, pieces, members, cotangent, weights, row, buffers, total_rows):
    w_gate, w_up, w_down = weights
    width, units = w_gate.shape
    rows = sum(piece.shape[0] for piece in pieces)
    blocks = 2
    hbm = pl.BlockSpec(memory_space=pl.ANY)
    operands = [*pieces, cotangent, *weights, *buffers]
    aliases = {5 + len(pieces) + index: index for index in range(len(buffers))}
    collected = lambda n: jax.ShapeDtypeStruct((total_rows, n), bf16)
    held = lambda *shape: pltpu.VMEM(shape, bf16)
    copies = lambda n: pltpu.SemaphoreType.DMA((n,))
    return pl.pallas_call(
        functools.partial(swiglu_kernel, len(pieces), tuple(members), row),
        grid_spec=pltpu.PrefetchScalarGridSpec(
            num_scalar_prefetch=1,
            grid=(1,),
            in_specs=[hbm] * len(operands),
            out_specs=[hbm] * 5 + [pl.BlockSpec((rows, width), lambda i, s: (0, 0))],
            scratch_shapes=[held(rows, width)] * 2
            + [held(width, units), held(width, units), held(units, width)]
            + [held(rows, units)] * 3
            + [copies(len(pieces) + len(members)), *([copies(blocks)] * 3), copies(5)],
        ),
        out_shape=[collected(width)] * 2
        + [collected(units)] * 3
        + [jax.ShapeDtypeStruct((rows, width), bf16)],
        input_output_aliases=aliases,
        compiler_params=grant(58),
        cost_estimate=cost(12 * rows * width * units, 6 * width * units + 16 * rows * width),
        name="swiglu_rows",
    )(ids, *operands)


def ring_order(count):
    inner = 2 if count <= 8 else 4
    outer = count // inner
    cells = [(0, 0)]
    for row in range(outer):
        cells += [(row, c) for c in (range(1, inner) if row % 2 == 0 else range(inner - 1, 0, -1))]
    cells += [(row, 0) for row in range(outer - 1, 0, -1)]
    return [row * inner + c for row, c in cells]


def tie(*values):
    return lax.optimization_barrier(values)


def other_core(array):
    replicas = lax.axis_size("dp")
    return lax.ppermute(array, "dp", [(i, i ^ 1) for i in range(replicas)])


def over_chips(keep, got):
    chips = keep.shape[0]
    arriving = []
    for step in range(1, chips):
        to = [(i, ((i // 2 + step) % chips) * 2 + i % 2) for i in range(2 * chips)]
        go = (keep[step].astype(f32) + got[step].astype(f32)).astype(keep.dtype)
        arriving.append(lax.ppermute(go, "dp", to))
    return keep, got, arriving


def total_of(keep, got, arriving):
    total = keep[0].astype(f32) + got[0].astype(f32)
    for term in arriving:
        total = total + term.astype(f32)
    return total


def local(
    hidden_in,
    seq_lengths,
    out_grad,
    attn_gain,
    mlp_gain,
    w_query,
    w_key,
    w_value,
    w_out,
    w_gate,
    w_up,
    w_down,
):
    rows_total, width = hidden_in.shape
    q_cols = w_query.shape[1]
    heads_here = q_cols // HD
    groups = lax.axis_size("tensor")
    replicas = lax.axis_size("dp")
    member = lax.axis_index("tensor")
    replica = lax.axis_index("dp")
    core = replica % 2
    share = rows_total // groups
    half = share // 2
    order = ring_order(groups)
    spot = [order.index(i) for i in range(groups)]
    ahead = [(order[i], order[(i + 1) % groups]) for i in range(groups)]
    behind = [(b, a) for a, b in ahead]
    half_way = groups // 2
    apart = [0]
    for d in range(1, half_way):
        apart += [-d, d]
    apart.append(half_way)
    ring = [[order[(spot[i] + d) % groups] for d in apart] for i in range(groups)]
    ids = jnp.concatenate(
        [
            seq_lengths,
            jnp.stack([core, replica // 2]).astype(jnp.int32),
            jnp.asarray(ring, jnp.int32)[member],
        ]
    )
    table = rope_tables(rows_total)
    gain_one = attn_gain[None, :]
    gain_two = mlp_gain[None, :]

    def exchange(array):
        return lax.all_to_all(array, "tensor", 0, 0, tiled=True)

    def onward(array):
        return lax.ppermute(array, "tensor", ahead)

    def back(array):
        return lax.ppermute(array, "tensor", behind)

    w_own = lax.dynamic_slice_in_dim(w_out, core * (width // 2), width // 2, 1)
    w_hop = onward(w_own), back(w_own)
    w_mine = [w_own]

    def w_next():
        w_mine.extend(w_hop)
        if len(w_mine) < groups - 1:
            return onward(w_hop[0]), back(w_hop[1])
        return onward(w_hop[0][: q_cols // 2]), back(w_hop[1][q_cols // 2 :])

    kv_of = [i * heads_here // (H // KVH) for i in range(groups)]
    w_kv = pick_heads(w_key, w_value, kv_of)
    w_kv = exchange(w_kv).reshape(width, 2 * HD)
    carried = front(0, hidden_in, gain_one, w_query, table, [])
    w_hop, carried = tie(w_hop, carried)
    for _ in range(half_way - 3):
        w_hop = w_next()
    normed_one, queries = front(1, hidden_in, gain_one, w_query, table, carried)
    keys, keys_t, values, values_t = keys_values(seq_lengths, normed_one, w_kv, table)
    w_hop, keys = tie(w_hop, keys)
    w_hop = w_next()
    carried = attend(0, queries, keys, values_t, [])
    w_hop, carried = tie(w_hop, carried)
    w_hop = w_next()
    attended, lse = attend(1, queries, keys, values_t, carried)
    w_hop, attended = tie(w_hop, attended)
    attended_rows = exchange(attended.reshape(groups, share, q_cols))
    w_mine = jnp.concatenate([*w_mine, *w_hop], 0)
    w_other = lax.ppermute(w_mine, "dp", [(i, i ^ 1) for i in range(replicas)])
    w_qkv = jnp.concatenate([w_query, w_kv], 1)
    middle, normed_two = out_norm(ids, attended_rows, w_mine, w_other, hidden_in, gain_two)

    weights = (w_gate, w_up, w_down)
    grads = []
    buffers = []

    def run(pieces, members, row):
        nonlocal buffers
        *buffers, grad = swiglu(
            ids, pieces, members, out_grad, weights, row, buffers, rows_total
        )
        grads.append(grad)

    pieces, members, row = [normed_two], [0], rows_total - 2 * share
    hop = [normed_two, normed_two]
    for d in range(1, half_way + 1):
        if d < half_way:
            hop = [onward(hop[0]), back(hop[1])]
        else:
            hop = [onward(hop[0][:half]), back(hop[1][half:])]
        run(pieces, members, row)
        hop, grads[-1], buffers = tie(hop, grads[-1], buffers)
        pieces = hop
        if d < half_way:
            members, row = [2 * d - 1, 2 * d], 2 * share * (d - 1)
        else:
            members, row = [groups - 1], rows_total - share
    run(pieces, members, row)
    normed_ring, down_ring, act, dgate, dup = buffers

    def first_hop(far):
        return onward(far[:half]), back(far[half:])

    def hop_sums(terms, block, got):
        down = ring_add(ids, terms, block, None, got[1], share - got[1].shape[0], share)
        up = ring_add(ids, terms, block + 1, None, got[0], 0, share)
        return up, down

    def send_on(sums):
        return onward(sums[0]), back(sums[1])

    def next_hop(terms, block, got):
        return send_on(hop_sums(terms, block, got))

    def natural_sums(terms, distance, got):
        first = share - got[1].shape[0]
        down = ring_add(ids, terms, None, 2 * distance - 1, got[1], first, share)
        up = ring_add(ids, terms, None, 2 * distance, got[0], 0, share)
        return up, down

    got = first_hop(grads[-1])
    mlp = mm(act, w_down, NN).astype(bf16)
    mlp_far = [mlp[rows_total - share : rows_total - half], mlp[rows_total - half :]]
    got, mlp, mlp_far = tie(got, mlp, mlp_far)
    fillers = [
        lambda: mm(act, down_ring, TN).astype(bf16),
        lambda: mm(normed_ring, dgate, TN).astype(bf16),
        lambda: mm(normed_ring, dup, TN).astype(bf16),
    ]
    filled = []
    for d in range(half_way - 1, 0, -1):
        got = next_hop(grads[d], 0, got)
        if len(filled) < 3:
            *got, value = tie(*got, fillers[len(filled)]())
            filled.append(value)
    down_wgrad, gate_wgrad, up_wgrad = filled
    scatter = lambda a, d: lax.psum_scatter(a, "dp", scatter_dimension=d, tiled=True)
    down_wgrad = scatter(down_wgrad, 1)
    gate_wgrad = scatter(gate_wgrad, 0)
    up_wgrad = scatter(up_wgrad, 0)

    got, mlp_far = tie(got, mlp_far)
    out_got = send_on(mlp_far)
    dh, da, gain_part, do_send = norm_back(
        ids, [grads[0], *got], middle, gain_two, out_grad, w_mine, w_other, q_cols
    )
    *out_got, do_send, da = tie(*out_got, do_send, da)
    do = exchange(do_send).reshape(rows_total, q_cols)
    out_parts = out_wgrad_parts(ids, attended_rows, da, replicas)
    out_sums = hop_sums(mlp, 2 * half_way - 4, out_got)
    do, out_parts, out_sums = tie(do, out_parts, out_sums)
    out_got = send_on(out_sums)
    out_send, out_keep = out_parts
    out_swapped = other_core(out_send)
    operands = [queries, do, attended, lse, keys, keys_t, values, table]
    carried = attend_back(0, *operands, [])
    out_got, carried, down_wgrad, out_swapped = tie(out_got, carried, down_wgrad, out_swapped)
    for d in range(half_way - 2, 1, -1):
        out_got = next_hop(mlp, 2 * d - 2, out_got)
    qkv_grad = attend_back(1, *operands, carried)
    out_got, qkv_grad, out_keep = tie(out_got, qkv_grad, out_keep)

    far = lax.dynamic_slice_in_dim(qkv_grad, ids[RING + groups - 1] * share, share, 0)
    far = mm(far, w_qkv, NT).astype(bf16)
    in_got = first_hop(far)
    qkv_grad, far, out_got, out_keep = tie(qkv_grad, far, out_got, out_keep)
    out_got = next_hop(mlp, 0, out_got)
    out_terms = over_chips(out_keep, out_swapped)
    first_grad = mm(qkv_grad, w_qkv, NT).astype(bf16)
    q_send, q_keep, s_send, s_keep = qkv_wgrad_parts(
        ids,
        normed_one,
        qkv_grad,
        w_qkv,
        attn_gain[:, None],
        gain_part.reshape(width, 1),
        replicas,
    )
    in_got, out_got, q_send, s_send, gate_wgrad, first_grad = tie(
        in_got, out_got, q_send, s_send, gate_wgrad, first_grad
    )
    s_swapped, q_swapped = other_core(s_send), other_core(q_send)
    for d in range(half_way - 1, 0, -1):
        in_sums = natural_sums(first_grad, d, in_got)
        if d == half_way - 1:
            in_got = send_on(in_sums)
            small = over_chips(s_keep, s_swapped)
            query_wgrad = over_chips(q_keep, q_swapped)
            in_got, small, query_wgrad, out_terms = tie(in_got, small, query_wgrad, out_terms)
            out_wgrad = total_of(*out_terms).astype(bf16)
            out_wgrad = lax.psum_scatter(out_wgrad, "tensor", scatter_dimension=0, tiled=True)
            small, query_wgrad = total_of(*small), total_of(*query_wgrad)
            layer_out = layer_output(middle, mlp, groups - 2, out_got)
            continue
        in_got = send_on(in_sums)
        if d == half_way - 2:
            in_got, layer_out, up_wgrad = tie(in_got, layer_out, up_wgrad)
    pieces = exchange(small.reshape(groups, small.shape[0] // groups, 256))
    input_grad = in_grad(ids, first_grad, in_got, hidden_in, gain_one, dh)
    gains = jnp.sum(pieces[:, :, 128:130], axis=0)
    kv = pieces[:, :, :128].reshape(KVH, groups // KVH, -1, 128).sum(axis=1)
    kv = jnp.swapaxes(kv, 0, 1)
    key_wgrad = kv[:, :, :HD].reshape(-1, KVH * HD)
    value_wgrad = kv[:, :, HD:].reshape(-1, KVH * HD)
    return (
        layer_out,
        input_grad,
        gains[:, 0],
        gains[:, 1],
        query_wgrad,
        key_wgrad,
        value_wgrad,
        out_wgrad.astype(f32),
        gate_wgrad.astype(f32),
        up_wgrad.astype(f32),
        down_wgrad.astype(f32),
    )


def solution(mesh):
    placed = (
        P("dp", None),
        P("dp"),
        P("dp", None),
        P(),
        P(),
        P(None, "tensor"),
        P("tensor", None),
        P("tensor", None),
        P("tensor", None),
        P(None, "tensor"),
        P(None, "tensor"),
        P("tensor", None),
    )
    return jax.shard_map(
        local,
        mesh=mesh,
        in_specs=placed,
        out_specs=(
            P(("dp", "tensor"), None),
            P(("dp", "tensor"), None),
            P(("dp", "tensor")),
            P(("dp", "tensor")),
            P("dp", "tensor"),
            P(("dp", "tensor"), None),
            P(("dp", "tensor"), None),
            P("tensor", "dp"),
            P("dp", "tensor"),
            P("dp", "tensor"),
            P("tensor", "dp"),
        ),
        check_vma=False,
    )
```

```python
import functools
import math

import jax
import jax.numpy as jnp
from jax import lax
from jax.experimental import pallas as pl
from jax.experimental.pallas import tpu as pltpu
from jax.sharding import PartitionSpec as P

H = 32
KVH = 8
HD = 64
SEQ_LEN = 2048
QB = 256
WIDE = 512

RESID = 0.22
ATTN_SCALE = 0.015625
EPSILON = 1e-05
THETA_LOG = math.log(10000000.0)
MASKED = -1e30

f32 = jnp.float32
bf16 = jnp.bfloat16
NN = (((1,), (0,)), ((), ()))
NT = (((1,), (1,)), ((), ()))
TN = (((0,), (0,)), ((), ()))


def mm(left, right, dims):
    return lax.dot_general(left, right, dims, preferred_element_type=f32)


def grant(mib):
    return pltpu.CompilerParams(vmem_limit_bytes=mib * 1024 * 1024)


def cost(flops, nbytes):
    return pl.CostEstimate(flops=int(flops), bytes_accessed=int(nbytes), transcendentals=0)


def rope_tables(count):
    lane = jnp.arange(128, dtype=jnp.int32) % (HD // 2)
    freqs = jnp.exp(-THETA_LOG * (2 * lane).astype(f32) / HD)[None, :]
    fine = jnp.arange(QB, dtype=jnp.int32)
    coarse = jnp.arange(count // QB * 8, dtype=jnp.int32) // 8 * QB
    angle_rows = jnp.concatenate([fine, coarse]).astype(f32)[:, None] * freqs
    return jnp.concatenate([jnp.cos(angle_rows), jnp.sin(angle_rows)], 1)


def turn_at(table_ref, block):
    fine = table_ref[:QB, :]
    coarse = table_ref[pl.ds(pl.multiple_of(QB + block * 8, 8), 8), :][:1, :]
    cos_f, sin_f, cos_c, sin_c = fine[:, :128], fine[:, 128:], coarse[:, :128], coarse[:, 128:]
    return cos_f * cos_c - sin_f * sin_c, sin_f * cos_c + cos_f * sin_c


def widen(table, count):
    return table if count == 128 else jnp.concatenate([table] * (count // 128), 1)


def swap_halves(rows):
    count = rows.shape[1]
    lane = lax.broadcasted_iota(jnp.int32, rows.shape, 1)
    ahead = pltpu.roll(rows, count - HD // 2, 1)
    behind = pltpu.roll(rows, HD // 2, 1)
    return jnp.where(lane % HD < HD // 2, ahead, behind)


def half_sign(shape):
    lane = lax.broadcasted_iota(jnp.int32, shape, 1)
    return jnp.where(lane % HD < HD // 2, -1.0, 1.0)


def rotate(rows, cosines, sines):
    count = rows.shape[1]
    turned = swap_halves(rows) * half_sign(rows.shape)
    return rows * widen(cosines, count) + turned * widen(sines, count)


def unrotate(rows, cosines, sines):
    count = rows.shape[1]
    turned = swap_halves(rows * widen(sines, count)) * half_sign(rows.shape)
    return rows * widen(cosines, count) - turned


def front_kernel(start, rows_ref, gain_ref, wq_ref, table_ref, *refs):
    normed_ref, q_ref = refs[-2:]
    rows = rows_ref[...].astype(f32)
    row_scale = lax.rsqrt(jnp.mean(rows * rows, axis=-1, keepdims=True) + EPSILON)
    normed_ref[...] = (rows * row_scale * gain_ref[...]).astype(bf16)
    q_raw = mm(normed_ref[...], wq_ref[...], NN)
    turned = rotate(q_raw, *turn_at(table_ref, start + pl.program_id(0)))
    q_ref[...] = (turned.astype(bf16).astype(f32) * ATTN_SCALE).astype(bf16)


def front(first, hidden, gain, w_query, table, carried):
    count, width = hidden.shape
    q_cols = w_query.shape[1]
    steps = count // QB // 2
    start = steps if first else 0
    row = lambda i: (start + i, 0)
    whole = lambda i: (0, 0)
    return pl.pallas_call(
        functools.partial(front_kernel, start),
        grid=(steps,),
        in_specs=[
            pl.BlockSpec((QB, width), row),
            pl.BlockSpec((1, width), whole),
            pl.BlockSpec((width, q_cols), whole),
            pl.BlockSpec(table.shape, whole),
        ]
        + [pl.BlockSpec(memory_space=pl.ANY)] * len(carried),
        out_specs=[pl.BlockSpec((QB, width), row), pl.BlockSpec((QB, q_cols), row)],
        out_shape=[
            jax.ShapeDtypeStruct((count, width), bf16),
            jax.ShapeDtypeStruct((count, q_cols), bf16),
        ],
        input_output_aliases={4 + index: index for index in range(len(carried))},
        cost_estimate=cost(count * width * q_cols, 3 * count * width),
        name="norm_and_query",
    )(hidden, gain, w_query, table, *carried)


def keys_kernel(length_ref, normed_ref, wkv_ref, table_ref, k_ref, kt_ref, v_ref, vt_ref):
    kv_raw = mm(normed_ref[...], wkv_ref[...], NN)
    lane = lax.broadcasted_iota(jnp.int32, kv_raw.shape, 1)
    position = pl.program_id(0) * WIDE + lax.broadcasted_iota(jnp.int32, kv_raw.shape, 0)
    blocks = [turn_at(table_ref, pl.program_id(0) * (WIDE // QB) + i) for i in range(WIDE // QB)]
    cosines, sines = (jnp.concatenate([b[i] for b in blocks], 0) for i in range(2))
    turned = rotate(kv_raw, cosines, sines)
    keys = jnp.where(lane < HD, turned, 0.0)
    blocked = jnp.where((lane == HD) & (position >= length_ref[0]), MASKED, 0.0)
    k_ref[...] = (keys + blocked).astype(bf16)
    kt_ref[...] = keys.T.astype(bf16)
    values = jnp.concatenate([kv_raw[:, HD:], kv_raw[:, :HD]], 1)
    values = jnp.where(lane < HD, values, 1.0)
    v_ref[...] = values.astype(bf16)
    vt_ref[...] = values.T.astype(bf16)


def keys_values(length, normed, w_kv, table):
    count, width = normed.shape
    row = lambda i, s: (i, 0)
    col = lambda i, s: (0, i)
    return pl.pallas_call(
        keys_kernel,
        grid_spec=pltpu.PrefetchScalarGridSpec(
            num_scalar_prefetch=1,
            grid=(count // WIDE,),
            in_specs=[
                pl.BlockSpec((WIDE, width), row),
                pl.BlockSpec((width, 128), lambda i, s: (0, 0)),
                pl.BlockSpec(table.shape, lambda i, s: (0, 0)),
            ],
            out_specs=[
                pl.BlockSpec((WIDE, 128), row),
                pl.BlockSpec((128, WIDE), col),
                pl.BlockSpec((WIDE, 128), row),
                pl.BlockSpec((128, WIDE), col),
            ],
        ),
        out_shape=[
            jax.ShapeDtypeStruct((count, 128), bf16),
            jax.ShapeDtypeStruct((128, count), bf16),
            jax.ShapeDtypeStruct((count, 128), bf16),
            jax.ShapeDtypeStruct((128, count), bf16),
        ],
        cost_estimate=cost(2 * count * width * 128, 2 * count * width),
        name="keys_and_values",
    )(length, normed, w_kv, table)


def pick_kernel(picks, k_ref, v_ref, out_ref):
    for index, head in enumerate(picks):
        both = [ref[:, 128 * (head // 2) : 128 * (head // 2) + 128] for ref in (k_ref, v_ref)]
        at = head % 2 * HD
        out_ref[index] = jnp.concatenate([b[:, at : at + HD] for b in both], 1)


def pick_heads(w_key, w_value, picks):
    return pl.pallas_call(
        functools.partial(pick_kernel, picks),
        out_shape=jax.ShapeDtypeStruct((len(picks), w_key.shape[0], 2 * HD), bf16),
        name="pick_heads",
    )(w_key, w_value)


def head_slab(rows, head, fill):
    pair = rows[:, 128 * (head // 2) : 128 * (head // 2) + 128]
    if head % 2:
        pair = jnp.concatenate([pair[:, HD:], pair[:, :HD]], 1)
    lane = lax.broadcasted_iota(jnp.int32, pair.shape, 1)
    other = jnp.where(lane == HD, jnp.full(pair.shape, fill, f32), 0.0).astype(pair.dtype)
    return jnp.where(lane < HD, pair, other)


def causal(keys_count, rows_count):
    key = lax.broadcasted_iota(jnp.int32, (keys_count, rows_count), 0)
    return key <= lax.broadcasted_iota(jnp.int32, (keys_count, rows_count), 1)


def attend_kernel(heads, start, q_ref, k_ref, vt_ref, *refs):
    o_ref, lse_ref, slab_ref, high_ref, total_ref = refs[-5:]
    block = start + pl.program_id(0)
    rows = q_ref[...]
    for head in range(heads):
        slab_ref[head] = head_slab(rows, head, 1.0)
    high_ref[...] = jnp.full(high_ref.shape, MASKED, f32)
    total_ref[...] = jnp.zeros(total_ref.shape, f32)

    def step(start, width, diagonal):
        keys = k_ref[pl.ds(start, width), :]
        values = vt_ref[:, pl.ds(start, width)]
        scores = [mm(keys, slab_ref[head], NT) for head in range(heads)]
        for head in range(heads):
            score = scores[head]
            if diagonal:
                score = jnp.where(causal(width, QB), score, MASKED)
            old = high_ref[head : head + 1, :]
            new = jnp.maximum(old, jnp.max(score, axis=0, keepdims=True))
            probs = jnp.exp(score - new).astype(bf16)
            high_ref[head : head + 1, :] = new
            total_ref[head] = total_ref[head] * jnp.exp(old - new) + mm(values, probs, NN)

    def body(index, carry):
        step(pl.multiple_of(index * WIDE, WIDE), WIDE, False)
        return carry

    lax.fori_loop(0, block // 2, body, 0)

    @pl.when(block % 2 == 1)
    def _():
        step(pl.multiple_of((block - 1) * QB, QB), QB, False)

    step(pl.multiple_of(block * QB, QB), QB, True)
    outs = []
    for head in range(heads):
        total = total_ref[head]
        mass = total[HD : HD + 1, :]
        lse_ref[head : head + 1, :] = high_ref[head : head + 1, :] + jnp.log(mass)
        outs.append(total[:HD, :] * (1.0 / mass))
    o_ref[...] = jnp.concatenate(outs, 0).T.astype(bf16)


def attend(first, queries, keys, values_t, carried):
    count, q_cols = queries.shape
    heads = q_cols // HD
    blocks = count // QB
    split = blocks * 5 // 8
    start = split if first else 0
    return pl.pallas_call(
        functools.partial(attend_kernel, heads, start),
        grid=(blocks - split if first else split,),
        in_specs=[
            pl.BlockSpec((QB, q_cols), lambda i: (start + i, 0)),
            pl.BlockSpec((count, 128), lambda i: (0, 0)),
            pl.BlockSpec((128, count), lambda i: (0, 0)),
        ]
        + [pl.BlockSpec(memory_space=pl.ANY)] * len(carried),
        out_specs=[
            pl.BlockSpec((QB, q_cols), lambda i: (start + i, 0)),
            pl.BlockSpec((8, QB), lambda i: (0, start + i)),
        ],
        out_shape=[
            jax.ShapeDtypeStruct((count, q_cols), bf16),
            jax.ShapeDtypeStruct((8, count), f32),
        ],
        scratch_shapes=[
            pltpu.VMEM((heads, QB, 128), bf16),
            pltpu.VMEM((8, QB), f32),
            pltpu.VMEM((heads, 128, QB), f32),
        ],
        input_output_aliases={3 + index: index for index in range(len(carried))},
        cost_estimate=cost(heads * count * count * 256, 2 * count * q_cols),
        name="attend",
    )(queries, keys, values_t, *carried)


def attend_back_kernel(
    heads,
    first,
    q_ref,
    do_ref,
    o_ref,
    lse_ref,
    k_ref,
    kt_ref,
    v_ref,
    table_ref,
    *refs,
):
    carried = refs[:3] if first else ()
    outs = refs[len(carried) : -6]
    qs_ref, ds_ref, delta_ref, dq_ref, dk_ref, dv_ref = refs[-6:]
    step_id = pl.program_id(0)
    block = first + step_id
    last = pl.num_programs(0) - 1
    q_cols = heads * HD

    @pl.when(step_id == 0)
    def _():
        dk_ref[...] = carried[1][...] if first else jnp.zeros(dk_ref.shape, f32)
        dv_ref[...] = carried[2][...] if first else jnp.zeros(dv_ref.shape, f32)
        if first:
            outs[0][: first * QB, :q_cols] = carried[0][...]

    rows = q_ref[...]
    grads = do_ref[...]
    product = (grads.astype(f32) * o_ref[...].astype(f32)).T
    for head in range(heads):
        qs_ref[head] = head_slab(rows, head, 1.0)
        ds_ref[head] = head_slab(grads, head, 0.0)
        delta_ref[head : head + 1, :] = jnp.sum(
            product[head * HD : (head + 1) * HD, :], axis=0, keepdims=True
        )
    dq_ref[...] = jnp.zeros(dq_ref.shape, f32)

    def step(start, diagonal):
        here = pl.ds(start, QB)
        keys = k_ref[here, :]
        keys_t = kt_ref[:, here]
        values = v_ref[here, :]
        dk = dk_ref[here, :]
        dv = dv_ref[here, :]

        def products(head):
            return (mm(keys, qs_ref[head], NT), mm(values, ds_ref[head], NT))

        ready = products(0)
        for head in range(heads):
            score, prob_grad = ready
            if head + 1 < heads:
                ready = products(head + 1)
            probs = jnp.exp(score - lse_ref[head : head + 1, :])
            if diagonal:
                probs = jnp.where(causal(QB, QB), probs, 0.0)
            dv = dv + mm(probs.astype(bf16), ds_ref[head], NN)
            score_grad = (probs * (prob_grad - delta_ref[head : head + 1, :])).astype(bf16)
            dk = dk + mm(score_grad, qs_ref[head], NN)
            dq_ref[head] = dq_ref[head] + mm(keys_t, score_grad, NN)
        dk_ref[here, :] = dk
        dv_ref[here, :] = dv

    def body(index, carry):
        step(pl.multiple_of(index * QB, QB), False)
        return carry

    lax.fori_loop(0, block, body, 0)
    step(pl.multiple_of(block * QB, QB), True)
    dq = jnp.concatenate([dq_ref[head, :HD, :] for head in range(heads)], 0).T * ATTN_SCALE
    here = pl.ds(pl.multiple_of(block * QB, QB), QB)
    dq = unrotate(dq, *turn_at(table_ref, block)).astype(bf16)
    if first:
        outs[0][here, :q_cols] = dq
    else:
        outs[0][...] = dq

    @pl.when(step_id == last)
    def _():
        if not first:
            outs[1][...] = dk_ref[...]
            outs[2][...] = dv_ref[...]
            return

        def finish(index, carry):
            there = pl.ds(pl.multiple_of(index * QB, QB), QB)
            dk = dk_ref[there, :]
            lane = lax.broadcasted_iota(jnp.int32, dk.shape, 1)
            dk = unrotate(jnp.where(lane < HD, dk, 0.0), *turn_at(table_ref, index))
            dv = dv_ref[there, :]
            outs[0][there, q_cols:] = jnp.concatenate([dk[:, :HD], dv[:, :HD]], 1).astype(bf16)
            return carry

        lax.fori_loop(0, dk_ref.shape[0] // QB, finish, 0)


def attend_back(first, queries, out_grads, attended, lse, keys, keys_t, values, table, carried):
    count, q_cols = queries.shape
    heads = q_cols // HD
    blocks = count // QB
    split = blocks * 5 // 8
    steps = blocks - split if first else split
    start = split if first else 0
    row = lambda i: (start + i, 0)
    whole = lambda i: (0, 0)
    total = pl.BlockSpec((count, 128), whole)
    total_shape = jax.ShapeDtypeStruct((count, 128), f32)
    early = (split * QB, q_cols)
    if first:
        out_specs = pl.BlockSpec((count, q_cols + 128), whole)
        out_shape = jax.ShapeDtypeStruct((count, q_cols + 128), bf16)
    else:
        out_specs = [pl.BlockSpec((QB, q_cols), row), total, total]
        out_shape = [jax.ShapeDtypeStruct(early, bf16), total_shape, total_shape]
    return pl.pallas_call(
        functools.partial(attend_back_kernel, heads, start),
        grid=(steps,),
        in_specs=[
            pl.BlockSpec((QB, q_cols), row),
            pl.BlockSpec((QB, q_cols), row),
            pl.BlockSpec((QB, q_cols), row),
            pl.BlockSpec((8, QB), lambda i: (0, start + i)),
            total,
            pl.BlockSpec((128, count), whole),
            total,
            pl.BlockSpec(table.shape, whole),
        ]
        + ([pl.BlockSpec(early, whole), total, total] if first else []),
        out_specs=out_specs,
        out_shape=out_shape,
        scratch_shapes=[
            pltpu.VMEM((heads, QB, 128), bf16),
            pltpu.VMEM((heads, QB, 128), bf16),
            pltpu.VMEM((8, QB), f32),
            pltpu.VMEM((heads, 128, QB), f32),
            pltpu.VMEM((count, 128), f32),
            pltpu.VMEM((count, 128), f32),
        ],
        cost_estimate=cost(heads * count * count * 640, 10 * count * q_cols),
        name="attend_back",
    )(queries, out_grads, attended, lse, keys, keys_t, values, table, *carried)


LENGTH, CORE, CHIP, RING = 0, 1, 2, 3


def out_norm_kernel(ids_ref, o_ref, mine_ref, other_ref, rows_ref, gain_ref, middle_ref, normed_ref):
    step = pl.program_id(0)
    steps = pl.num_programs(0)
    groups, _, q_cols = o_ref.shape
    cols = mine_ref.shape[1]

    def work(w_ref, core, index):
        total = None
        for place in range(groups):
            term = mm(
                o_ref[ids_ref[RING + place]], w_ref[place * q_cols : (place + 1) * q_cols, :], NN
            )
            total = term if total is None else total + term
        first = core * (steps // 2) + index
        here = pl.ds(pl.multiple_of(first * cols, cols), cols)
        middle_ref[:, here] = rows_ref[:, here].astype(f32) + RESID * total

    core = ids_ref[CORE]
    pl.when(step < steps // 2)(lambda: work(mine_ref, core, step))
    pl.when(step >= steps // 2)(lambda: work(other_ref, 1 - core, step - steps // 2))

    @pl.when(step == steps - 1)
    def _():
        middle = middle_ref[...]
        row_scale = lax.rsqrt(jnp.mean(middle * middle, axis=-1, keepdims=True) + EPSILON)
        normed_ref[...] = (middle * row_scale * gain_ref[...]).astype(bf16)


def out_norm(ids, attended, w_mine, w_other, hidden, gain):
    groups, share, q_cols = attended.shape
    width = hidden.shape[1]
    whole = lambda j, s: (0, 0)
    steps = 2
    return pl.pallas_call(
        out_norm_kernel,
        grid_spec=pltpu.PrefetchScalarGridSpec(
            num_scalar_prefetch=1,
            grid=(steps,),
            in_specs=[
                pl.BlockSpec((groups, share, q_cols), lambda j, s: (0, 0, 0)),
                pl.BlockSpec(
                    (groups * q_cols, width // steps), lambda j, s: (0, jnp.minimum(j, steps // 2 - 1))
                ),
                pl.BlockSpec(
                    (groups * q_cols, width // steps), lambda j, s: (0, jnp.maximum(j - steps // 2, 0))
                ),
                pl.BlockSpec((share, width), lambda j, s: (s[RING], 0)),
                pl.BlockSpec((1, width), whole),
            ],
            out_specs=[pl.BlockSpec((share, width), whole), pl.BlockSpec((share, width), whole)],
        ),
        out_shape=[
            jax.ShapeDtypeStruct((share, width), f32),
            jax.ShapeDtypeStruct((share, width), bf16),
        ],
        cost_estimate=cost(2 * groups * share * q_cols * width, 2 * groups * q_cols * width),
        name="out_project_and_norm",
    )(ids, attended, w_mine, w_other, hidden, gain)


def norm_back_kernel(
    ids_ref,
    own_ref,
    up_ref,
    down_ref,
    middle_ref,
    gain_ref,
    cotangent_ref,
    mine_ref,
    other_ref,
    dh_ref,
    da_ref,
    gain_grad_ref,
    do_ref,
):
    step = pl.program_id(0)

    @pl.when(step == 0)
    def _():
        incoming = own_ref[...].astype(f32) + up_ref[...].astype(f32) + down_ref[...].astype(f32)
        middle = middle_ref[...]
        row_scale = lax.rsqrt(jnp.mean(middle * middle, axis=-1, keepdims=True) + EPSILON)
        normed = middle * row_scale
        gain_grad_ref[...] = jnp.sum(incoming * normed, axis=0, keepdims=True)
        scaled = incoming * gain_ref[...]
        branch = row_scale * (scaled - normed * jnp.mean(scaled * normed, axis=-1, keepdims=True))
        share = middle.shape[0]
        position = ids_ref[RING] * share + lax.broadcasted_iota(jnp.int32, (share, 1), 0)
        direct = jnp.where(position < ids_ref[LENGTH], cotangent_ref[...].astype(f32), 0.0)
        dh = direct + branch
        dh_ref[...] = dh
        da_ref[...] = (RESID * dh).astype(bf16)

    rows, cols = mine_ref.shape
    q_cols = do_ref.shape[2]
    core = ids_ref[CORE]
    mine = da_ref[:, pl.ds(pl.multiple_of(core * cols, cols), cols)]
    other = da_ref[:, pl.ds(pl.multiple_of((1 - core) * cols, cols), cols)]
    per_step = rows // q_cols
    for index in range(per_step):
        here = slice(index * q_cols, (index + 1) * q_cols)
        grad = mm(mine, mine_ref[here, :], NT) + mm(other, other_ref[here, :], NT)
        do_ref[ids_ref[RING + step * per_step + index]] = grad.astype(bf16)


def norm_back(ids, parts, middle, gain, cotangent, w_mine, w_other, q_cols):
    share, width = middle.shape
    groups = w_mine.shape[0] // q_cols
    whole = lambda t, s: (0, 0)
    weight = pl.BlockSpec((groups * q_cols // 2, width // 2), lambda t, s: (t, 0))
    return pl.pallas_call(
        norm_back_kernel,
        grid_spec=pltpu.PrefetchScalarGridSpec(
            num_scalar_prefetch=1,
            grid=(2,),
            in_specs=[pl.BlockSpec((share, width), whole)] * 4
            + [
                pl.BlockSpec((1, width), whole),
                pl.BlockSpec((share, width), lambda t, s: (s[RING], 0)),
                weight,
                weight,
            ],
            out_specs=[
                pl.BlockSpec((share, width), whole),
                pl.BlockSpec((share, width), whole),
                pl.BlockSpec((1, width), whole),
                pl.BlockSpec((groups, share, q_cols), lambda t, s: (0, 0, 0)),
            ],
        ),
        out_shape=[
            jax.ShapeDtypeStruct((share, width), f32),
            jax.ShapeDtypeStruct((share, width), bf16),
            jax.ShapeDtypeStruct((1, width), f32),
            jax.ShapeDtypeStruct((groups, share, q_cols), bf16),
        ],
        cost_estimate=cost(2 * groups * share * q_cols * width, 2 * groups * q_cols * width),
        name="norm_back_and_project",
    )(ids, *parts, middle, gain, cotangent, w_mine, w_other)


def in_grad_kernel(ids_ref, own_ref, up_ref, down_ref, rows_ref, gain_ref, dh_ref, out_ref):
    incoming = own_ref[...].astype(f32) + up_ref[...].astype(f32) + down_ref[...].astype(f32)
    rows = rows_ref[...].astype(f32)
    row_scale = lax.rsqrt(jnp.mean(rows * rows, axis=-1, keepdims=True) + EPSILON)
    normed = rows * row_scale
    scaled = incoming * gain_ref[...]
    branch = row_scale * (scaled - normed * jnp.mean(scaled * normed, axis=-1, keepdims=True))
    out_ref[...] = dh_ref[...] + branch


def in_grad(ids, terms, got, hidden, gain, dh):
    share, width = dh.shape
    steps = 4
    rows = share // steps
    row = lambda j, s: (j, 0)
    own = lambda j, s: (steps * s[RING] + j, 0)
    return pl.pallas_call(
        in_grad_kernel,
        grid_spec=pltpu.PrefetchScalarGridSpec(
            num_scalar_prefetch=1,
            grid=(steps,),
            in_specs=[
                pl.BlockSpec((rows, width), own),
                pl.BlockSpec((rows, width), row),
                pl.BlockSpec((rows, width), row),
                pl.BlockSpec((rows, width), own),
                pl.BlockSpec((1, width), lambda j, s: (0, 0)),
                pl.BlockSpec((rows, width), row),
            ],
            out_specs=pl.BlockSpec((rows, width), row),
        ),
        out_shape=jax.ShapeDtypeStruct((share, width), f32),
        cost_estimate=cost(20 * share * width, 16 * share * width),
        name="input_grad",
    )(ids, terms, *got, hidden, gain, dh)


def core_halves(chips):
    def piece(i, s):
        chip = (s[CHIP] + i) % chips
        return 2 * chip + jnp.where(i < chips, 1 - s[CORE], s[CORE])

    sent = lambda i: jnp.minimum(i, chips - 1)
    kept = lambda i: jnp.maximum(i - chips, 0)
    return piece, sent, kept


def out_wgrad_kernel(ids_ref, o_ref, da_ref, send_ref, keep_ref):
    step = pl.program_id(0)
    groups, _, q_cols = o_ref.shape

    def store(ref):
        for group in range(groups):
            part = mm(o_ref[group], da_ref[...], TN)
            ref[0, group * q_cols : (group + 1) * q_cols, :] = part.astype(bf16)

    half = pl.num_programs(0) // 2
    pl.when(step < half)(lambda: store(send_ref))
    pl.when(step >= half)(lambda: store(keep_ref))


def out_wgrad_parts(ids, attended, branch_grad, replicas):
    groups, share, q_cols = attended.shape
    width = branch_grad.shape[1]
    cols = width // replicas
    chips = replicas // 2
    piece, sent, kept = core_halves(chips)
    out = jax.ShapeDtypeStruct((chips, groups * q_cols, cols), bf16)
    block = (1, groups * q_cols, cols)
    return pl.pallas_call(
        out_wgrad_kernel,
        grid_spec=pltpu.PrefetchScalarGridSpec(
            num_scalar_prefetch=1,
            grid=(replicas,),
            in_specs=[
                pl.BlockSpec((groups, share, q_cols), lambda i, s: (0, 0, 0)),
                pl.BlockSpec((share, cols), lambda i, s: (0, piece(i, s))),
            ],
            out_specs=[
                pl.BlockSpec(block, lambda i, s: (sent(i), 0, 0)),
                pl.BlockSpec(block, lambda i, s: (kept(i), 0, 0)),
            ],
        ),
        out_shape=[out, out],
        cost_estimate=cost(2 * groups * share * q_cols * width, 2 * groups * q_cols * width),
        name="out_weight_grad",
    )(ids, attended, branch_grad)


def qkv_wgrad_kernel(
    ids_ref,
    normed_ref,
    grad_ref,
    w_ref,
    gain_ref,
    other_gain_ref,
    q_send_ref,
    q_keep_ref,
    s_send_ref,
    s_keep_ref,
):
    step = pl.program_id(0)
    cols = normed_ref.shape[1]
    q_cols = q_send_ref.shape[2]

    def store(q_ref, s_ref):
        grad = mm(normed_ref[...], grad_ref[...], TN)
        q_ref[0] = grad[:, :q_cols].astype(bf16)
        s_ref[0, :, : 2 * HD] = grad[:, q_cols:]
        gain = jnp.sum(grad * w_ref[...].astype(f32), axis=1, keepdims=True)
        lane = lax.broadcasted_iota(jnp.int32, (cols, 128), 1)
        first = jnp.where(lane == 0, gain / gain_ref[...], 0.0)
        s_ref[0, :, 2 * HD :] = jnp.where(lane == 1, other_gain_ref[...], first)

    half = pl.num_programs(0) // 2
    pl.when(step < half)(lambda: store(q_send_ref, s_send_ref))
    pl.when(step >= half)(lambda: store(q_keep_ref, s_keep_ref))


def qkv_wgrad_parts(ids, normed, grads, w_qkv, gain, other_gain, replicas):
    count, width = normed.shape
    all_cols = grads.shape[1]
    q_cols = all_cols - 2 * HD
    chips = replicas // 2
    cols = width // replicas
    piece, sent, kept = core_halves(chips)
    down = lambda n: pl.BlockSpec((cols, n), lambda i, s: (piece(i, s), 0))
    out = lambda n, where: pl.BlockSpec((1, cols, n), lambda i, s: (where(i), 0, 0))
    shape = lambda n, kind: jax.ShapeDtypeStruct((chips, cols, n), kind)
    return pl.pallas_call(
        qkv_wgrad_kernel,
        grid_spec=pltpu.PrefetchScalarGridSpec(
            num_scalar_prefetch=1,
            grid=(replicas,),
            in_specs=[
                pl.BlockSpec((count, cols), lambda i, s: (0, piece(i, s))),
                pl.BlockSpec((count, all_cols), lambda i, s: (0, 0)),
                down(all_cols),
                down(1),
                down(1),
            ],
            out_specs=[out(q_cols, sent), out(q_cols, kept), out(256, sent), out(256, kept)],
        ),
        out_shape=[shape(q_cols, bf16)] * 2 + [shape(256, f32)] * 2,
        cost_estimate=cost(2 * count * width * all_cols, 3 * count * width),
        name="projection_weight_grads",
    )(ids, normed, grads, w_qkv, gain, other_gain)


def layer_out_kernel(middle_ref, own_ref, up_ref, down_ref, out_ref):
    total = own_ref[...].astype(f32) + up_ref[...].astype(f32) + down_ref[...].astype(f32)
    out_ref[...] = (middle_ref[...] + RESID * total).astype(bf16)


def layer_output(middle, own, own_row, got):
    share, width = middle.shape
    spec = lambda row: pl.BlockSpec((share, WIDE), lambda j: (row, j))
    return pl.pallas_call(
        layer_out_kernel,
        grid=(width // WIDE,),
        in_specs=[spec(0), spec(own_row), spec(0), spec(0)],
        out_specs=spec(0),
        out_shape=jax.ShapeDtypeStruct((share, width), bf16),
        cost_estimate=cost(5 * share * width, 12 * share * width),
        name="layer_output",
    )(middle, own, *got)


def ring_add_kernel(first, ids_ref, term_ref, got_ref, out_ref):
    rows = got_ref.shape[0]
    if rows < out_ref.shape[0]:
        out_ref[...] = term_ref[...]
    here = slice(first, first + rows)
    out_ref[here, :] = (term_ref[here, :].astype(f32) + got_ref[...].astype(f32)).astype(bf16)


def ring_add(ids, terms, block, place, got, first, share):
    width = terms.shape[1]
    cols = width // 2
    which = lambda j, s: (s[RING + place] if block is None else block, j)
    column = lambda j, s: (0, j)
    return pl.pallas_call(
        functools.partial(ring_add_kernel, first),
        grid_spec=pltpu.PrefetchScalarGridSpec(
            num_scalar_prefetch=1,
            grid=(2,),
            in_specs=[
                pl.BlockSpec((share, cols), which),
                pl.BlockSpec((got.shape[0], cols), column),
            ],
            out_specs=pl.BlockSpec((share, cols), column),
        ),
        out_shape=jax.ShapeDtypeStruct((share, width), bf16),
        cost_estimate=cost(2 * share * width, 6 * share * width),
        name="ring_add",
    )(ids, terms, got)


def swiglu_kernel(pieces, members, row, ids_ref, *refs):
    piece_refs = refs[:pieces]
    cot_ref, gate_ref, up_ref, down_ref = refs[pieces : pieces + 4]
    outs = refs[-19:-13]
    x, dm, wg, wu, wd, act, dgate, dup, in_sem, gate_sem, up_sem, down_sem, out_sem = refs[-13:]
    kept, dn_ref = outs[:5], outs[5]
    rows = x.shape[0]
    share = rows // len(members)
    width, units = wg.shape
    blocks = gate_sem.shape[0]
    block = units // blocks
    part = width // blocks
    arrivals = []
    at = 0
    for ref in piece_refs:
        count = ref.shape[0]
        arrivals.append((ref, x.at[at : at + count, :]))
        at += count
    for index, place in enumerate(members):
        first = pl.multiple_of(ids_ref[RING + place] * share, share)
        here = slice(index * share, (index + 1) * share)
        arrivals.append((cot_ref.at[pl.ds(first, share), :], dm.at[here, :]))
    arrivals = [pltpu.make_async_copy(*pair, in_sem.at[i]) for i, pair in enumerate(arrivals)]

    def weights(u):
        here = pl.ds(pl.multiple_of(u * block, block), block)
        return (
            pltpu.make_async_copy(gate_ref.at[:, here], wg.at[:, here], gate_sem.at[u]),
            pltpu.make_async_copy(up_ref.at[:, here], wu.at[:, here], up_sem.at[u]),
            pltpu.make_async_copy(down_ref.at[here, :], wd.at[here, :], down_sem.at[u]),
        )

    for copy in arrivals[:pieces]:
        copy.start()
    for copy in weights(0):
        copy.start()
    for copy in arrivals[pieces:]:
        copy.start()
    for u in range(1, blocks):
        for copy in weights(u):
            copy.start()
    for copy in arrivals:
        copy.wait()
    for index, place in enumerate(members):
        here = slice(index * share, (index + 1) * share)
        position = ids_ref[RING + place] * share + lax.broadcasted_iota(jnp.int32, (share, 1), 0)
        scaled = dm[here, :].astype(f32) * RESID
        dm[here, :] = jnp.where(position < ids_ref[LENGTH], scaled, 0.0).astype(bf16)

    def one_block(u, carry):
        for copy in weights(u):
            copy.wait()
        here = pl.ds(pl.multiple_of(u * block, block), block)
        gate = mm(x[...], wg[:, here], NN)
        up = mm(x[...], wu[:, here], NN)
        grad = mm(dm[...], wd[here, :], NT)
        sg = jax.nn.sigmoid(gate)
        silu = gate * sg
        act[:, here] = (silu * up).astype(bf16)
        dgate[:, here] = (grad * up * sg * (1.0 + gate * (1.0 - sg))).astype(bf16)
        dup[:, here] = (grad * silu).astype(bf16)
        return carry

    lax.fori_loop(0, blocks, one_block, 0)

    def one_part(n, carry):
        here = pl.ds(pl.multiple_of(n * part, part), part)
        grad = mm(dgate[...], wg[here, :], NT) + mm(dup[...], wu[here, :], NT)
        dn_ref[:, here] = grad.astype(bf16)
        return carry

    one_part(0, 0)
    leaving = [
        pltpu.make_async_copy(src, dst.at[pl.ds(row, rows), :], out_sem.at[i])
        for i, (src, dst) in enumerate(zip((x, dm, act, dgate, dup), kept))
    ]
    for copy in leaving:
        copy.start()
    lax.fori_loop(1, blocks, one_part, 0)
    for copy in leaving:
        copy.wait()


def swiglu(ids, pieces, members, cotangent, weights, row, buffers, total_rows):
    w_gate, w_up, w_down = weights
    width, units = w_gate.shape
    rows = sum(piece.shape[0] for piece in pieces)
    blocks = 2
    hbm = pl.BlockSpec(memory_space=pl.ANY)
    operands = [*pieces, cotangent, *weights, *buffers]
    aliases = {5 + len(pieces) + index: index for index in range(len(buffers))}
    collected = lambda n: jax.ShapeDtypeStruct((total_rows, n), bf16)
    held = lambda *shape: pltpu.VMEM(shape, bf16)
    copies = lambda n: pltpu.SemaphoreType.DMA((n,))
    return pl.pallas_call(
        functools.partial(swiglu_kernel, len(pieces), tuple(members), row),
        grid_spec=pltpu.PrefetchScalarGridSpec(
            num_scalar_prefetch=1,
            grid=(1,),
            in_specs=[hbm] * len(operands),
            out_specs=[hbm] * 5 + [pl.BlockSpec((rows, width), lambda i, s: (0, 0))],
            scratch_shapes=[held(rows, width)] * 2
            + [held(width, units), held(width, units), held(units, width)]
            + [held(rows, units)] * 3
            + [copies(len(pieces) + len(members)), *([copies(blocks)] * 3), copies(5)],
        ),
        out_shape=[collected(width)] * 2
        + [collected(units)] * 3
        + [jax.ShapeDtypeStruct((rows, width), bf16)],
        input_output_aliases=aliases,
        compiler_params=grant(58),
        cost_estimate=cost(12 * rows * width * units, 6 * width * units + 16 * rows * width),
        name="swiglu_rows",
    )(ids, *operands)


def ring_order(count):
    inner = 2 if count <= 8 else 4
    outer = count // inner
    cells = [(0, 0)]
    for row in range(outer):
        cells += [(row, c) for c in (range(1, inner) if row % 2 == 0 else range(inner - 1, 0, -1))]
    cells += [(row, 0) for row in range(outer - 1, 0, -1)]
    return [row * inner + c for row, c in cells]


def tie(*values):
    return lax.optimization_barrier(values)


def other_core(array):
    replicas = lax.axis_size("dp")
    return lax.ppermute(array, "dp", [(i, i ^ 1) for i in range(replicas)])


def over_chips(keep, got):
    chips = keep.shape[0]
    arriving = []
    for step in range(1, chips):
        to = [(i, ((i // 2 + step) % chips) * 2 + i % 2) for i in range(2 * chips)]
        go = (keep[step].astype(f32) + got[step].astype(f32)).astype(keep.dtype)
        arriving.append(lax.ppermute(go, "dp", to))
    return keep, got, arriving


def total_of(keep, got, arriving):
    total = keep[0].astype(f32) + got[0].astype(f32)
    for term in arriving:
        total = total + term.astype(f32)
    return total


def local(
    hidden_in,
    seq_lengths,
    out_grad,
    attn_gain,
    mlp_gain,
    w_query,
    w_key,
    w_value,
    w_out,
    w_gate,
    w_up,
    w_down,
):
    rows_total, width = hidden_in.shape
    q_cols = w_query.shape[1]
    heads_here = q_cols // HD
    groups = lax.axis_size("tensor")
    replicas = lax.axis_size("dp")
    member = lax.axis_index("tensor")
    replica = lax.axis_index("dp")
    core = replica % 2
    share = rows_total // groups
    half = share // 2
    order = ring_order(groups)
    spot = [order.index(i) for i in range(groups)]
    ahead = [(order[i], order[(i + 1) % groups]) for i in range(groups)]
    behind = [(b, a) for a, b in ahead]
    half_way = groups // 2
    apart = [0]
    for d in range(1, half_way):
        apart += [-d, d]
    apart.append(half_way)
    ring = [[order[(spot[i] + d) % groups] for d in apart] for i in range(groups)]
    ids = jnp.concatenate(
        [
            seq_lengths,
            jnp.stack([core, replica // 2]).astype(jnp.int32),
            jnp.asarray(ring, jnp.int32)[member],
        ]
    )
    table = rope_tables(rows_total)
    gain_one = attn_gain[None, :]
    gain_two = mlp_gain[None, :]

    def exchange(array):
        return lax.all_to_all(array, "tensor", 0, 0, tiled=True)

    def onward(array):
        return lax.ppermute(array, "tensor", ahead)

    def back(array):
        return lax.ppermute(array, "tensor", behind)

    w_own = lax.dynamic_slice_in_dim(w_out, core * (width // 2), width // 2, 1)
    w_hop = onward(w_own), back(w_own)
    w_mine = [w_own]

    def w_next():
        w_mine.extend(w_hop)
        if len(w_mine) < groups - 1:
            return onward(w_hop[0]), back(w_hop[1])
        return onward(w_hop[0][: q_cols // 2]), back(w_hop[1][q_cols // 2 :])

    kv_of = [i * heads_here // (H // KVH) for i in range(groups)]
    w_kv = pick_heads(w_key, w_value, kv_of)
    w_kv = exchange(w_kv).reshape(width, 2 * HD)
    carried = front(0, hidden_in, gain_one, w_query, table, [])
    w_hop, carried = tie(w_hop, carried)
    for _ in range(half_way - 3):
        w_hop = w_next()
    normed_one, queries = front(1, hidden_in, gain_one, w_query, table, carried)
    keys, keys_t, values, values_t = keys_values(seq_lengths, normed_one, w_kv, table)
    w_hop, keys = tie(w_hop, keys)
    w_hop = w_next()
    carried = attend(0, queries, keys, values_t, [])
    w_hop, carried = tie(w_hop, carried)
    w_hop = w_next()
    attended, lse = attend(1, queries, keys, values_t, carried)
    w_hop, attended = tie(w_hop, attended)
    attended_rows = exchange(attended.reshape(groups, share, q_cols))
    w_mine = jnp.concatenate([*w_mine, *w_hop], 0)
    w_other = lax.ppermute(w_mine, "dp", [(i, i ^ 1) for i in range(replicas)])
    w_qkv = jnp.concatenate([w_query, w_kv], 1)
    middle, normed_two = out_norm(ids, attended_rows, w_mine, w_other, hidden_in, gain_two)

    weights = (w_gate, w_up, w_down)
    grads = []
    buffers = []

    def run(pieces, members, row):
        nonlocal buffers
        *buffers, grad = swiglu(
            ids, pieces, members, out_grad, weights, row, buffers, rows_total
        )
        grads.append(grad)

    pieces, members, row = [normed_two], [0], rows_total - 2 * share
    hop = [normed_two, normed_two]
    split = 2 * share * (half_way - 2)
    for d in range(1, half_way + 1):
        if d < half_way:
            hop = [onward(hop[0]), back(hop[1])]
        else:
            hop = [onward(hop[0][:half]), back(hop[1][half:])]
        if d < half_way:
            run(pieces, members, row)
            hop, grads[-1], buffers = tie(hop, grads[-1], buffers)
        else:
            last_pair = pieces, members, row
            early = mm(buffers[2][:split], w_down, NN).astype(bf16)
            hop, early, buffers = tie(hop, early, buffers)
        pieces = hop
        if d < half_way:
            members, row = [2 * d - 1, 2 * d], 2 * share * (d - 1)
        else:
            members, row = [groups - 1], rows_total - share
    run(pieces, members, row)

    def first_hop(far):
        return onward(far[:half]), back(far[half:])

    def hop_sums(terms, block, got):
        down = ring_add(ids, terms, block, None, got[1], share - got[1].shape[0], share)
        up = ring_add(ids, terms, block + 1, None, got[0], 0, share)
        return up, down

    def send_on(sums):
        return onward(sums[0]), back(sums[1])

    def next_hop(terms, block, got):
        return send_on(hop_sums(terms, block, got))

    def natural_sums(terms, distance, got):
        first = share - got[1].shape[0]
        down = ring_add(ids, terms, None, 2 * distance - 1, got[1], first, share)
        up = ring_add(ids, terms, None, 2 * distance, got[0], 0, share)
        return up, down

    got = first_hop(grads.pop())
    run(*last_pair)
    got, grads[-1], buffers = tie(got, grads[-1], buffers)
    normed_ring, down_ring, act, dgate, dup = buffers
    late_act = act[split:]
    fillers = [
        lambda: mm(act, down_ring, TN).astype(bf16),
        lambda: mm(normed_ring, dgate, TN).astype(bf16),
        lambda: mm(normed_ring, dup, TN).astype(bf16),
    ]
    filled = []
    for d in range(half_way - 1, 0, -1):
        hop = hop_sums(grads[d], 0, got)
        hop, normed_ring, act, late_act = tie(hop, normed_ring, act, late_act)
        got = send_on(hop)
        work = [fillers[len(filled)]()] if len(filled) < 3 else []
        if d == half_way - 2:
            late = mm(late_act, w_down, NN).astype(bf16)
            mlp_far = [late[-share:-half], late[-half:]]
            got, work, late, mlp_far = tie(got, work, late, mlp_far)
        else:
            got, work = tie(got, work)
        filled += work
    down_wgrad, gate_wgrad, up_wgrad = filled
    scatter = lambda a, d: lax.psum_scatter(a, "dp", scatter_dimension=d, tiled=True)
    down_wgrad = scatter(down_wgrad, 1)
    gate_wgrad = scatter(gate_wgrad, 0)
    up_wgrad = scatter(up_wgrad, 0)

    got, mlp_far = tie(got, mlp_far)
    out_got = send_on(mlp_far)
    dh, da, gain_part, do_send = norm_back(
        ids, [grads[0], *got], middle, gain_two, out_grad, w_mine, w_other, q_cols
    )
    *out_got, do_send, da = tie(*out_got, do_send, da)
    do = exchange(do_send).reshape(rows_total, q_cols)
    out_parts = out_wgrad_parts(ids, attended_rows, da, replicas)
    out_sums = hop_sums(late, 0, out_got)
    do, out_parts, out_sums = tie(do, out_parts, out_sums)
    out_got = send_on(out_sums)
    out_send, out_keep = out_parts
    out_swapped = other_core(out_send)
    operands = [queries, do, attended, lse, keys, keys_t, values, table]
    carried = attend_back(0, *operands, [])
    out_got, carried, down_wgrad, out_swapped = tie(out_got, carried, down_wgrad, out_swapped)
    for d in range(half_way - 2, 1, -1):
        out_got = next_hop(early, 2 * d - 2, out_got)
    qkv_grad = attend_back(1, *operands, carried)
    out_got, qkv_grad, out_keep = tie(out_got, qkv_grad, out_keep)

    far = lax.dynamic_slice_in_dim(qkv_grad, ids[RING + groups - 1] * share, share, 0)
    far = mm(far, w_qkv, NT).astype(bf16)
    in_got = first_hop(far)
    qkv_grad, far, out_got, out_keep = tie(qkv_grad, far, out_got, out_keep)
    out_got = next_hop(early, 0, out_got)
    out_terms = over_chips(out_keep, out_swapped)
    first_grad = mm(qkv_grad, w_qkv, NT).astype(bf16)
    q_send, q_keep, s_send, s_keep = qkv_wgrad_parts(
        ids,
        normed_one,
        qkv_grad,
        w_qkv,
        attn_gain[:, None],
        gain_part.reshape(width, 1),
        replicas,
    )
    in_got, out_got, q_send, s_send, gate_wgrad, first_grad = tie(
        in_got, out_got, q_send, s_send, gate_wgrad, first_grad
    )
    s_swapped, q_swapped = other_core(s_send), other_core(q_send)
    for d in range(half_way - 1, 0, -1):
        in_sums = natural_sums(first_grad, d, in_got)
        if d == half_way - 1:
            in_got = send_on(in_sums)
            small = over_chips(s_keep, s_swapped)
            query_wgrad = over_chips(q_keep, q_swapped)
            in_got, small, query_wgrad, out_terms = tie(in_got, small, query_wgrad, out_terms)
            out_wgrad = total_of(*out_terms).astype(bf16)
            out_wgrad = lax.psum_scatter(out_wgrad, "tensor", scatter_dimension=0, tiled=True)
            small, query_wgrad = total_of(*small), total_of(*query_wgrad)
            layer_out = layer_output(middle, late, 2, out_got)
            continue
        in_got = send_on(in_sums)
        if d == half_way - 2:
            in_got, layer_out, up_wgrad = tie(in_got, layer_out, up_wgrad)
    pieces = exchange(small.reshape(groups, small.shape[0] // groups, 256))
    input_grad = in_grad(ids, first_grad, in_got, hidden_in, gain_one, dh)
    gains = jnp.sum(pieces[:, :, 128:130], axis=0)
    kv = pieces[:, :, :128].reshape(KVH, groups // KVH, -1, 128).sum(axis=1)
    kv = jnp.swapaxes(kv, 0, 1)
    key_wgrad = kv[:, :, :HD].reshape(-1, KVH * HD)
    value_wgrad = kv[:, :, HD:].reshape(-1, KVH * HD)
    return (
        layer_out,
        input_grad,
        gains[:, 0],
        gains[:, 1],
        query_wgrad,
        key_wgrad,
        value_wgrad,
        out_wgrad.astype(f32),
        gate_wgrad.astype(f32),
        up_wgrad.astype(f32),
        down_wgrad.astype(f32),
    )


def solution(mesh):
    placed = (
        P("dp", None),
        P("dp"),
        P("dp", None),
        P(),
        P(),
        P(None, "tensor"),
        P("tensor", None),
        P("tensor", None),
        P("tensor", None),
        P(None, "tensor"),
        P(None, "tensor"),
        P("tensor", None),
    )
    return jax.shard_map(
        local,
        mesh=mesh,
        in_specs=placed,
        out_specs=(
            P(("dp", "tensor"), None),
            P(("dp", "tensor"), None),
            P(("dp", "tensor")),
            P(("dp", "tensor")),
            P("dp", "tensor"),
            P(("dp", "tensor"), None),
            P(("dp", "tensor"), None),
            P("tensor", "dp"),
            P("dp", "tensor"),
            P("dp", "tensor"),
            P("tensor", "dp"),
        ),
        check_vma=False,
    )
```
